32 devices in a mesh: dp: 4 (over y, x), seq: 8 (over z, core).
Axes of the slice: x: 2, y: 2, z: 4, core: 2. Of those that a mesh axis runs over, the one named last changes fastest.
Arguments:
- queries: bfloat16 [16, 4096, 128], P(None, ('dp', 'seq')), parts along dimension 1, may hold values from -6 to 6
- key_pairs: bfloat16 [16, 4096, 256], P(None, ('dp', 'seq')), parts along dimension 1, may hold values from -6 to 6
- value_pairs: bfloat16 [16, 4096, 256], P(None, ('dp', 'seq')), parts along dimension 1, may hold values from -6 to 6
- strengths: float32 [16, 8192], P(None, ('dp', 'seq')), parts along dimension 1, may hold values from 0.002 to 1.99
- decays: float32 [16, 4096], P(None, ('dp', 'seq')), parts along dimension 1, may hold values from 0 to 1, as said below
- conv_query: float32 [16, 4, 128], replicated, may hold values from -1.5 to 1.5
- conv_key: float32 [16, 4, 256], replicated, may hold values from -1.5 to 1.5
- conv_value: float32 [16, 4, 256], replicated, may hold values from -1.5 to 1.5
- doc_lengths: int32 [32], P('dp'), parts along dimension 0, may hold values from 1 to 512, 1024 in all
Outputs:
- readout: bfloat16 [16, 4096, 128], P(None, ('dp', 'seq')), parts along dimension 1
The draws below stay inside these ranges and needn't reach their ends.
There are 4 independent parts, one for each index of `dp`. The reference program is written for one: setup_inputs(seed, part) draws one part's arguments, and reference() takes and returns one part's arrays. A program takes and returns all parts, laid end to end along the dimension named above; an argument that names none is the same for every part. Nothing has to cross between parts.
Inputs may be any that keep to these rules, and one draw needn't show every extreme that they name: `doc_lengths`: they sum to 1024, and the longest document has exactly 512 tokens. Every gate exp(-decays) lies between 0.36 and 1.
All inputs are finite; a program needn't handle non-finite values.
Results may differ from the reference program's by a relative error of at most 0.0062.
Values may be sent and summed in bfloat16 or wider, within the bound.
A program may use at most 320 MiB of HBM per device.

```python
import math
import jax
import jax.numpy as jnp
import numpy as np
from jax import lax

HEAD_COUNT = 16
DK = 128
DV = 128
TAPS = 4
LONGEST_DOC = 4
TOKENS_PER_SHARD = 128
PACKED_TOKENS = 1024
MOST = 512
NDOCS = 8
N_SEQ = 8


def head_speed(key):
    picker = jax.random.uniform(jax.random.fold_in(key, 101), (HEAD_COUNT,))
    return picker < 0.5


def draw_decays(key, part):
    fast = head_speed(key)
    parallel_lanes = jax.random.split(jax.random.fold_in(key, 202), 6)
    fast_rate = jnp.exp(jax.random.uniform(parallel_lanes[0], (HEAD_COUNT,), jnp.float32, jnp.log(1.0 / 50.0), jnp.log(1.0 / 30.0)))
    slow_rate = jnp.exp(jax.random.uniform(parallel_lanes[1], (HEAD_COUNT,), jnp.float32, jnp.log(0.05), jnp.log(0.4))) / (LONGEST_DOC * TOKENS_PER_SHARD)
    rate = jnp.where(fast, fast_rate, slow_rate)
    blocks = PACKED_TOKENS // TOKENS_PER_SHARD
    block_factor = jnp.exp(jax.random.uniform(parallel_lanes[2], (HEAD_COUNT, blocks, 1), jnp.float32, -jnp.log(2.0), jnp.log(2.0)))
    token_factor = jax.random.uniform(parallel_lanes[3], (HEAD_COUNT, blocks, TOKENS_PER_SHARD), jnp.float32, 0.5, 1.5)
    token_groups = jax.random.bernoulli(parallel_lanes[4], 2.0 / (LONGEST_DOC * TOKENS_PER_SHARD), (1, PACKED_TOKENS)).astype(jnp.float32)
    group_length = jax.random.uniform(parallel_lanes[5], (HEAD_COUNT, PACKED_TOKENS), jnp.float32, 0.223, 0.693)
    smoothed_values = (rate[:, None, None] * block_factor * token_factor).reshape(HEAD_COUNT, PACKED_TOKENS)
    return (smoothed_values + token_groups * group_length).astype(jnp.float32)


def draw_strengths(key, part):
    fast = head_speed(key)
    parallel_lanes = jax.random.split(jax.random.fold_in(key, 404), 3)
    slow_scale = jnp.exp(jax.random.uniform(parallel_lanes[0], (HEAD_COUNT,), jnp.float32, jnp.log(0.01), jnp.log(0.05)))
    fast_values = jax.random.uniform(parallel_lanes[1], (HEAD_COUNT, 2 * PACKED_TOKENS), jnp.float32, 0.3, 1.9)
    slow_values = slow_scale[:, None] * jax.random.uniform(parallel_lanes[2], (HEAD_COUNT, 2 * PACKED_TOKENS), jnp.float32, 0.5, 1.5)
    return jnp.where(fast[:, None], fast_values, slow_values).astype(jnp.float32)


def block_scale(key, shape, cuts, least, top_value):
    def one(axis_at, parts):
        heights = jax.random.uniform(jax.random.fold_in(jax.random.fold_in(key, 6), axis_at), (parts,), jnp.float32, least / len(cuts), top_value / len(cuts))
        return jnp.repeat(jnp.exp(heights), shape[axis_at] // parts).reshape((-1,) + (1,) * (len(shape) - axis_at - 1))

    loudness = one(*cuts[0])
    for cut in cuts[1:]:
        loudness = loudness * one(*cut)
    return loudness


def length_profile(count, total, reach, skew):
    portions = [(1 << 20) // math.isqrt(rank ** skew) + 1 for rank in range(2, count + 1)]
    spare, counts = total - reach - (count - 1), [1] * (count - 1)
    while spare > 0:
        candidates = [i for i in range(count - 1) if counts[i] < reach]
        whole, remaining = sum([portions[i] for i in candidates]), spare
        for i in candidates:
            extra = min(reach - counts[i], max(1, remaining * portions[i] // whole), spare)
            counts[i] = counts[i] + extra
            spare = spare - extra
    return np.array([reach] + counts)


def uneven(own_key, amount, total, bound, slope):
    if amount == 2:
        one = jax.random.randint(own_key, (), max(1, total - bound), min(bound, total - 1) + 1)
        return jnp.stack([one, total - one])
    tallies = jnp.asarray(length_profile(amount, total, bound, slope), jnp.int32)
    twos = (amount - 1) // 2
    source_of, sink = tallies[1:1 + 2 * twos:2], tallies[2:2 + 2 * twos:2]
    slack = jnp.minimum(source_of - 1, bound - sink)
    moved = jax.random.randint(jax.random.fold_in(own_key, 1), (twos,), 0, 1 << 20) % (slack + 1)
    tallies = tallies.at[1:1 + 2 * twos:2].set(source_of - moved).at[2:2 + 2 * twos:2].set(sink + moved)
    return tallies[jax.random.permutation(jax.random.fold_in(own_key, 2), amount)]


def normal_values(own_key, dims, deviation, reach, cuts=(), kind=jnp.bfloat16):
    gain = block_scale(own_key, dims, cuts, -0.22, 0.18) if cuts else 1.0
    result = jax.random.normal(own_key, dims, jnp.float32) * deviation * gain
    return jnp.minimum(jnp.maximum(result, -reach), reach).astype(kind)


def setup_inputs(seed: int = 0, part: int = 0) -> dict:
    arg_keys = jax.random.split(jax.random.key(seed), 10)
    own_keys = jax.random.split(jax.random.fold_in(arg_keys[9], part), 10)
    return {
        "queries": normal_values(own_keys[0], (HEAD_COUNT, PACKED_TOKENS, DK), 1.0, 6.0, ((1, 8),)),
        "key_pairs": normal_values(own_keys[1], (HEAD_COUNT, PACKED_TOKENS, 2 * DK), 1.0, 6.0, ((1, 8),)),
        "value_pairs": normal_values(own_keys[2], (HEAD_COUNT, PACKED_TOKENS, 2 * DV), 1.0, 6.0, ((1, 8),)),
        "strengths": draw_strengths(jax.random.fold_in(jax.random.fold_in(arg_keys[9], part), 71), part),
        "decays": draw_decays(jax.random.fold_in(jax.random.fold_in(arg_keys[9], part), 71), part),
        "conv_query": normal_values(arg_keys[5], (HEAD_COUNT, TAPS, DK), 0.5, 1.5, (), jnp.float32),
        "conv_key": normal_values(arg_keys[6], (HEAD_COUNT, TAPS, 2 * DK), 0.5, 1.5, (), jnp.float32),
        "conv_value": normal_values(arg_keys[7], (HEAD_COUNT, TAPS, 2 * DV), 0.5, 1.5, (), jnp.float32),
        "doc_lengths": uneven(own_keys[8], NDOCS, PACKED_TOKENS, MOST, 2).astype(jnp.int32),
    }


highest = lax.Precision.HIGHEST

def doc_starts(doc_lengths):
    ending = jnp.cumsum(doc_lengths).astype(jnp.int32)
    return (ending - doc_lengths).astype(jnp.int32)

def since_start(starts, offset, span_len):
    position = (offset + jnp.arange(span_len, dtype=jnp.int32)).astype(jnp.int32)
    reached = starts[None, :] <= position[:, None]
    latest = lax.optimization_barrier(jnp.max(jnp.where(reached, starts[None, :], 0), axis=1)).astype(jnp.int32)
    return (position - latest).astype(jnp.int32)

def short_conv(values, border, kernel, since):
    length = values.shape[1]
    border_len = border.shape[1]
    extended = jnp.concatenate([border, values], axis=1).astype(jnp.float32)
    summed = kernel[:, 0:1, :] * extended[:, border_len:, :]
    for lag_step in range(1, border_len + 1):
        shifted = extended[:, border_len - lag_step:border_len - lag_step + length, :]
        usable = (since >= lag_step)[None, :, None]
        summed = summed + jnp.where(usable, kernel[:, lag_step:lag_step + 1, :] * shifted, 0.0)
    return jax.nn.silu(summed)

def unit_rows(values, width):
    grouped = values.reshape(values.shape[0], -1, width)
    scale = lax.rsqrt(lax.optimization_barrier(jnp.sum(grouped * grouped, axis=-1, keepdims=True)) + 1e-06)
    return (grouped * scale).astype(jnp.bfloat16)

def prepare(queries, key_pairs, value_pairs, query_border, key_border, value_border, conv_query, conv_key, conv_value, since):
    heads = queries.shape[0]
    key_width = queries.shape[2]
    value_width = value_pairs.shape[2] // 2
    query_unit = unit_rows(short_conv(queries, query_border, conv_query, since), key_width)
    key_unit = unit_rows(short_conv(key_pairs, key_border, conv_key, since), key_width)
    value_unit = short_conv(value_pairs, value_border, conv_value, since).astype(jnp.bfloat16).reshape(heads, -1, value_width)
    return (query_unit, key_unit, value_unit)

def head_terms(query, keys, values, strength, decay, since):
    tokens_here = query.shape[0]
    steps = keys.shape[0]
    key_width = keys.shape[1]
    value_width = values.shape[1]
    log_gate = jnp.stack([-decay, jnp.zeros_like(decay)], axis=1).reshape(steps)
    opening = jnp.stack([since == 0, since < 0], axis=1).reshape(steps)
    running = jnp.cumsum(log_gate)
    segment = jnp.cumsum(opening.astype(jnp.int32)).astype(jnp.int32)
    sub_index = jnp.arange(steps, dtype=jnp.int32)
    linked = (segment[:, None] == segment[None, :]) & (sub_index[:, None] > sub_index[None, :])
    log_gap = jnp.where(linked, running[:, None] - running[None, :], 0.0)
    keys_wide = keys.astype(jnp.float32)
    intersection = jnp.einsum('sk,rk->sr', keys_wide, keys_wide, precision=highest)
    system = jnp.eye(steps, dtype=jnp.float32) + jnp.where(linked, strength[:, None] * jnp.exp(log_gap) * intersection, 0.0)
    open_gain = jnp.where(segment == 0, jnp.exp(running), 0.0)
    targets = jnp.concatenate([strength[:, None] * values.astype(jnp.float32), (strength * open_gain)[:, None] * keys_wide], axis=1)
    solved = jax.scipy.linalg.solve_triangular(system, targets, lower=True, unit_diagonal=True)
    end_gain = jnp.where(segment == segment[steps - 1], jnp.exp(running[steps - 1] - running), 0.0)
    weighted = keys_wide * end_gain[:, None]
    moved = jnp.einsum('nr,nk->rk', solved, weighted, precision=highest)
    transit = open_gain[steps - 1] * jnp.eye(key_width, dtype=jnp.float32) - moved[value_width:]
    carry_pair = jnp.concatenate([transit, moved[:value_width]], axis=0)
    out_rows = jnp.arange(tokens_here, dtype=jnp.int32) * 2 + 1
    out_segment = segment.reshape(tokens_here, 2)[:, 1]
    out_running = running.reshape(tokens_here, 2)[:, 1]
    reads = (out_segment[:, None] == segment[None, :]) & (out_rows[:, None] >= sub_index[None, :])
    read_gap = jnp.where(reads, out_running[:, None] - running[None, :], 0.0)
    query_wide = query.astype(jnp.float32)
    scores = jnp.einsum('ck,nk->cn', query_wide, keys_wide, precision=highest)
    mixing = jnp.where(reads, jnp.exp(read_gap) * scores, 0.0)
    gathered = jnp.dot(mixing.astype(jnp.float32), solved.astype(jnp.float32), precision=highest, preferred_element_type=jnp.float32)
    out_gain = open_gain.reshape(tokens_here, 2)[:, 1]
    correction = out_gain[:, None] * query_wide - gathered[:, value_width:]
    return (carry_pair, gathered[:, :value_width], correction)

def reference(queries, key_pairs, value_pairs, strengths, decays, conv_query, conv_key, conv_value, doc_lengths):
    starts = doc_starts(doc_lengths)
    heads = queries.shape[0]
    border_len = conv_query.shape[1] - 1

    def padded(values):
        return jnp.concatenate([jnp.zeros((heads, border_len, values.shape[2]), values.dtype), values], axis=1)
    padded_query = padded(queries)
    padded_key = padded(key_pairs)
    padded_value = padded(value_pairs)

    def one_stretch(state, index):
        offset = (index * TOKENS_PER_SHARD).astype(jnp.int32)
        since = since_start(starts, offset, TOKENS_PER_SHARD)

        def window(values):
            piece = lax.dynamic_slice_in_dim(values, offset, TOKENS_PER_SHARD + border_len, axis=1)
            return (piece[:, border_len:], piece[:, :border_len])
        query_here, query_border = window(padded_query)
        key_here, key_border = window(padded_key)
        value_here, value_border = window(padded_value)
        strength_here = lax.dynamic_slice_in_dim(strengths, (2 * offset).astype(jnp.int32), 2 * TOKENS_PER_SHARD, axis=1)
        decay_here = lax.dynamic_slice_in_dim(decays, offset, TOKENS_PER_SHARD, axis=1)
        query_unit, key_unit, value_unit = prepare(query_here, key_here, value_here, query_border, key_border, value_border, conv_query, conv_key, conv_value, since)

        def per_head(pieces):
            return head_terms(pieces[0], pieces[1], pieces[2], pieces[3], pieces[4], since)
        carry_pairs, local_out, correction = lax.map(per_head, (query_unit, key_unit, value_unit, strength_here, decay_here))
        stretch_out = (local_out + jnp.einsum('hck,hvk->hcv', correction, state, precision=highest)).astype(jnp.bfloat16)
        next_state = jnp.einsum('hvj,hjk->hvk', state, carry_pairs[:, :DK], precision=highest) + carry_pairs[:, DK:]
        return (next_state, stretch_out)
    initial = jnp.zeros((heads, DV, DK), jnp.float32)
    _, outputs = lax.scan(one_stretch, initial, jnp.arange(N_SEQ, dtype=jnp.int32))
    return jnp.transpose(outputs, (1, 0, 2, 3)).reshape(heads, PACKED_TOKENS, DV)
```

```python
import functools

import jax
import jax.numpy as jnp
from jax import lax
from jax.experimental import pallas as pl
from jax.experimental.pallas import tpu as pltpu
from jax.sharding import PartitionSpec as P

MESH = pl.DeviceIdType.MESH
BF = jnp.bfloat16
F32 = jnp.float32
GROUP = 8
PART = 4
ROWS = 8
NT = (((1,), (1,)), ((), ()))
NN = (((1,), (0,)), ((), ()))


def mm(a, b):
    return jnp.dot(a.astype(BF), b.astype(BF), preferred_element_type=F32)


def thirds(a):
    high = a.astype(BF)
    rest = a - high.astype(F32)
    middle = rest.astype(BF)
    return high, middle, (rest - middle.astype(F32)).astype(BF)


def iota(shape, axis):
    return lax.broadcasted_iota(jnp.int32, shape, axis)


def token_in_half(index):
    return index // ROWS + ROWS * (index % ROWS)


def kernel(
    n_seq,
    docs_hbm,
    q_hbm,
    k_hbm,
    v_hbm,
    strength_hbm,
    decay_hbm,
    cq_hbm,
    ck_hbm,
    cv_hbm,
    out_ref,
    docs_ref,
    q_ref,
    k_ref,
    v_ref,
    strength_ref,
    decay_ref,
    cq_ref,
    ck_ref,
    cv_ref,
    bq_ref,
    bk_ref,
    bv_ref,
    ext_ref,
    usable_ref,
    ordered_ref,
    reads_ref,
    open_ref,
    level_ref,
    rows_ref,
    open_lane_ref,
    run_cols_ref,
    keys_ref,
    solved_ref,
    rest_ref,
    middle_ref,
    spread_ref,
    terms_ref,
    transit_ref,
    local_ref,
    correction_ref,
    arrived_ref,
    leaving_ref,
    pair_in_ref,
    pair_out_ref,
    load_sem,
    border_send,
    border_recv,
    pair_send,
    pair_recv,
    state_send,
    state_recv,
    back_send,
    back_recv,
):
    heads, tokens, width = q_ref.shape
    half = tokens // 2
    steps = 2 * tokens
    parts = heads // GROUP
    me = lax.axis_index("seq")
    chip = me // 2
    chips = n_seq // 2
    upper = me % 2 == 1
    lower = me % 2 == 0
    offset = me * tokens
    has_left = me > 0
    has_right = me < n_seq - 1
    passes_on = upper & has_right
    barrier = pltpu.get_barrier_semaphore()

    @pl.when(has_left)
    def _():
        pl.semaphore_signal(barrier, inc=1, device_id={"seq": me - 1}, device_id_type=MESH)

    @pl.when(upper & (chip > 0))
    def _():
        pl.semaphore_signal(barrier, inc=1, device_id={"seq": me - 2}, device_id_type=MESH)

    @pl.when(lower)
    def _():
        pl.semaphore_signal(barrier, inc=1, device_id={"seq": me + 1}, device_id_type=MESH)

    spans = [pl.ds(part * GROUP, GROUP) for part in range(parts)]
    wide = [(q_hbm, q_ref), (k_hbm, k_ref), (v_hbm, v_ref)]
    small = [
        (docs_hbm, docs_ref),
        (decay_hbm, decay_ref),
        (strength_hbm, strength_ref),
        (cq_hbm, cq_ref),
        (ck_hbm, ck_ref),
        (cv_hbm, cv_ref),
    ]
    small_loads = [
        pltpu.make_async_copy(source, target, load_sem.at[i])
        for i, (source, target) in enumerate(small)
    ]
    wide_loads = [
        [
            pltpu.make_async_copy(
                source.at[span], target.at[span], load_sem.at[len(small) + 3 * part + i]
            )
            for i, (source, target) in enumerate(wide)
        ]
        for part, span in enumerate(spans)
    ]
    for copy in small_loads + sum(wide_loads, []):
        copy.start()

    def border_copies(part):
        return [
            pltpu.make_async_remote_copy(
                src_ref=source.at[spans[part], pl.ds(tokens - 16, 16), :],
                dst_ref=target.at[spans[part]],
                send_sem=border_send.at[which, part],
                recv_sem=border_recv.at[which, part],
                device_id={"seq": me + 1},
                device_id_type=MESH,
            )
            for which, (source, target) in enumerate(
                [(q_hbm, bq_ref), (k_hbm, bk_ref), (v_hbm, bv_ref)]
            )
        ]

    def pair_copy(head):
        return pltpu.make_async_remote_copy(
            src_ref=pair_out_ref.at[head],
            dst_ref=pair_in_ref.at[head],
            send_sem=pair_send.at[head],
            recv_sem=pair_recv.at[head],
            device_id={"seq": me + 1},
            device_id_type=MESH,
        )

    def state_copy(head):
        return pltpu.make_async_remote_copy(
            src_ref=leaving_ref.at[head],
            dst_ref=arrived_ref.at[head],
            send_sem=state_send.at[head],
            recv_sem=state_recv.at[head],
            device_id={"seq": me + 2},
            device_id_type=MESH,
        )

    def back_copy(head):
        return pltpu.make_async_remote_copy(
            src_ref=arrived_ref.at[head],
            dst_ref=arrived_ref.at[head],
            send_sem=back_send.at[head],
            recv_sem=back_recv.at[head],
            device_id={"seq": me - 1},
            device_id_type=MESH,
        )

    def send_borders():
        for part in range(parts):
            for copy in border_copies(part):
                copy.start()

    @pl.when(lower)
    def _():
        pl.semaphore_wait(barrier, 1)
        send_borders()

    @pl.when(passes_on)
    def _():
        pl.semaphore_wait(barrier, 3)
        send_borders()

    @pl.when(me == n_seq - 1)
    def _():
        pl.semaphore_wait(barrier, 1)

    @pl.when(me == 0)
    def _():
        bq_ref[...] = jnp.zeros_like(bq_ref)
        bk_ref[...] = jnp.zeros_like(bk_ref)
        bv_ref[...] = jnp.zeros_like(bv_ref)

    @pl.when(chip == 0)
    def _():
        arrived_ref[...] = jnp.zeros_like(arrived_ref)

    for copy in small_loads:
        copy.wait()

    starts = []
    total = jnp.int32(0)
    for m in range(docs_ref.shape[0]):
        starts.append(total)
        total = total + docs_ref[m]

    def latest_of(position):
        latest = jnp.zeros_like(position)
        for start in starts:
            latest = jnp.where(start <= position, start, latest)
        return latest

    def token_of(row):
        return (row // half) * half + token_in_half(row % half)

    def lane_token(lane):
        return (lane // tokens) * half + token_in_half(lane % half)

    square = (tokens, tokens)
    token_col = token_of(iota(square, 0))
    latest_col = latest_of(offset + token_col)
    since = offset + token_col - latest_col
    for lag in range(1, 4):
        usable_ref[lag - 1] = jnp.where(since >= lag, 1.0, 0.0)
    lane = iota((8, steps), 1)
    token_row = lane_token(lane)
    latest_row = latest_of(offset + token_row)
    half_start = offset + (lane // tokens) * half
    open_row = jnp.where(latest_row < half_start, 1.0, 0.0)
    final = [
        jnp.max(latest_row[:, h * tokens : (h + 1) * tokens], axis=1, keepdims=True)
        for h in range(2)
    ]
    same_row = jnp.where(
        latest_row == jnp.where(lane < tokens, final[0], final[1]), 1.0, 0.0
    )
    whole = [jnp.where(final[h] < offset + h * half, 1.0, 0.0) for h in range(2)]
    for h in range(2):
        here = slice(h * half, (h + 1) * half)
        lanes = slice(h * tokens, (h + 1) * tokens)
        sub_row = 2 * token_row[0:1, lanes] + (iota((1, tokens), 1) // half)
        token_here = jnp.concatenate([token_col[here], token_col[here]], axis=0)
        latest_here = jnp.concatenate([latest_col[here], latest_col[here]], axis=0)
        sub_col = 2 * token_here + iota(square, 0) // half
        linked = (latest_here == latest_row[0:1, lanes]) & (sub_col > sub_row)
        ordered_ref[h] = jnp.where(linked, -1.0, 0.0)
        reads = (latest_col[here] == latest_row[0:1, lanes]) & (
            token_col[here] >= token_row[0:1, lanes]
        )
        reads_ref[h] = jnp.where(reads, 1.0, 0.0)
    open_col = latest_col < offset + (iota(square, 0) // half) * half
    open_ref[...] = jnp.where(open_col, 1.0, 0.0)
    apart = token_in_half(iota(square, 0) % half) ^ token_in_half(iota(square, 1) % half)
    depth = jnp.zeros(square, F32)
    level = 1
    while level < half:
        depth = depth + jnp.where(apart >= level, 1.0, 0.0)
        level *= 2
    level_ref[...] = depth

    def exact(pieces, chosen, dims=NN):
        return sum(
            lax.dot_general(piece, chosen, dims, preferred_element_type=F32)
            for piece in pieces
        )

    sub_row = 2 * token_row[0:1] + (iota((1, steps), 1) % tokens) // half
    pick = jnp.where(iota((steps, steps), 0) == sub_row, 1.0, 0.0).astype(BF)
    beta = exact(thirds(strength_ref[...]), pick)
    decay = thirds(decay_ref[...])
    at = iota((tokens, steps), 0)
    lane_half = iota((tokens, steps), 1) // tokens
    middle = lane_half * half + half // 2
    opening = (at >= lane_half * half) & (at < middle)
    closing = (at >= middle) & (at < (lane_half + 1) * half)
    to_middle = jnp.exp(-exact(decay, jnp.where(opening, 1.0, 0.0).astype(BF)))
    to_end = jnp.exp(-exact(decay, jnp.where(closing, 1.0, 0.0).astype(BF)))
    open_lane_ref[...] = open_row
    whole_row = jnp.where(lane < tokens, whole[0], whole[1])
    for which, table in enumerate(
        (
            beta,
            beta * to_end * same_row[0:1],
            to_middle,
            to_middle * to_end * whole_row[0:1],
        )
    ):
        for h in range(2):
            place = (2 * which + h) * heads
            rows_ref[place : place + heads, :] = table[:, h * tokens : (h + 1) * tokens]
    middle_col = (token_col // half) * half + half // 2
    past_col = jnp.where(iota(square, 1) <= token_col, 1.0, 0.0) - jnp.where(
        iota(square, 1) < middle_col, 1.0, 0.0
    )
    past_col = past_col.astype(BF)
    from_middle_col = sum(
        lax.dot_general(past_col, piece, NT, preferred_element_type=F32)
        for piece in decay
    )
    run_cols_ref[0] = jnp.exp(-from_middle_col)
    run_cols_ref[1] = jnp.exp(from_middle_col)

    lane_head = iota((tokens, heads), 1)
    eye = jnp.where(iota((width, width), 0) == iota((width, width), 1), 1.0, 0.0)
    unit_eye = eye.astype(BF)
    both = range(GROUP)

    def convolved(u, head, lane, kernel_ref, column):
        taps = [kernel_ref[head, lag : lag + 1, column : column + width] for lag in range(4)]
        pieces = []
        for h in range(2):
            loaded = [
                ext_ref[u, lane, pl.ds(16 + h * half + k, ROWS, stride=half // ROWS), :]
                for k in range(-3, half // ROWS)
            ]
            for i in range(half // ROWS):
                rows = slice(h * half + i * ROWS, h * half + (i + 1) * ROWS)
                summed = taps[0] * loaded[i + 3]
                for lag in range(1, 4):
                    summed = summed + usable_ref[lag - 1, rows, :] * (
                        taps[lag] * loaded[i + 3 - lag]
                    )
                pieces.append(summed)
        summed = jnp.concatenate(pieces, axis=0)
        return summed / (1.0 + jnp.exp(-summed))

    def unit(rows):
        scale = lax.rsqrt(jnp.sum(rows * rows, axis=1, keepdims=True) + 1e-6)
        return (rows * scale).astype(BF)

    def column(which, head):
        return jnp.sum(
            jnp.where(lane_head == head, run_cols_ref[which], 0.0), axis=1, keepdims=True
        )

    def split(a):
        high = a.astype(BF)
        return high, (a - high.astype(F32)).astype(BF)

    def arranged(first, second):
        return [
            jnp.concatenate([first[h * half : (h + 1) * half], second[h * half : (h + 1) * half]], axis=0)
            for h in range(2)
        ]

    def local(part):
        ids = [part * GROUP + u for u in both]
        for u in both:
            head = ids[u]
            for j in range(2):
                lanes = slice(j * width, (j + 1) * width)
                ext_ref[u, 1 + j, 0:16] = bk_ref[head, :, lanes].astype(F32)
                ext_ref[u, 3 + j, 0:16] = bv_ref[head, :, lanes].astype(F32)
                ext_ref[u, 1 + j, 16 : 16 + tokens] = k_ref[head, :, lanes].astype(F32)
                ext_ref[u, 3 + j, 16 : 16 + tokens] = v_ref[head, :, lanes].astype(F32)
        keys = [
            arranged(
                unit(convolved(u, ids[u], 1, ck_ref, 0)),
                unit(convolved(u, ids[u], 2, ck_ref, width)),
            )
            for u in both
        ]
        def value(u, j):
            rows = convolved(u, ids[u], 3 + j, cv_ref, j * width).astype(BF).astype(F32)
            return (rows * column(1, ids[u])).astype(BF)

        waiting = [(u, j) for u in both for j in range(2)]
        ready = {}

        def some_values(count):
            for _ in range(min(count, len(waiting))):
                u, j = waiting.pop(0)
                ready[u, j] = value(u, j)

        sides = [(u, h) for u in both for h in range(2)]

        def row(which, u, h):
            return rows_ref[pl.ds((2 * which + h) * heads + ids[u], 1), :]

        products = [
            lax.dot_general(
                jnp.concatenate([keys[u][h], unit_eye], axis=0),
                keys[u][h],
                NT,
                preferred_element_type=F32,
            )
            for u, h in sides
        ]
        depth = level_ref[...]
        blocks = [
            (products[i][:tokens] * ordered_ref[h]) * row(0, u, h)
            for i, (u, h) in enumerate(sides)
        ]
        weighted = [
            (products[i][tokens:] * row(1, u, h)).astype(BF) for i, (u, h) in enumerate(sides)
        ]
        inverse = [jnp.where(depth == 0.0, block + eye, 0.0).astype(BF) for block in blocks]
        blocks = [block.astype(BF) for block in blocks]
        level = 1
        at_level = 1.0
        while level < half:
            inner = [mm(block, x) for block, x in zip(blocks, inverse)]
            outer = [mm(x, y) for x, y in zip(inverse, inner)]
            chosen = depth == at_level
            inverse = [
                jnp.where(chosen, z, x.astype(F32)).astype(BF) for z, x in zip(outer, inverse)
            ]
            level *= 2
            at_level += 1.0
            some_values(3)
        some_values(2 * GROUP)
        values = [arranged(ready[u, 0], ready[u, 1]) for u in both]
        scaled = [mm(inverse[i], values[u][h]) for i, (u, h) in enumerate(sides)]
        opens = [
            open_lane_ref[0:1, h * tokens : (h + 1) * tokens].astype(BF) for h in range(2)
        ]
        carried = [mm(inverse[i] * opens[h], keys[u][h]) for i, (u, h) in enumerate(sides)]
        start = [row(2, u, 0) for u in both]
        first = [
            split(jnp.concatenate([scaled[2 * u], carried[2 * u] * start[u]], axis=1))
            for u in both
        ]
        moved = [mm(weighted[2 * u], first[u][0]) for u in both]
        through = [[row(3, u, h) for h in range(2)] for u in both]
        terms = [moved[u][:, :width] for u in both]
        transit = [through[u][0] * eye - moved[u][:, width:] for u in both]
        later = [row(2, u, 1) for u in both]
        between = [
            jnp.concatenate(
                [(later[u] * terms[u]).astype(BF), (later[u] * transit[u]).astype(BF)], axis=1
            )
            for u in both
        ]
        brought = [mm(carried[2 * u + 1], between[u]) for u in both]
        second = [
            split(
                jnp.concatenate(
                    [scaled[2 * u + 1] - brought[u][:, :width], brought[u][:, width:]], axis=1
                )
            )
            for u in both
        ]
        moved = [mm(weighted[2 * u + 1], second[u][0]) for u in both]
        for u in both:
            term = through[u][1] * terms[u] + moved[u][:, :width]
            on = (through[u][1] * transit[u] - moved[u][:, width:]).astype(BF)
            terms_ref[ids[u]] = term
            transit_ref[ids[u]] = on
            pair_out_ref[ids[u]] = jnp.concatenate([term.astype(BF), on], axis=1)
            middle_ref[ids[u]] = between[u]
            for h, solved in enumerate((first[u], second[u])):
                keys_ref[ids[u], h] = keys[u][h]
                solved_ref[ids[u], h] = solved[0]
                rest_ref[ids[u], h] = solved[1]

    def read_local(part):
        some = range(PART)
        ids = [part * PART + u for u in some]
        for u in some:
            ext_ref[u, 0, 0:16] = bq_ref[ids[u]].astype(F32)
            ext_ref[u, 0, 16 : 16 + tokens] = q_ref[ids[u]].astype(F32)
        query = [unit(convolved(u, ids[u], 0, cq_ref, 0)) for u in some]
        sides = [(u, h) for u in some for h in range(2)]

        def side(rows, h):
            return rows[h * half : (h + 1) * half]

        def row(which, u, h):
            return rows_ref[pl.ds((2 * which + h) * heads + ids[u], 1), :]

        scores = [
            lax.dot_general(
                side(query[u], h), keys_ref[ids[u], h], NT, preferred_element_type=F32
            )
            for u, h in sides
        ]
        mixing = [
            split((scores[i] * reads_ref[h]) * row(0, u, h))
            for i, (u, h) in enumerate(sides)
        ]
        gathered = [
            mm(jnp.concatenate(mixing[i], axis=0), solved_ref[ids[u], h])
            for i, (u, h) in enumerate(sides)
        ]
        gathered = [
            gathered[i][:half] + (gathered[i][half:] + mm(mixing[i][0], rest_ref[ids[u], h]))
            for i, (u, h) in enumerate(sides)
        ]
        opened = [query[u].astype(F32) * open_ref[...] for u in some]
        brought = [mm(side(opened[u], 1), middle_ref[ids[u]]) for u in some]
        for u in some:
            start = row(2, u, 0)
            early, late = gathered[2 * u], gathered[2 * u + 1]
            local_ref[ids[u]] = jnp.concatenate(
                [early[:, :width], brought[u][:, :width] + late[:, :width]], axis=0
            )
            correction_ref[ids[u]] = jnp.concatenate(
                [
                    (start * side(opened[u], 0) - early[:, width:]).astype(BF),
                    (brought[u][:, width:] - late[:, width:]).astype(BF),
                ],
                axis=0,
            )

    def finish_rows(u, head, state):
        rows = local_ref[head] + mm(correction_ref[head], state)
        rows = rows * column(0, head)
        for h in range(2):
            for i in range(half // ROWS):
                spread_ref[u, pl.ds(h * half + i, ROWS, stride=half // ROWS), :] = rows[
                    h * half + i * ROWS : h * half + (i + 1) * ROWS
                ]
        out_ref[head] = spread_ref[u].astype(BF)

    some = range(PART)
    pieces = heads // PART
    each = GROUP // PART

    def compose(part):
        ids = [part * PART + u for u in some]
        for head in ids:
            pair_copy(head).wait_recv()
        composed = [mm(transit_ref[head], pair_in_ref[head]) for head in ids]
        for head, both_maps in zip(ids, composed):
            terms_ref[head] = terms_ref[head] + both_maps[:, :width]
            transit_ref[head] = both_maps[:, width:].astype(BF)

    def chain(part):
        for first in range(0, PART, 2):
            ids = [part * PART + first + u for u in range(2)]

            @pl.when(chip > 0)
            def _():
                for head in ids:
                    state_copy(head).wait_recv()

            @pl.when(has_right)
            def _():
                ends = [terms_ref[head] + mm(transit_ref[head], arrived_ref[head]) for head in ids]
                for head, end in zip(ids, ends):
                    leaving_ref[head] = end.astype(BF)
                for head in ids:
                    state_copy(head).start()

            @pl.when(chip > 0)
            def _():
                for head in ids:
                    back_copy(head).start()

    def read_upper(part):
        ids = [part * PART + u for u in some]
        inner = [
            mm(pair_in_ref[head, :, width:], arrived_ref[head])
            + pair_in_ref[head, :, :width].astype(F32)
            for head in ids
        ]
        for u in some:
            finish_rows(u, ids[u], inner[u])

    def read_lower(part):
        ids = [part * PART + u for u in some]

        @pl.when(chip > 0)
        def _():
            for head in ids:
                back_copy(head).wait_recv()

        for u in some:
            finish_rows(u, ids[u], arrived_ref[ids[u]])

    def first_phase(step, carry):
        for part in range(parts):

            @pl.when(step == part)
            def _():
                for copy in wide_loads[part]:
                    copy.wait()

                @pl.when(has_left)
                def _():
                    for copy in border_copies(part):
                        copy.wait_recv()

        local(step)

        @pl.when(lower)
        def _():
            for u in both:
                pair_copy(step * GROUP + u).start()

        for sub in range(each):

            @pl.when(upper & (step >= 1))
            def _():
                compose((step - 1) * each + sub)

            ready = (step - 1) * each + sub - chip

            @pl.when(upper & (step >= 1) & (ready >= 0))
            def _():
                chain(ready)

        return carry

    lax.fori_loop(0, parts, first_phase, 0)

    def second_phase(step, carry):
        read_local(step)
        return carry

    lax.fori_loop(0, pieces, second_phase, 0)
    done = (parts - 1) * each
    late = jnp.maximum(0, chip)

    def third_phase(step, carry):
        ready = step - chip

        @pl.when(upper & (step >= done) & (step < pieces))
        def _():
            compose(step)

        @pl.when(upper & (step >= done) & (ready >= 0) & (ready < pieces))
        def _():
            chain(ready)

        read = step - late

        @pl.when(upper & (read >= 0) & (read < pieces))
        def _():
            read_upper(read)

        @pl.when(lower & (read >= 0) & (read < pieces))
        def _():
            read_lower(read)

        return carry

    lax.fori_loop(0, pieces + chips - 1, third_phase, 0)

    @pl.when(has_right)
    def _():
        for part in range(parts):
            for copy in border_copies(part):
                copy.wait_send()

    @pl.when(lower)
    def _():
        def finish(head, carry):
            pair_copy(head).wait_send()
            return carry

        lax.fori_loop(0, heads, finish, 0)

    @pl.when(passes_on)
    def _():
        def finish(head, carry):
            state_copy(head).wait_send()
            return carry

        lax.fori_loop(0, heads, finish, 0)

    @pl.when(upper & (chip > 0))
    def _():
        def finish(head, carry):
            back_copy(head).wait_send()
            return carry

        lax.fori_loop(0, heads, finish, 0)


def body(
    queries,
    key_pairs,
    value_pairs,
    strengths,
    decays,
    conv_query,
    conv_key,
    conv_value,
    doc_lengths,
):
    heads, tokens, width = queries.shape
    n_seq = lax.axis_size("seq")
    steps = 2 * tokens
    vmem = pl.BlockSpec(memory_space=pltpu.VMEM)
    return pl.pallas_call(
        functools.partial(kernel, n_seq),
        out_shape=jax.ShapeDtypeStruct((heads, tokens, width), BF),
        in_specs=[pl.BlockSpec(memory_space=pltpu.HBM)] * 9,
        out_specs=vmem,
        scratch_shapes=[
            pltpu.SMEM(doc_lengths.shape, jnp.int32),
            pltpu.VMEM(queries.shape, BF),
            pltpu.VMEM(key_pairs.shape, BF),
            pltpu.VMEM(value_pairs.shape, BF),
            pltpu.VMEM(strengths.shape, F32),
            pltpu.VMEM(decays.shape, F32),
            pltpu.VMEM(conv_query.shape, F32),
            pltpu.VMEM(conv_key.shape, F32),
            pltpu.VMEM(conv_value.shape, F32),
            pltpu.VMEM((heads, 16, width), BF),
            pltpu.VMEM((heads, 16, 2 * width), BF),
            pltpu.VMEM((heads, 16, 2 * width), BF),
            pltpu.VMEM((GROUP, 5, 16 + tokens, width), F32),
            pltpu.VMEM((3, tokens, tokens), F32),
            pltpu.VMEM((2, tokens, tokens), F32),
            pltpu.VMEM((2, tokens // 2, tokens), F32),
            pltpu.VMEM((tokens, tokens), F32),
            pltpu.VMEM((tokens, tokens), F32),
            pltpu.VMEM((8 * heads, tokens), F32),
            pltpu.VMEM((8, steps), F32),
            pltpu.VMEM((2, tokens, heads), F32),
            pltpu.VMEM((heads, 2, tokens, width), BF),
            pltpu.VMEM((heads, 2, tokens, 2 * width), BF),
            pltpu.VMEM((heads, 2, tokens, 2 * width), BF),
            pltpu.VMEM((heads, width, 2 * width), BF),
            pltpu.VMEM((PART, tokens, width), F32),
            pltpu.VMEM((heads, width, width), F32),
            pltpu.VMEM((heads, width, width), BF),
            pltpu.VMEM((heads, tokens, width), F32),
            pltpu.VMEM((heads, tokens, width), BF),
            pltpu.VMEM((heads, width, width), BF),
            pltpu.VMEM((heads, width, width), BF),
            pltpu.VMEM((heads, width, 2 * width), BF),
            pltpu.VMEM((heads, width, 2 * width), BF),
            pltpu.SemaphoreType.DMA((6 + 3 * (heads // GROUP),)),
            pltpu.SemaphoreType.DMA((3, heads // GROUP)),
            pltpu.SemaphoreType.DMA((3, heads // GROUP)),
            pltpu.SemaphoreType.DMA((heads,)),
            pltpu.SemaphoreType.DMA((heads,)),
            pltpu.SemaphoreType.DMA((heads,)),
            pltpu.SemaphoreType.DMA((heads,)),
            pltpu.SemaphoreType.DMA((heads,)),
            pltpu.SemaphoreType.DMA((heads,)),
        ],
        compiler_params=pltpu.CompilerParams(
            collective_id=0, has_side_effects=True, vmem_limit_bytes=60 << 20
        ),
        name="delta_product",
    )(
        doc_lengths,
        queries,
        key_pairs,
        value_pairs,
        strengths,
        decays,
        conv_query,
        conv_key,
        conv_value,
    )


def solution(mesh):
    in_specs = (
        P(None, ("dp", "seq"), None),
        P(None, ("dp", "seq"), None),
        P(None, ("dp", "seq"), None),
        P(None, ("dp", "seq")),
        P(None, ("dp", "seq")),
        P(),
        P(),
        P(),
        P("dp"),
    )
    out_specs = P(None, ("dp", "seq"), None)
    return jax.shard_map(body, mesh=mesh, in_specs=in_specs, out_specs=out_specs, check_vma=False)
```

```python
import functools

import jax
import jax.numpy as jnp
from jax import lax
from jax.experimental import pallas as pl
from jax.experimental.pallas import tpu as pltpu
from jax.sharding import PartitionSpec as P

MESH = pl.DeviceIdType.MESH
BF = jnp.bfloat16
F32 = jnp.float32
GROUP = 8
PART = 4
ROWS = 8
NT = (((1,), (1,)), ((), ()))
NN = (((1,), (0,)), ((), ()))


def mm(a, b):
    return jnp.dot(a.astype(BF), b.astype(BF), preferred_element_type=F32)


def thirds(a):
    high = a.astype(BF)
    rest = a - high.astype(F32)
    middle = rest.astype(BF)
    return high, middle, (rest - middle.astype(F32)).astype(BF)


def iota(shape, axis):
    return lax.broadcasted_iota(jnp.int32, shape, axis)


def token_in_half(index):
    return index // ROWS + ROWS * (index % ROWS)


def kernel(
    n_seq,
    docs_hbm,
    q_hbm,
    k_hbm,
    v_hbm,
    strength_hbm,
    decay_hbm,
    cq_hbm,
    ck_hbm,
    cv_hbm,
    out_ref,
    docs_ref,
    q_ref,
    k_ref,
    v_ref,
    strength_ref,
    decay_ref,
    cq_ref,
    ck_ref,
    cv_ref,
    bq_ref,
    bk_ref,
    bv_ref,
    edge_out_ref,
    edge_in_ref,
    ext_ref,
    usable_ref,
    ordered_ref,
    reads_ref,
    open_ref,
    level_ref,
    rows_ref,
    open_lane_ref,
    run_cols_ref,
    weighted_ref,
    inverse_ref,
    system_ref,
    values_ref,
    keys_ref,
    solved_ref,
    rest_ref,
    middle_ref,
    spread_ref,
    terms_ref,
    transit_ref,
    local_ref,
    correction_ref,
    arrived_ref,
    leaving_ref,
    maps_ref,
    states_ref,
    given_ref,
    load_sem,
    border_send,
    border_recv,
    pair_send,
    pair_recv,
    state_send,
    state_recv,
    back_send,
    back_recv,
):
    heads, tokens, width = q_ref.shape
    half = tokens // 2
    steps = 2 * tokens
    parts = heads // GROUP
    me = lax.axis_index("seq")
    chip = me // 2
    chips = n_seq // 2
    upper = me % 2 == 1
    lower = me % 2 == 0
    offset = me * tokens
    has_left = me > 0
    has_right = me < n_seq - 1
    barrier = pltpu.get_barrier_semaphore()

    side = me % 2
    partner = me + 1 - 2 * side
    forwards = chip < chips - 1
    pl.semaphore_signal(barrier, inc=1, device_id={"seq": partner}, device_id_type=MESH)

    @pl.when(lower & has_left)
    def _():
        pl.semaphore_signal(barrier, inc=1, device_id={"seq": me - 1}, device_id_type=MESH)

    @pl.when(chip > 0)
    def _():
        pl.semaphore_signal(barrier, inc=1, device_id={"seq": me - 2}, device_id_type=MESH)

    spans = [pl.ds(part * GROUP, GROUP) for part in range(parts)]
    wide = [(q_hbm, q_ref), (k_hbm, k_ref), (v_hbm, v_ref)]
    small = [
        (docs_hbm, docs_ref),
        (decay_hbm, decay_ref),
        (strength_hbm, strength_ref),
        (cq_hbm, cq_ref),
        (ck_hbm, ck_ref),
        (cv_hbm, cv_ref),
    ]
    small_loads = [
        pltpu.make_async_copy(source, target, load_sem.at[i])
        for i, (source, target) in enumerate(small)
    ]
    wide_loads = [
        [
            pltpu.make_async_copy(
                source.at[span], target.at[span], load_sem.at[len(small) + 3 * part + i]
            )
            for i, (source, target) in enumerate(wide)
        ]
        for part, span in enumerate(spans)
    ]
    tails = [
        pltpu.make_async_copy(
            source.at[:, pl.ds(tokens - 16, 16), :], target, load_sem.at[len(small) + 3 * parts + i]
        )
        for i, (source, target) in enumerate([(q_hbm, bq_ref), (k_hbm, bk_ref), (v_hbm, bv_ref)])
    ]
    for copy in tails + small_loads + sum(wide_loads, []):
        copy.start()

    border_copy = pltpu.make_async_remote_copy(
        src_ref=edge_out_ref,
        dst_ref=edge_in_ref,
        send_sem=border_send,
        recv_sem=border_recv,
        device_id={"seq": me + 1},
        device_id_type=MESH,
    )
    columns = [(bq_ref, 0), (bk_ref, 0), (bk_ref, width), (bv_ref, 0), (bv_ref, width)]

    def pack_edges():
        low = iota((ROWS, width), 0) < 4
        for place, (tail_ref, lane) in enumerate(columns):
            for quad in range(heads // 4):
                rows = [
                    tail_ref[4 * quad + i, :, lane : lane + width].astype(F32)[8:16]
                    for i in range(4)
                ]
                tiles = [
                    jnp.where(low, pltpu.roll(rows[2 * i], 4, 0), rows[2 * i + 1])
                    for i in range(2)
                ]
                edge_out_ref[16 * quad : 16 * quad + 16, place * width : (place + 1) * width] = (
                    jnp.concatenate(tiles, axis=0).astype(BF)
                )

    def place_edge(u, quad, place):
        rows = edge_in_ref[
            pl.ds(pl.multiple_of(16 * quad, 16), 16), place * width : (place + 1) * width
        ].astype(F32)
        tile = rows[8 * (u % 4 // 2) : 8 * (u % 4 // 2) + 8]
        ext_ref[u, place, 8:16] = pltpu.roll(tile, 4, 0) if u % 2 == 0 else tile

    def exchange(source, target, head, sends, receives, device):
        return pltpu.make_async_remote_copy(
            src_ref=source,
            dst_ref=target,
            send_sem=sends.at[head],
            recv_sem=receives.at[head],
            device_id={"seq": device},
            device_id_type=MESH,
        )

    def pair_copy(head):
        place = maps_ref.at[head, side]
        return exchange(place, place, head, pair_send, pair_recv, partner)

    def pair_arrival(head):
        place = maps_ref.at[head, 1 - side]
        return exchange(place, place, head, pair_send, pair_recv, partner)

    def state_copy(head):
        return exchange(
            leaving_ref.at[head], arrived_ref.at[head], head, state_send, state_recv, me + 2
        )

    def back_copy(head):
        return exchange(
            given_ref.at[head], states_ref.at[head], head, back_send, back_recv, partner
        )

    for copy in tails:
        copy.wait()
    pack_edges()

    @pl.when(forwards)
    def _():
        pl.semaphore_wait(barrier, 2 + side)

    @pl.when(jnp.logical_not(forwards))
    def _():
        pl.semaphore_wait(barrier, 1)

    @pl.when(has_right)
    def _():
        border_copy.start()

    @pl.when(me == 0)
    def _():
        edge_in_ref[...] = jnp.zeros_like(edge_in_ref)

    @pl.when(chip == 0)
    def _():
        arrived_ref[...] = jnp.zeros_like(arrived_ref)

    for copy in small_loads:
        copy.wait()

    starts = []
    total = jnp.int32(0)
    for m in range(docs_ref.shape[0]):
        starts.append(total)
        total = total + docs_ref[m]

    def latest_of(position):
        latest = jnp.zeros_like(position)
        for start in starts:
            latest = jnp.where(start <= position, start, latest)
        return latest

    def token_of(row):
        return (row // half) * half + token_in_half(row % half)

    def lane_token(lane):
        return (lane // tokens) * half + token_in_half(lane % half)

    square = (tokens, tokens)
    token_col = token_of(iota(square, 0))
    latest_col = latest_of(offset + token_col)
    since = offset + token_col - latest_col
    for lag in range(1, 4):
        usable_ref[lag - 1] = jnp.where(since >= lag, 1.0, 0.0)
    lane = iota((8, steps), 1)
    token_row = lane_token(lane)
    latest_row = latest_of(offset + token_row)
    half_start = offset + (lane // tokens) * half
    open_row = jnp.where(latest_row < half_start, 1.0, 0.0)
    final = [
        jnp.max(latest_row[:, h * tokens : (h + 1) * tokens], axis=1, keepdims=True)
        for h in range(2)
    ]
    same_row = jnp.where(
        latest_row == jnp.where(lane < tokens, final[0], final[1]), 1.0, 0.0
    )
    whole = [jnp.where(final[h] < offset + h * half, 1.0, 0.0) for h in range(2)]
    for h in range(2):
        here = slice(h * half, (h + 1) * half)
        lanes = slice(h * tokens, (h + 1) * tokens)
        sub_row = 2 * token_row[0:1, lanes] + (iota((1, tokens), 1) // half)
        token_here = jnp.concatenate([token_col[here], token_col[here]], axis=0)
        latest_here = jnp.concatenate([latest_col[here], latest_col[here]], axis=0)
        sub_col = 2 * token_here + iota(square, 0) // half
        linked = (latest_here == latest_row[0:1, lanes]) & (sub_col > sub_row)
        ordered_ref[h] = jnp.where(linked, -1.0, 0.0)
        reads = (latest_col[here] == latest_row[0:1, lanes]) & (
            token_col[here] >= token_row[0:1, lanes]
        )
        reads_ref[h] = jnp.where(reads, 1.0, 0.0)
    open_col = latest_col < offset + (iota(square, 0) // half) * half
    open_ref[...] = jnp.where(open_col, 1.0, 0.0)
    apart = token_in_half(iota(square, 0) % half) ^ token_in_half(iota(square, 1) % half)
    depth = jnp.zeros(square, F32)
    level = 1
    while level < half:
        depth = depth + jnp.where(apart >= level, 1.0, 0.0)
        level *= 2
    level_ref[...] = depth

    def exact(pieces, chosen, dims=NN):
        return sum(
            lax.dot_general(piece, chosen, dims, preferred_element_type=F32)
            for piece in pieces
        )

    sub_row = 2 * token_row[0:1] + (iota((1, steps), 1) % tokens) // half
    pick = jnp.where(iota((steps, steps), 0) == sub_row, 1.0, 0.0).astype(BF)
    beta = exact(thirds(strength_ref[...]), pick)
    decay = thirds(decay_ref[...])
    at = iota((tokens, steps), 0)
    lane_half = iota((tokens, steps), 1) // tokens
    middle = lane_half * half + half // 2
    opening = (at >= lane_half * half) & (at < middle)
    closing = (at >= middle) & (at < (lane_half + 1) * half)
    to_middle = jnp.exp(-exact(decay, jnp.where(opening, 1.0, 0.0).astype(BF)))
    to_end = jnp.exp(-exact(decay, jnp.where(closing, 1.0, 0.0).astype(BF)))
    open_lane_ref[...] = open_row
    whole_row = jnp.where(lane < tokens, whole[0], whole[1])
    for which, table in enumerate(
        (
            beta,
            beta * to_end * same_row[0:1],
            to_middle,
            to_middle * to_end * whole_row[0:1],
        )
    ):
        for h in range(2):
            place = (2 * which + h) * heads
            rows_ref[place : place + heads, :] = table[:, h * tokens : (h + 1) * tokens]
    middle_col = (token_col // half) * half + half // 2
    past_col = jnp.where(iota(square, 1) <= token_col, 1.0, 0.0) - jnp.where(
        iota(square, 1) < middle_col, 1.0, 0.0
    )
    past_col = past_col.astype(BF)
    from_middle_col = sum(
        lax.dot_general(past_col, piece, NT, preferred_element_type=F32)
        for piece in decay
    )
    run_cols_ref[0] = jnp.exp(-from_middle_col)
    run_cols_ref[1] = jnp.exp(from_middle_col)

    lane_head = iota((tokens, heads), 1)
    eye = jnp.where(iota((width, width), 0) == iota((width, width), 1), 1.0, 0.0)
    unit_eye = eye.astype(BF)
    both = range(GROUP)

    def convolved(u, head, lane, kernel_ref, column):
        taps = [kernel_ref[head, lag : lag + 1, column : column + width] for lag in range(4)]
        pieces = []
        for h in range(2):
            loaded = [
                ext_ref[u, lane, pl.ds(16 + h * half + k, ROWS, stride=half // ROWS), :]
                for k in range(-3, half // ROWS)
            ]
            for i in range(half // ROWS):
                rows = slice(h * half + i * ROWS, h * half + (i + 1) * ROWS)
                summed = taps[0] * loaded[i + 3]
                for lag in range(1, 4):
                    summed = summed + usable_ref[lag - 1, rows, :] * (
                        taps[lag] * loaded[i + 3 - lag]
                    )
                pieces.append(summed)
        summed = jnp.concatenate(pieces, axis=0)
        return summed / (1.0 + jnp.exp(-summed))

    def unit(rows):
        scale = lax.rsqrt(jnp.sum(rows * rows, axis=1, keepdims=True) + 1e-6)
        return (rows * scale).astype(BF)

    def column(which, head):
        return jnp.sum(
            jnp.where(lane_head == head, run_cols_ref[which], 0.0), axis=1, keepdims=True
        )

    def split(a):
        high = a.astype(BF)
        return high, (a - high.astype(F32)).astype(BF)

    def arranged(first, second):
        return [
            jnp.concatenate([first[h * half : (h + 1) * half], second[h * half : (h + 1) * half]], axis=0)
            for h in range(2)
        ]

    def prepare(part):
        ids = [part * GROUP + u for u in both]
        for u in both:
            head = ids[u]
            for j in range(2):
                lanes = slice(j * width, (j + 1) * width)
                place_edge(u, part * (GROUP // 4) + u // 4, 1 + j)
                place_edge(u, part * (GROUP // 4) + u // 4, 3 + j)
                ext_ref[u, 1 + j, 16 : 16 + tokens] = k_ref[head, :, lanes].astype(F32)
                ext_ref[u, 3 + j, 16 : 16 + tokens] = v_ref[head, :, lanes].astype(F32)
        keys = [
            arranged(
                unit(convolved(u, ids[u], 1, ck_ref, 0)),
                unit(convolved(u, ids[u], 2, ck_ref, width)),
            )
            for u in both
        ]
        for u in both:
            scale = column(1, ids[u])
            for j in range(2):
                rows = convolved(u, ids[u], 3 + j, cv_ref, j * width).astype(BF).astype(F32)
                rows = (rows * scale).astype(BF)
                for h in range(2):
                    values_ref[u, h, j * half : (j + 1) * half] = rows[h * half : (h + 1) * half]

        sides = [(u, h) for u in both for h in range(2)]

        def row(which, u, h):
            return rows_ref[pl.ds((2 * which + h) * heads + ids[u], 1), :]

        products = [
            lax.dot_general(
                jnp.concatenate([keys[u][h], unit_eye], axis=0),
                keys[u][h],
                NT,
                preferred_element_type=F32,
            )
            for u, h in sides
        ]
        for u, h in sides:
            keys_ref[ids[u], h] = keys[u][h]
        depth = level_ref[...]
        blocks = [
            (products[i][:tokens] * ordered_ref[h]) * row(0, u, h)
            for i, (u, h) in enumerate(sides)
        ]
        for i, (u, h) in enumerate(sides):
            weighted_ref[i] = (products[i][tokens:] * row(1, u, h)).astype(BF)
        for i, block in enumerate(blocks):
            inverse_ref[i] = jnp.where(depth == 0.0, block + eye, 0.0).astype(BF)
            system_ref[i] = block.astype(BF)

    def invert():
        depth = level_ref[...]
        for level in range(int(half).bit_length() - 1):
            inner = [mm(system_ref[i], inverse_ref[i]).astype(BF) for i in range(2 * GROUP)]
            chosen = depth == level + 1.0
            for i in range(2 * GROUP):
                outer = mm(inverse_ref[i], inner[i])
                inverse_ref[i] = jnp.where(chosen, outer, inverse_ref[i].astype(F32)).astype(BF)

    def solve(part):
        ids = [part * GROUP + u for u in both]
        sides = [(u, h) for u in both for h in range(2)]

        def row(which, u, h):
            return rows_ref[pl.ds((2 * which + h) * heads + ids[u], 1), :]

        scaled = [mm(inverse_ref[i], values_ref[u, h]) for i, (u, h) in enumerate(sides)]
        opens = [
            open_lane_ref[0:1, h * tokens : (h + 1) * tokens].astype(BF) for h in range(2)
        ]
        carried = [mm(inverse_ref[i] * opens[h], keys_ref[ids[u], h]) for i, (u, h) in enumerate(sides)]
        start = [row(2, u, 0) for u in both]
        first = [
            split(jnp.concatenate([scaled[2 * u], carried[2 * u] * start[u]], axis=1))
            for u in both
        ]
        moved = [mm(weighted_ref[2 * u], first[u][0]) for u in both]
        through = [[row(3, u, h) for h in range(2)] for u in both]
        terms = [moved[u][:, :width] for u in both]
        transit = [through[u][0] * eye - moved[u][:, width:] for u in both]
        later = [row(2, u, 1) for u in both]
        between = [
            jnp.concatenate(
                [(later[u] * terms[u]).astype(BF), (later[u] * transit[u]).astype(BF)], axis=1
            )
            for u in both
        ]
        brought = [mm(carried[2 * u + 1], between[u]) for u in both]
        second = [
            split(
                jnp.concatenate(
                    [scaled[2 * u + 1] - brought[u][:, :width], brought[u][:, width:]], axis=1
                )
            )
            for u in both
        ]
        moved = [mm(weighted_ref[2 * u + 1], second[u][0]) for u in both]
        for u in both:
            term = through[u][1] * terms[u] + moved[u][:, :width]
            on = (through[u][1] * transit[u] - moved[u][:, width:]).astype(BF)
            maps_ref[ids[u], side] = jnp.concatenate([term.astype(BF), on], axis=1)
            middle_ref[ids[u]] = between[u]
            for h, solved in enumerate((first[u], second[u])):
                solved_ref[ids[u], h] = solved[0]
                rest_ref[ids[u], h] = solved[1]

    def read_local(part):
        some = range(PART)
        ids = [part * PART + u for u in some]
        for u in some:
            place_edge(u, part, 0)
            ext_ref[u, 0, 16 : 16 + tokens] = q_ref[ids[u]].astype(F32)
        query = [unit(convolved(u, ids[u], 0, cq_ref, 0)) for u in some]
        sides = [(u, h) for u in some for h in range(2)]

        def here(rows, h):
            return rows[h * half : (h + 1) * half]

        def row(which, u, h):
            return rows_ref[pl.ds((2 * which + h) * heads + ids[u], 1), :]

        scores = [
            lax.dot_general(
                here(query[u], h), keys_ref[ids[u], h], NT, preferred_element_type=F32
            )
            for u, h in sides
        ]
        mixing = [
            split((scores[i] * reads_ref[h]) * row(0, u, h))
            for i, (u, h) in enumerate(sides)
        ]
        gathered = [
            mm(jnp.concatenate(mixing[i], axis=0), solved_ref[ids[u], h])
            for i, (u, h) in enumerate(sides)
        ]
        gathered = [
            gathered[i][:half] + (gathered[i][half:] + mm(mixing[i][0], rest_ref[ids[u], h]))
            for i, (u, h) in enumerate(sides)
        ]
        opened = [query[u].astype(F32) * open_ref[...] for u in some]
        brought = [mm(here(opened[u], 1), middle_ref[ids[u]]) for u in some]
        for u in some:
            start = row(2, u, 0)
            early, late = gathered[2 * u], gathered[2 * u + 1]
            local_ref[ids[u]] = jnp.concatenate(
                [early[:, :width], brought[u][:, :width] + late[:, :width]], axis=0
            )
            correction_ref[ids[u]] = jnp.concatenate(
                [
                    (start * here(opened[u], 0) - early[:, width:]).astype(BF),
                    (brought[u][:, width:] - late[:, width:]).astype(BF),
                ],
                axis=0,
            )

    def finish_rows(u, head, state):
        rows = local_ref[head] + mm(correction_ref[head], state)
        rows = rows * column(0, head)
        for h in range(2):
            for i in range(half // ROWS):
                spread_ref[u, pl.ds(h * half + i, ROWS, stride=half // ROWS), :] = rows[
                    h * half + i * ROWS : h * half + (i + 1) * ROWS
                ]
        out_ref[head] = spread_ref[u].astype(BF)

    some = range(PART)
    pieces = heads // PART
    owned = GROUP // 2
    items = heads // 4

    def mine(index):
        return (index // owned) * GROUP + side * owned + index % owned

    def theirs(index):
        return (index // owned) * GROUP + (1 - side) * owned + index % owned

    def send_maps(part):
        for u in range(owned):
            pair_copy(theirs(part * owned + u)).start()

    def compose(part):
        ids = [mine(part * owned + u) for u in range(owned)]
        for head in ids:
            pair_arrival(head).wait_recv()
        composed = [mm(maps_ref[head, 1, :, width:], maps_ref[head, 0]) for head in ids]
        for head, both_maps in zip(ids, composed):
            terms_ref[head] = maps_ref[head, 1, :, :width].astype(F32) + both_maps[:, :width]
            transit_ref[head] = both_maps[:, width:].astype(BF)

    def chain(item):
        ids = [mine(2 * item + u) for u in range(2)]

        @pl.when(chip > 0)
        def _():
            for head in ids:
                state_copy(head).wait_recv()

        @pl.when(forwards)
        def _():
            ends = [terms_ref[head] + mm(transit_ref[head], arrived_ref[head]) for head in ids]
            for head, end in zip(ids, ends):
                leaving_ref[head] = end.astype(BF)
            for head in ids:
                state_copy(head).start()

        inner = [
            (
                mm(maps_ref[head, 0, :, width:], arrived_ref[head])
                + maps_ref[head, 0, :, :width].astype(F32)
            ).astype(BF)
            for head in ids
        ]

        @pl.when(lower)
        def _():
            for head, state in zip(ids, inner):
                given_ref[head] = state
                states_ref[head] = arrived_ref[head]

        @pl.when(upper)
        def _():
            for head, state in zip(ids, inner):
                states_ref[head] = state
                given_ref[head] = arrived_ref[head]

        for head in ids:
            back_copy(head).start()

    def read(part):
        ids = [part * PART + u for u in some]

        @pl.when(part % 2 != side)
        def _():
            for head in ids:
                back_copy(head).wait_recv()

        for u in some:
            finish_rows(u, ids[u], states_ref[ids[u]])

    early = items // parts

    def chain_some(slot, first, last):
        later = jnp.where(chip == 0, 0, jnp.where(chip == 1, pieces - 1, pieces + 3))

        def one(item, carry):
            soon = jnp.where(chip == 2, pieces - early + item, pieces)
            final = jnp.where(chip == 2, pieces, later)
            when = jnp.where(item < early, jnp.where(chip < 2, -1, soon), final)

            @pl.when(when == slot)
            def _():
                chain(item)

            return carry

        lax.fori_loop(first, last, one, 0)

    def first_phase(step, carry):
        for part in range(parts):

            @pl.when(step == part)
            def _():
                for copy in wide_loads[part]:
                    copy.wait()


        @pl.when((step == 0) & has_left)
        def _():
            border_copy.wait_recv()

        prepare(step)

        @pl.when(step == 1)
        def _():
            compose(0)

            @pl.when(chip == 0)
            def _():
                lax.fori_loop(0, early, lambda item, none: (chain(item), none)[1], 0)

        invert()
        solve(step)
        send_maps(step)
        return carry

    lax.fori_loop(0, parts, first_phase, 0)

    @pl.when(chip == 1)
    def _():
        lax.fori_loop(0, early, lambda item, none: (chain(item), none)[1], 0)

    def second_phase(slot, carry):
        @pl.when(slot < pieces)
        def _():
            read_local(slot)

        @pl.when(slot == 0)
        def _():
            compose(1)

        chain_some(slot, 0, items)

        @pl.when(slot > pieces)
        def _():
            read(slot - pieces - 1)

        return carry

    lax.fori_loop(0, 2 * pieces + 1, second_phase, 0)

    @pl.when(has_right)
    def _():
        border_copy.wait_send()

    def finish(index, carry):
        pair_copy(theirs(index)).wait_send()
        back_copy(mine(index)).wait_send()

        @pl.when(forwards)
        def _():
            state_copy(mine(index)).wait_send()

        return carry

    lax.fori_loop(0, heads // 2, finish, 0)


def body(
    queries,
    key_pairs,
    value_pairs,
    strengths,
    decays,
    conv_query,
    conv_key,
    conv_value,
    doc_lengths,
):
    heads, tokens, width = queries.shape
    n_seq = lax.axis_size("seq")
    steps = 2 * tokens
    vmem = pl.BlockSpec(memory_space=pltpu.VMEM)
    return pl.pallas_call(
        functools.partial(kernel, n_seq),
        out_shape=pltpu.VMEM((heads, tokens, width), BF),
        in_specs=[pl.BlockSpec(memory_space=pltpu.HBM)] * 9,
        out_specs=vmem,
        scratch_shapes=[
            pltpu.SMEM(doc_lengths.shape, jnp.int32),
            pltpu.VMEM(queries.shape, BF),
            pltpu.VMEM(key_pairs.shape, BF),
            pltpu.VMEM(value_pairs.shape, BF),
            pltpu.VMEM(strengths.shape, F32),
            pltpu.VMEM(decays.shape, F32),
            pltpu.VMEM(conv_query.shape, F32),
            pltpu.VMEM(conv_key.shape, F32),
            pltpu.VMEM(conv_value.shape, F32),
            pltpu.VMEM((heads, 16, width), BF),
            pltpu.VMEM((heads, 16, 2 * width), BF),
            pltpu.VMEM((heads, 16, 2 * width), BF),
            pltpu.VMEM((4 * heads, 5 * width), BF),
            pltpu.VMEM((4 * heads, 5 * width), BF),
            pltpu.VMEM((GROUP, 5, 16 + tokens, width), F32),
            pltpu.VMEM((3, tokens, tokens), F32),
            pltpu.VMEM((2, tokens, tokens), F32),
            pltpu.VMEM((2, tokens // 2, tokens), F32),
            pltpu.VMEM((tokens, tokens), F32),
            pltpu.VMEM((tokens, tokens), F32),
            pltpu.VMEM((8 * heads, tokens), F32),
            pltpu.VMEM((8, steps), F32),
            pltpu.VMEM((2, tokens, heads), F32),
            pltpu.VMEM((2 * GROUP, tokens, tokens), BF),
            pltpu.VMEM((2 * GROUP, tokens, tokens), BF),
            pltpu.VMEM((2 * GROUP, tokens, tokens), BF),
            pltpu.VMEM((GROUP, 2, tokens, width), BF),
            pltpu.VMEM((heads, 2, tokens, width), BF),
            pltpu.VMEM((heads, 2, tokens, 2 * width), BF),
            pltpu.VMEM((heads, 2, tokens, 2 * width), BF),
            pltpu.VMEM((heads, width, 2 * width), BF),
            pltpu.VMEM((PART, tokens, width), F32),
            pltpu.VMEM((heads, width, width), F32),
            pltpu.VMEM((heads, width, width), BF),
            pltpu.VMEM((heads, tokens, width), F32),
            pltpu.VMEM((heads, tokens, width), BF),
            pltpu.VMEM((heads, width, width), BF),
            pltpu.VMEM((heads, width, width), BF),
            pltpu.VMEM((heads, 2, width, 2 * width), BF),
            pltpu.VMEM((heads, width, width), BF),
            pltpu.VMEM((heads, width, width), BF),
            pltpu.SemaphoreType.DMA((9 + 3 * (heads // GROUP),)),
            pltpu.SemaphoreType.DMA,
            pltpu.SemaphoreType.DMA,
            pltpu.SemaphoreType.DMA((heads,)),
            pltpu.SemaphoreType.DMA((heads,)),
            pltpu.SemaphoreType.DMA((heads,)),
            pltpu.SemaphoreType.DMA((heads,)),
            pltpu.SemaphoreType.DMA((heads,)),
            pltpu.SemaphoreType.DMA((heads,)),
        ],
        compiler_params=pltpu.CompilerParams(
            collective_id=0, has_side_effects=True, vmem_limit_bytes=60 << 20
        ),
        name="delta_product",
    )(
        doc_lengths,
        queries,
        key_pairs,
        value_pairs,
        strengths,
        decays,
        conv_query,
        conv_key,
        conv_value,
    )


def solution(mesh):
    in_specs = (
        P(None, ("dp", "seq"), None),
        P(None, ("dp", "seq"), None),
        P(None, ("dp", "seq"), None),
        P(None, ("dp", "seq")),
        P(None, ("dp", "seq")),
        P(),
        P(),
        P(),
        P("dp"),
    )
    out_specs = P(None, ("dp", "seq"), None)
    return jax.shard_map(body, mesh=mesh, in_specs=in_specs, out_specs=out_specs, check_vma=False)
```

```python
import functools

import jax
import jax.numpy as jnp
from jax import lax
from jax.experimental import pallas as pl
from jax.experimental.pallas import tpu as pltpu
from jax.sharding import PartitionSpec as P

MESH = pl.DeviceIdType.MESH
BF = jnp.bfloat16
F32 = jnp.float32
GROUP = 8
PART = 4
TOGETHER = 1
ROWS = 8
NT = (((1,), (1,)), ((), ()))
NN = (((1,), (0,)), ((), ()))


def mm(a, b):
    return jnp.dot(a.astype(BF), b.astype(BF), preferred_element_type=F32)


def thirds(a):
    high = a.astype(BF)
    rest = a - high.astype(F32)
    middle = rest.astype(BF)
    return high, middle, (rest - middle.astype(F32)).astype(BF)


def iota(shape, axis):
    return lax.broadcasted_iota(jnp.int32, shape, axis)


def token_in_half(index):
    return index // ROWS + ROWS * (index % ROWS)


def kernel(
    n_seq,
    docs_hbm,
    q_hbm,
    k_hbm,
    v_hbm,
    strength_hbm,
    decay_hbm,
    cq_hbm,
    ck_hbm,
    cv_hbm,
    out_ref,
    docs_ref,
    q_ref,
    k_ref,
    v_ref,
    strength_ref,
    decay_ref,
    cq_ref,
    ck_ref,
    cv_ref,
    bq_ref,
    bk_ref,
    bv_ref,
    edge_out_ref,
    edge_in_ref,
    ext_ref,
    usable_ref,
    ordered_ref,
    reads_ref,
    open_ref,
    level_ref,
    rows_ref,
    open_lane_ref,
    run_cols_ref,
    weighted_ref,
    inverse_ref,
    system_ref,
    values_ref,
    keys_ref,
    solved_ref,
    rest_ref,
    middle_ref,
    spread_ref,
    terms_ref,
    transit_ref,
    local_ref,
    correction_ref,
    leaving_ref,
    maps_ref,
    states_ref,
    load_sem,
    border_send,
    border_recv,
    pair_send,
    pair_recv,
    state_send,
    state_recv,
    back_send,
    back_recv,
):
    heads, tokens, width = q_ref.shape
    half = tokens // 2
    steps = 2 * tokens
    parts = heads // GROUP
    me = lax.axis_index("seq")
    chip = me // 2
    chips = n_seq // 2
    upper = me % 2 == 1
    lower = me % 2 == 0
    offset = me * tokens
    has_left = me > 0
    has_right = me < n_seq - 1
    barrier = pltpu.get_barrier_semaphore()

    side = me % 2
    partner = me + 1 - 2 * side
    forwards = chip < chips - 1
    pl.semaphore_signal(barrier, inc=1, device_id={"seq": partner}, device_id_type=MESH)

    @pl.when(lower & has_left)
    def _():
        pl.semaphore_signal(barrier, inc=1, device_id={"seq": me - 1}, device_id_type=MESH)

    @pl.when(chip > 0)
    def _():
        pl.semaphore_signal(barrier, inc=1, device_id={"seq": me - 2}, device_id_type=MESH)

    spans = [pl.ds(part * GROUP, GROUP) for part in range(parts)]
    wide = [(q_hbm, q_ref), (k_hbm, k_ref), (v_hbm, v_ref)]
    small = [
        (docs_hbm, docs_ref),
        (decay_hbm, decay_ref),
        (strength_hbm, strength_ref),
        (cq_hbm, cq_ref),
        (ck_hbm, ck_ref),
        (cv_hbm, cv_ref),
    ]
    small_loads = [
        pltpu.make_async_copy(source, target, load_sem.at[i])
        for i, (source, target) in enumerate(small)
    ]
    wide_loads = [
        [
            pltpu.make_async_copy(
                source.at[span], target.at[span], load_sem.at[len(small) + 3 * part + i]
            )
            for i, (source, target) in enumerate(wide)
        ]
        for part, span in enumerate(spans)
    ]
    tails = [
        pltpu.make_async_copy(
            source.at[:, pl.ds(tokens - 16, 16), :], target, load_sem.at[len(small) + 3 * parts + i]
        )
        for i, (source, target) in enumerate([(q_hbm, bq_ref), (k_hbm, bk_ref), (v_hbm, bv_ref)])
    ]
    for copy in tails + small_loads + sum(wide_loads, []):
        copy.start()

    border_copy = pltpu.make_async_remote_copy(
        src_ref=edge_out_ref,
        dst_ref=edge_in_ref,
        send_sem=border_send,
        recv_sem=border_recv,
        device_id={"seq": me + 1},
        device_id_type=MESH,
    )
    columns = [(bq_ref, 0), (bk_ref, 0), (bk_ref, width), (bv_ref, 0), (bv_ref, width)]

    def pack_edges():
        low = iota((ROWS, width), 0) < 4
        for place, (tail_ref, lane) in enumerate(columns):
            for quad in range(heads // 4):
                rows = [
                    tail_ref[4 * quad + i, :, lane : lane + width].astype(F32)[8:16]
                    for i in range(4)
                ]
                tiles = [
                    jnp.where(low, pltpu.roll(rows[2 * i], 4, 0), rows[2 * i + 1])
                    for i in range(2)
                ]
                edge_out_ref[16 * quad : 16 * quad + 16, place * width : (place + 1) * width] = (
                    jnp.concatenate(tiles, axis=0).astype(BF)
                )

    def place_edge(slot, u, quad, place):
        rows = edge_in_ref[
            pl.ds(pl.multiple_of(16 * quad, 16), 16), place * width : (place + 1) * width
        ].astype(F32)
        tile = rows[8 * (u % 4 // 2) : 8 * (u % 4 // 2) + 8]
        ext_ref[slot, place, 8:16] = pltpu.roll(tile, 4, 0) if u % 2 == 0 else tile

    def exchange(source, target, head, sends, receives, device):
        return pltpu.make_async_remote_copy(
            src_ref=source,
            dst_ref=target,
            send_sem=sends.at[head],
            recv_sem=receives.at[head],
            device_id={"seq": device},
            device_id_type=MESH,
        )

    def pair_copy(head):
        place = maps_ref.at[head, side]
        return exchange(place, place, head, pair_send, pair_recv, partner)

    def pair_arrival(head):
        place = maps_ref.at[head, 1 - side]
        return exchange(place, place, head, pair_send, pair_recv, partner)

    def state_copy(head):
        return exchange(
            leaving_ref.at[head], states_ref.at[head, 0], head, state_send, state_recv, me + 2
        )

    def back_copy(head):
        place = states_ref.at[head, 1 - side]
        return exchange(place, place, head, back_send, back_recv, partner)

    def back_arrival(head):
        place = states_ref.at[head, side]
        return exchange(place, place, head, back_send, back_recv, partner)

    for copy in tails:
        copy.wait()
    pack_edges()

    @pl.when(forwards)
    def _():
        pl.semaphore_wait(barrier, 2 + side)

    @pl.when(jnp.logical_not(forwards))
    def _():
        pl.semaphore_wait(barrier, 1)

    @pl.when(has_right)
    def _():
        border_copy.start()

    @pl.when(me == 0)
    def _():
        edge_in_ref[...] = jnp.zeros_like(edge_in_ref)

    @pl.when(chip == 0)
    def _():
        states_ref[...] = jnp.zeros_like(states_ref)

    for copy in small_loads:
        copy.wait()

    starts = []
    total = jnp.int32(0)
    for m in range(docs_ref.shape[0]):
        starts.append(total)
        total = total + docs_ref[m]

    def latest_of(position):
        latest = jnp.zeros_like(position)
        for start in starts:
            latest = jnp.where(start <= position, start, latest)
        return latest

    def token_of(row):
        return (row // half) * half + token_in_half(row % half)

    def lane_token(lane):
        return (lane // tokens) * half + token_in_half(lane % half)

    square = (tokens, tokens)
    token_col = token_of(iota(square, 0))
    latest_col = latest_of(offset + token_col)
    since = offset + token_col - latest_col
    for lag in range(1, 4):
        usable_ref[lag - 1] = jnp.where(since >= lag, 1.0, 0.0)
    lane = iota((8, steps), 1)
    token_row = lane_token(lane)
    latest_row = latest_of(offset + token_row)
    half_start = offset + (lane // tokens) * half
    open_row = jnp.where(latest_row < half_start, 1.0, 0.0)
    final = [
        jnp.max(latest_row[:, h * tokens : (h + 1) * tokens], axis=1, keepdims=True)
        for h in range(2)
    ]
    same_row = jnp.where(
        latest_row == jnp.where(lane < tokens, final[0], final[1]), 1.0, 0.0
    )
    whole = [jnp.where(final[h] < offset + h * half, 1.0, 0.0) for h in range(2)]
    for h in range(2):
        here = slice(h * half, (h + 1) * half)
        lanes = slice(h * tokens, (h + 1) * tokens)
        sub_row = 2 * token_row[0:1, lanes] + (iota((1, tokens), 1) // half)
        token_here = jnp.concatenate([token_col[here], token_col[here]], axis=0)
        latest_here = jnp.concatenate([latest_col[here], latest_col[here]], axis=0)
        sub_col = 2 * token_here + iota(square, 0) // half
        linked = (latest_here == latest_row[0:1, lanes]) & (sub_col > sub_row)
        ordered_ref[h] = jnp.where(linked, -1.0, 0.0)
        reads = (latest_col[here] == latest_row[0:1, lanes]) & (
            token_col[here] >= token_row[0:1, lanes]
        )
        reads_ref[h] = jnp.where(reads, 1.0, 0.0)
    open_col = latest_col < offset + (iota(square, 0) // half) * half
    open_ref[...] = jnp.where(open_col, 1.0, 0.0)
    apart = token_in_half(iota(square, 0) % half) ^ token_in_half(iota(square, 1) % half)
    depth = jnp.zeros(square, F32)
    level = 1
    while level < half:
        depth = depth + jnp.where(apart >= level, 1.0, 0.0)
        level *= 2
    level_ref[...] = depth

    def exact(pieces, chosen, dims=NN):
        return sum(
            lax.dot_general(piece, chosen, dims, preferred_element_type=F32)
            for piece in pieces
        )

    sub_row = 2 * token_row[0:1] + (iota((1, steps), 1) % tokens) // half
    pick = jnp.where(iota((steps, steps), 0) == sub_row, 1.0, 0.0).astype(BF)
    beta = exact(thirds(strength_ref[...]), pick)
    decay = thirds(decay_ref[...])
    at = iota((tokens, steps), 0)
    lane_half = iota((tokens, steps), 1) // tokens
    middle = lane_half * half + half // 2
    opening = (at >= lane_half * half) & (at < middle)
    closing = (at >= middle) & (at < (lane_half + 1) * half)
    to_middle = jnp.exp(-exact(decay, jnp.where(opening, 1.0, 0.0).astype(BF)))
    to_end = jnp.exp(-exact(decay, jnp.where(closing, 1.0, 0.0).astype(BF)))
    open_lane_ref[...] = open_row
    whole_row = jnp.where(lane < tokens, whole[0], whole[1])
    for which, table in enumerate(
        (
            beta,
            beta * to_end * same_row[0:1],
            to_middle,
            to_middle * to_end * whole_row[0:1],
        )
    ):
        for h in range(2):
            place = (2 * which + h) * heads
            rows_ref[place : place + heads, :] = table[:, h * tokens : (h + 1) * tokens]
    middle_col = (token_col // half) * half + half // 2
    past_col = jnp.where(iota(square, 1) <= token_col, 1.0, 0.0) - jnp.where(
        iota(square, 1) < middle_col, 1.0, 0.0
    )
    past_col = past_col.astype(BF)
    from_middle_col = sum(
        lax.dot_general(past_col, piece, NT, preferred_element_type=F32)
        for piece in decay
    )
    run_cols_ref[0] = jnp.exp(-from_middle_col)
    run_cols_ref[1] = jnp.exp(from_middle_col)

    lane_head = iota((tokens, heads), 1)
    eye = jnp.where(iota((width, width), 0) == iota((width, width), 1), 1.0, 0.0)
    unit_eye = eye.astype(BF)
    both = range(GROUP)

    def convolved(u, head, lane, kernel_ref, column, h):
        taps = [kernel_ref[head, lag : lag + 1, column : column + width] for lag in range(4)]
        pieces = []
        loaded = [
            ext_ref[u, lane, pl.ds(16 + h * half + k, ROWS, stride=half // ROWS), :]
            for k in range(-3, half // ROWS)
        ]
        for i in range(half // ROWS):
            rows = slice(h * half + i * ROWS, h * half + (i + 1) * ROWS)
            summed = taps[0] * loaded[i + 3]
            for lag in range(1, 4):
                summed = summed + usable_ref[lag - 1, rows, :] * (taps[lag] * loaded[i + 3 - lag])
            pieces.append(summed)
        summed = jnp.concatenate(pieces, axis=0)
        return summed / (1.0 + jnp.exp(-summed))

    def unit(rows):
        scale = lax.rsqrt(jnp.sum(rows * rows, axis=1, keepdims=True) + 1e-6)
        return (rows * scale).astype(BF)

    def column(which, head, h):
        rows = slice(h * half, (h + 1) * half)
        return jnp.sum(
            jnp.where(lane_head[:half] == head, run_cols_ref[which, rows, :], 0.0),
            axis=1,
            keepdims=True,
        )

    def split(a):
        high = a.astype(BF)
        return high, (a - high.astype(F32)).astype(BF)

    def stage(part):
        for u in both:
            head = part * GROUP + u
            for j in range(2):
                lanes = slice(j * width, (j + 1) * width)
                ext_ref[head, 1 + j, 16 : 16 + tokens] = k_ref[head, :, lanes].astype(F32)
                ext_ref[head, 3 + j, 16 : 16 + tokens] = v_ref[head, :, lanes].astype(F32)

    def edges(part):
        for u in both:
            for place in range(1, 5):
                place_edge(part * GROUP + u, u, part * (GROUP // 4) + u // 4, place)

    def prepare(part, h):
        ids = [part * GROUP + u for u in both]

        def row(which, u):
            return rows_ref[pl.ds((2 * which + h) * heads + ids[u], 1), :]

        keys = [
            jnp.concatenate(
                [
                    unit(convolved(head, head, 1 + j, ck_ref, j * width, h))
                    for j in range(2)
                ],
                axis=0,
            )
            for head in ids
        ]
        products = [
            lax.dot_general(
                jnp.concatenate([key, unit_eye], axis=0), key, NT, preferred_element_type=F32
            )
            for key in keys
        ]
        for u in both:
            place = 2 * ids[u] + h
            keys_ref[ids[u], h] = keys[u]
            weighted_ref[place] = (products[u][tokens:] * row(1, u)).astype(BF)
            block = (products[u][:tokens] * ordered_ref[h]) * row(0, u)
            inverse_ref[place] = jnp.where(level_ref[...] == 0.0, block + eye, 0.0).astype(BF)
            system_ref[place] = block.astype(BF)
        for head in ids:
            scale = column(1, head, h)
            for j in range(2):
                rows = convolved(head, head, 3 + j, cv_ref, j * width, h).astype(BF).astype(F32)
                values_ref[head, h, j * half : (j + 1) * half] = (rows * scale).astype(BF)

    def invert(part):
        base = part * 2 * GROUP
        depth = level_ref[...]
        for level in range(int(half).bit_length() - 1):
            inner = [mm(system_ref[base + i], inverse_ref[base + i]).astype(BF) for i in range(2 * GROUP)]
            chosen = depth == level + 1.0
            for i in range(2 * GROUP):
                outer = mm(inverse_ref[base + i], inner[i])
                inverse_ref[base + i] = jnp.where(chosen, outer, inverse_ref[base + i].astype(F32)).astype(BF)

    def solve(part):
        ids = [part * PART + u for u in range(PART)]
        base = 2 * part * PART
        sides = [(u, h) for u in range(PART) for h in range(2)]

        def row(which, u, h):
            return rows_ref[pl.ds((2 * which + h) * heads + ids[u], 1), :]

        scaled = [mm(inverse_ref[base + i], values_ref[ids[u], h]) for i, (u, h) in enumerate(sides)]
        opens = [
            open_lane_ref[0:1, h * tokens : (h + 1) * tokens].astype(BF) for h in range(2)
        ]
        carried = [mm(inverse_ref[base + i] * opens[h], keys_ref[ids[u], h]) for i, (u, h) in enumerate(sides)]
        start = [row(2, u, 0) for u in range(PART)]
        first = [
            split(jnp.concatenate([scaled[2 * u], carried[2 * u] * start[u]], axis=1))
            for u in range(PART)
        ]
        moved = [mm(weighted_ref[base + 2 * u], first[u][0]) for u in range(PART)]
        through = [[row(3, u, h) for h in range(2)] for u in range(PART)]
        terms = [moved[u][:, :width] for u in range(PART)]
        transit = [through[u][0] * eye - moved[u][:, width:] for u in range(PART)]
        later = [row(2, u, 1) for u in range(PART)]
        between = [
            jnp.concatenate(
                [(later[u] * terms[u]).astype(BF), (later[u] * transit[u]).astype(BF)], axis=1
            )
            for u in range(PART)
        ]
        brought = [mm(carried[2 * u + 1], between[u]) for u in range(PART)]
        second = [
            split(
                jnp.concatenate(
                    [scaled[2 * u + 1] - brought[u][:, :width], brought[u][:, width:]], axis=1
                )
            )
            for u in range(PART)
        ]
        moved = [mm(weighted_ref[base + 2 * u + 1], second[u][0]) for u in range(PART)]
        for u in range(PART):
            term = through[u][1] * terms[u] + moved[u][:, :width]
            on = (through[u][1] * transit[u] - moved[u][:, width:]).astype(BF)
            maps_ref[ids[u], side] = jnp.concatenate([term.astype(BF), on], axis=1)
            middle_ref[ids[u]] = between[u]
            for h, solved in enumerate((first[u], second[u])):
                solved_ref[ids[u], h] = solved[0]
                rest_ref[ids[u], h] = solved[1]

    def read_local(part):
        some = range(PART)
        ids = [part * PART + u for u in some]
        for u in some:
            place_edge(ids[u], u, part, 0)
            ext_ref[ids[u], 0, 16 : 16 + tokens] = q_ref[ids[u]].astype(F32)
        query = [
            jnp.concatenate(
                [unit(convolved(head, head, 0, cq_ref, 0, h)) for h in range(2)], axis=0
            )
            for head in ids
        ]
        sides = [(u, h) for u in some for h in range(2)]

        def here(rows, h):
            return rows[h * half : (h + 1) * half]

        def row(which, u, h):
            return rows_ref[pl.ds((2 * which + h) * heads + ids[u], 1), :]

        scores = [
            lax.dot_general(
                here(query[u], h), keys_ref[ids[u], h], NT, preferred_element_type=F32
            )
            for u, h in sides
        ]
        mixing = [
            split((scores[i] * reads_ref[h]) * row(0, u, h))
            for i, (u, h) in enumerate(sides)
        ]
        gathered = [
            mm(jnp.concatenate(mixing[i], axis=0), solved_ref[ids[u], h])
            for i, (u, h) in enumerate(sides)
        ]
        gathered = [
            gathered[i][:half] + (gathered[i][half:] + mm(mixing[i][0], rest_ref[ids[u], h]))
            for i, (u, h) in enumerate(sides)
        ]
        opened = [query[u].astype(F32) * open_ref[...] for u in some]
        brought = [mm(here(opened[u], 1), middle_ref[ids[u]]) for u in some]
        for u in some:
            start = row(2, u, 0)
            early, late = gathered[2 * u], gathered[2 * u + 1]
            local_ref[ids[u]] = jnp.concatenate(
                [early[:, :width], brought[u][:, :width] + late[:, :width]], axis=0
            )
            correction_ref[ids[u]] = jnp.concatenate(
                [
                    (start * here(opened[u], 0) - early[:, width:]).astype(BF),
                    (brought[u][:, width:] - late[:, width:]).astype(BF),
                ],
                axis=0,
            )

    def finish_rows(u, head, state):
        rows = local_ref[head] + mm(correction_ref[head], state)
        rows = rows * jnp.concatenate([column(0, head, h) for h in range(2)], axis=0)
        for h in range(2):
            for i in range(half // ROWS):
                spread_ref[u, pl.ds(h * half + i, ROWS, stride=half // ROWS), :] = rows[
                    h * half + i * ROWS : h * half + (i + 1) * ROWS
                ]
        out_ref[head] = spread_ref[u].astype(BF)

    some = range(PART)
    pieces = heads // PART
    owned = PART // 2
    items = heads // 2 // TOGETHER

    def mine(index):
        return (index // owned) * PART + side * owned + index % owned

    def theirs(index):
        return (index // owned) * PART + (1 - side) * owned + index % owned

    def send_maps(part):
        for u in range(owned):
            pair_copy(theirs(part * owned + u)).start()

    def compose(part):
        ids = [mine(part * owned + u) for u in range(owned)]
        for head in ids:
            pair_arrival(head).wait_recv()
        composed = [mm(maps_ref[head, 1, :, width:], maps_ref[head, 0]) for head in ids]
        for head, both_maps in zip(ids, composed):
            terms_ref[head] = maps_ref[head, 1, :, :width].astype(F32) + both_maps[:, :width]
            transit_ref[head] = both_maps[:, width:].astype(BF)

    def chain(item):
        ids = [mine(item * TOGETHER + u) for u in range(TOGETHER)]

        @pl.when(chip > 0)
        def _():
            for head in ids:
                state_copy(head).wait_recv()

        steps_on = [
            mm(
                jnp.concatenate([transit_ref[head], maps_ref[head, 0, :, width:]], axis=0),
                states_ref[head, 0],
            )
            for head in ids
        ]
        for head, both_ends in zip(ids, steps_on):
            leaving_ref[head] = (terms_ref[head] + both_ends[:width]).astype(BF)
            inner = maps_ref[head, 0, :, :width].astype(F32) + both_ends[width:]
            states_ref[head, 1] = inner.astype(BF)

        @pl.when(forwards)
        def _():
            for head in ids:
                state_copy(head).start()

        for head in ids:
            back_copy(head).start()

    def read(part):
        ids = [part * PART + u for u in some]

        for u in range(owned):
            back_arrival(theirs(part * owned + u)).wait_recv()

        for u in some:
            finish_rows(u, ids[u], states_ref[ids[u], side])

    early = items // parts
    each = GROUP // PART

    def chain_range(first, last):
        lax.fori_loop(first, last, lambda item, none: (chain(item), none)[1], 0)

    def later_half(step, carry):
        for part in range(parts):

            @pl.when(step == part)
            def _():
                for copy in wide_loads[part]:
                    copy.wait()

        stage(step)
        prepare(step, 1)
        return carry

    lax.fori_loop(0, parts, later_half, 0)

    @pl.when(has_left)
    def _():
        border_copy.wait_recv()

    def first_phase(step, carry):
        edges(step)
        prepare(step, 0)

        @pl.when(step == 1)
        def _():
            for sub in range(each):
                compose(sub)

            @pl.when(chip == 0)
            def _():
                chain_range(0, early)

        invert(step)

        def finish_solve(sub, none):
            solve(step * each + sub)
            send_maps(step * each + sub)
            return none

        lax.fori_loop(0, each, finish_solve, 0)
        return carry

    lax.fori_loop(0, parts, first_phase, 0)

    @pl.when(chip == 1)
    def _():
        chain_range(0, early)

    middle = early // 2
    compose(each)

    @pl.when(chip == 0)
    def _():
        chain_range(early, early + middle)


    def second_phase(slot, carry):
        @pl.when(slot < pieces)
        def _():
            read_local(slot)

        @pl.when(slot == 0)
        def _():
            for sub in range(1, each):
                compose(each + sub)

        later = jnp.where(chip == 0, 0, jnp.where(chip == 1, pieces - 1, pieces + 3))
        later = jnp.where(chip == 2, pieces, later)
        soon = jnp.where(chip < 2, -1, jnp.where(chip == 2, pieces - 2, pieces))
        first = jnp.where(slot == later, jnp.where(chip == 0, early + middle, early), jnp.where(slot == soon, 0, middle))
        last = jnp.where(slot == later, items, jnp.where(slot == soon, middle, middle))
        halfway = (chip == 2) & (slot == pieces - 1)
        last = jnp.where(halfway | ((slot == soon) & (chip > 2)), early, last)
        chain_range(first, last)

        @pl.when(slot > pieces)
        def _():
            read(slot - pieces - 1)

        return carry

    lax.fori_loop(0, 2 * pieces + 1, second_phase, 0)

    @pl.when(has_right)
    def _():
        border_copy.wait_send()

    def finish(index, carry):
        pair_copy(theirs(index)).wait_send()
        back_copy(mine(index)).wait_send()

        @pl.when(forwards)
        def _():
            state_copy(mine(index)).wait_send()

        return carry

    lax.fori_loop(0, heads // 2, finish, 0)


def body(
    queries,
    key_pairs,
    value_pairs,
    strengths,
    decays,
    conv_query,
    conv_key,
    conv_value,
    doc_lengths,
):
    heads, tokens, width = queries.shape
    n_seq = lax.axis_size("seq")
    steps = 2 * tokens
    vmem = pl.BlockSpec(memory_space=pltpu.VMEM)
    return pl.pallas_call(
        functools.partial(kernel, n_seq),
        out_shape=pltpu.VMEM((heads, tokens, width), BF),
        in_specs=[pl.BlockSpec(memory_space=pltpu.HBM)] * 9,
        out_specs=vmem,
        scratch_shapes=[
            pltpu.SMEM(doc_lengths.shape, jnp.int32),
            pltpu.VMEM(queries.shape, BF),
            pltpu.VMEM(key_pairs.shape, BF),
            pltpu.VMEM(value_pairs.shape, BF),
            pltpu.VMEM(strengths.shape, F32),
            pltpu.VMEM(decays.shape, F32),
            pltpu.VMEM(conv_query.shape, F32),
            pltpu.VMEM(conv_key.shape, F32),
            pltpu.VMEM(conv_value.shape, F32),
            pltpu.VMEM((heads, 16, width), BF),
            pltpu.VMEM((heads, 16, 2 * width), BF),
            pltpu.VMEM((heads, 16, 2 * width), BF),
            pltpu.VMEM((4 * heads, 5 * width), BF),
            pltpu.VMEM((4 * heads, 5 * width), BF),
            pltpu.VMEM((heads, 5, 16 + tokens, width), F32),
            pltpu.VMEM((3, tokens, tokens), F32),
            pltpu.VMEM((2, tokens, tokens), F32),
            pltpu.VMEM((2, tokens // 2, tokens), F32),
            pltpu.VMEM((tokens, tokens), F32),
            pltpu.VMEM((tokens, tokens), F32),
            pltpu.VMEM((8 * heads, tokens), F32),
            pltpu.VMEM((8, steps), F32),
            pltpu.VMEM((2, tokens, heads), F32),
            pltpu.VMEM((2 * heads, tokens, tokens), BF),
            pltpu.VMEM((2 * heads, tokens, tokens), BF),
            pltpu.VMEM((2 * heads, tokens, tokens), BF),
            pltpu.VMEM((heads, 2, tokens, width), BF),
            pltpu.VMEM((heads, 2, tokens, width), BF),
            pltpu.VMEM((heads, 2, tokens, 2 * width), BF),
            pltpu.VMEM((heads, 2, tokens, 2 * width), BF),
            pltpu.VMEM((heads, width, 2 * width), BF),
            pltpu.VMEM((PART, tokens, width), F32),
            pltpu.VMEM((heads, width, width), F32),
            pltpu.VMEM((heads, width, width), BF),
            pltpu.VMEM((heads, tokens, width), F32),
            pltpu.VMEM((heads, tokens, width), BF),
            pltpu.VMEM((heads, width, width), BF),
            pltpu.VMEM((heads, 2, width, 2 * width), BF),
            pltpu.VMEM((heads, 2, width, width), BF),
            pltpu.SemaphoreType.DMA((9 + 3 * (heads // GROUP),)),
            pltpu.SemaphoreType.DMA,
            pltpu.SemaphoreType.DMA,
            pltpu.SemaphoreType.DMA((heads,)),
            pltpu.SemaphoreType.DMA((heads,)),
            pltpu.SemaphoreType.DMA((heads,)),
            pltpu.SemaphoreType.DMA((heads,)),
            pltpu.SemaphoreType.DMA((heads,)),
            pltpu.SemaphoreType.DMA((heads,)),
        ],
        compiler_params=pltpu.CompilerParams(
            collective_id=0, has_side_effects=True, vmem_limit_bytes=60 << 20
        ),
        name="delta_product",
    )(
        doc_lengths,
        queries,
        key_pairs,
        value_pairs,
        strengths,
        decays,
        conv_query,
        conv_key,
        conv_value,
    )


def solution(mesh):
    in_specs = (
        P(None, ("dp", "seq"), None),
        P(None, ("dp", "seq"), None),
        P(None, ("dp", "seq"), None),
        P(None, ("dp", "seq")),
        P(None, ("dp", "seq")),
        P(),
        P(),
        P(),
        P("dp"),
    )
    out_specs = P(None, ("dp", "seq"), None)
    return jax.shard_map(body, mesh=mesh, in_specs=in_specs, out_specs=out_specs, check_vma=False)
```

```python
import functools

import jax
import jax.numpy as jnp
from jax import lax
from jax.experimental import pallas as pl
from jax.experimental.pallas import tpu as pltpu
from jax.sharding import PartitionSpec as P

MESH = pl.DeviceIdType.MESH
BF = jnp.bfloat16
F32 = jnp.float32
GROUP = 8
PART = 4
TOGETHER = 1
ROWS = 8
NT = (((1,), (1,)), ((), ()))
NN = (((1,), (0,)), ((), ()))


def mm(a, b):
    return jnp.dot(a.astype(BF), b.astype(BF), preferred_element_type=F32)


def thirds(a):
    high = a.astype(BF)
    rest = a - high.astype(F32)
    middle = rest.astype(BF)
    return high, middle, (rest - middle.astype(F32)).astype(BF)


def iota(shape, axis):
    return lax.broadcasted_iota(jnp.int32, shape, axis)


def token_in_half(index):
    return index // ROWS + ROWS * (index % ROWS)


def kernel(
    n_seq,
    docs_hbm,
    q_hbm,
    k_hbm,
    v_hbm,
    strength_hbm,
    decay_hbm,
    cq_hbm,
    ck_hbm,
    cv_hbm,
    out_ref,
    docs_ref,
    q_ref,
    k_ref,
    v_ref,
    strength_ref,
    decay_ref,
    cq_ref,
    ck_ref,
    cv_ref,
    bq_ref,
    bk_ref,
    bv_ref,
    edge_out_ref,
    edge_in_ref,
    ext_ref,
    usable_ref,
    ordered_ref,
    reads_ref,
    open_ref,
    level_ref,
    rows_ref,
    open_lane_ref,
    run_cols_ref,
    weighted_ref,
    inverse_ref,
    system_ref,
    values_ref,
    keys_ref,
    solved_ref,
    rest_ref,
    middle_ref,
    spread_ref,
    terms_ref,
    transit_ref,
    local_ref,
    correction_ref,
    leaving_ref,
    maps_ref,
    states_ref,
    load_sem,
    border_send,
    border_recv,
    pair_send,
    pair_recv,
    state_send,
    state_recv,
    back_send,
    back_recv,
):
    heads, tokens, width = q_ref.shape
    half = tokens // 2
    steps = 2 * tokens
    parts = heads // GROUP
    me = lax.axis_index("seq")
    chip = me // 2
    chips = n_seq // 2
    upper = me % 2 == 1
    lower = me % 2 == 0
    offset = me * tokens
    has_left = me > 0
    has_right = me < n_seq - 1
    barrier = pltpu.get_barrier_semaphore()

    side = me % 2
    partner = me + 1 - 2 * side
    forwards = chip < chips - 1
    pl.semaphore_signal(barrier, inc=1, device_id={"seq": partner}, device_id_type=MESH)

    @pl.when(lower & has_left)
    def _():
        pl.semaphore_signal(barrier, inc=1, device_id={"seq": me - 1}, device_id_type=MESH)

    @pl.when(chip > 0)
    def _():
        pl.semaphore_signal(barrier, inc=1, device_id={"seq": me - 2}, device_id_type=MESH)

    spans = [pl.ds(part * GROUP, GROUP) for part in range(parts)]
    wide = [(q_hbm, q_ref), (k_hbm, k_ref), (v_hbm, v_ref)]
    small = [
        (docs_hbm, docs_ref),
        (decay_hbm, decay_ref),
        (strength_hbm, strength_ref),
        (cq_hbm, cq_ref),
        (ck_hbm, ck_ref),
        (cv_hbm, cv_ref),
    ]
    small_loads = [
        pltpu.make_async_copy(source, target, load_sem.at[i])
        for i, (source, target) in enumerate(small)
    ]
    wide_loads = [
        [
            pltpu.make_async_copy(
                source.at[span], target.at[span], load_sem.at[len(small) + 3 * part + i]
            )
            for i, (source, target) in enumerate(wide)
        ]
        for part, span in enumerate(spans)
    ]
    tails = [
        pltpu.make_async_copy(
            source.at[:, pl.ds(tokens - 16, 16), :], target, load_sem.at[len(small) + 3 * parts + i]
        )
        for i, (source, target) in enumerate([(q_hbm, bq_ref), (k_hbm, bk_ref), (v_hbm, bv_ref)])
    ]
    for copy in tails + small_loads + sum(wide_loads, []):
        copy.start()

    border_copy = pltpu.make_async_remote_copy(
        src_ref=edge_out_ref,
        dst_ref=edge_in_ref,
        send_sem=border_send,
        recv_sem=border_recv,
        device_id={"seq": me + 1},
        device_id_type=MESH,
    )
    columns = [(bq_ref, 0), (bk_ref, 0), (bk_ref, width), (bv_ref, 0), (bv_ref, width)]

    def pack_edges():
        low = iota((ROWS, width), 0) < 4
        for place, (tail_ref, lane) in enumerate(columns):
            for quad in range(heads // 4):
                rows = [
                    tail_ref[4 * quad + i, :, lane : lane + width].astype(F32)[8:16]
                    for i in range(4)
                ]
                tiles = [
                    jnp.where(low, pltpu.roll(rows[2 * i], 4, 0), rows[2 * i + 1])
                    for i in range(2)
                ]
                edge_out_ref[16 * quad : 16 * quad + 16, place * width : (place + 1) * width] = (
                    jnp.concatenate(tiles, axis=0).astype(BF)
                )

    def place_edge(slot, u, quad, place):
        rows = edge_in_ref[
            pl.ds(pl.multiple_of(16 * quad, 16), 16), place * width : (place + 1) * width
        ].astype(F32)
        tile = rows[8 * (u % 4 // 2) : 8 * (u % 4 // 2) + 8]
        ext_ref[slot, place, 8:16] = pltpu.roll(tile, 4, 0) if u % 2 == 0 else tile

    def exchange(source, target, head, sends, receives, device):
        return pltpu.make_async_remote_copy(
            src_ref=source,
            dst_ref=target,
            send_sem=sends.at[head],
            recv_sem=receives.at[head],
            device_id={"seq": device},
            device_id_type=MESH,
        )

    def pair_copy(head):
        place = maps_ref.at[head, side]
        return exchange(place, place, head, pair_send, pair_recv, partner)

    def pair_arrival(head):
        place = maps_ref.at[head, 1 - side]
        return exchange(place, place, head, pair_send, pair_recv, partner)

    def state_copy(head):
        return exchange(
            leaving_ref.at[head], states_ref.at[head, 0], head, state_send, state_recv, me + 2
        )

    def back_copy(head):
        place = states_ref.at[head, 1 - side]
        return exchange(place, place, head, back_send, back_recv, partner)

    def back_arrival(head):
        place = states_ref.at[head, side]
        return exchange(place, place, head, back_send, back_recv, partner)

    for copy in tails:
        copy.wait()
    pack_edges()

    @pl.when(forwards)
    def _():
        pl.semaphore_wait(barrier, 2 + side)

    @pl.when(jnp.logical_not(forwards))
    def _():
        pl.semaphore_wait(barrier, 1)

    @pl.when(has_right)
    def _():
        border_copy.start()

    @pl.when(me == 0)
    def _():
        edge_in_ref[...] = jnp.zeros_like(edge_in_ref)

    @pl.when(chip == 0)
    def _():
        states_ref[...] = jnp.zeros_like(states_ref)

    for copy in small_loads:
        copy.wait()

    starts = []
    total = jnp.int32(0)
    for m in range(docs_ref.shape[0]):
        starts.append(total)
        total = total + docs_ref[m]

    def latest_of(position):
        latest = jnp.zeros_like(position)
        for start in starts:
            latest = jnp.where(start <= position, start, latest)
        return latest

    def token_of(row):
        return (row // half) * half + token_in_half(row % half)

    def lane_token(lane):
        return (lane // tokens) * half + token_in_half(lane % half)

    square = (tokens, tokens)
    token_col = token_of(iota(square, 0))
    latest_col = latest_of(offset + token_col)
    since = offset + token_col - latest_col
    for lag in range(1, 4):
        usable_ref[lag - 1] = jnp.where(since >= lag, 1.0, 0.0)
    lane = iota((8, steps), 1)
    token_row = lane_token(lane)
    latest_row = latest_of(offset + token_row)
    half_start = offset + (lane // tokens) * half
    open_row = jnp.where(latest_row < half_start, 1.0, 0.0)
    final = [
        jnp.max(latest_row[:, h * tokens : (h + 1) * tokens], axis=1, keepdims=True)
        for h in range(2)
    ]
    same_row = jnp.where(
        latest_row == jnp.where(lane < tokens, final[0], final[1]), 1.0, 0.0
    )
    whole = [jnp.where(final[h] < offset + h * half, 1.0, 0.0) for h in range(2)]
    for h in range(2):
        here = slice(h * half, (h + 1) * half)
        lanes = slice(h * tokens, (h + 1) * tokens)
        sub_row = 2 * token_row[0:1, lanes] + (iota((1, tokens), 1) // half)
        token_here = jnp.concatenate([token_col[here], token_col[here]], axis=0)
        latest_here = jnp.concatenate([latest_col[here], latest_col[here]], axis=0)
        sub_col = 2 * token_here + iota(square, 0) // half
        linked = (latest_here == latest_row[0:1, lanes]) & (sub_col > sub_row)
        ordered_ref[h] = jnp.where(linked, -1.0, 0.0)
        reads = (latest_col[here] == latest_row[0:1, lanes]) & (
            token_col[here] >= token_row[0:1, lanes]
        )
        reads_ref[h] = jnp.where(reads, 1.0, 0.0)
    open_col = latest_col < offset + (iota(square, 0) // half) * half
    open_ref[...] = jnp.where(open_col, 1.0, 0.0)
    apart = token_in_half(iota(square, 0) % half) ^ token_in_half(iota(square, 1) % half)
    depth = jnp.zeros(square, F32)
    level = 1
    while level < half:
        depth = depth + jnp.where(apart >= level, 1.0, 0.0)
        level *= 2
    level_ref[...] = depth

    def exact(pieces, chosen, dims=NN):
        return sum(
            lax.dot_general(piece, chosen, dims, preferred_element_type=F32)
            for piece in pieces
        )

    sub_row = 2 * token_row[0:1] + (iota((1, steps), 1) % tokens) // half
    pick = jnp.where(iota((steps, steps), 0) == sub_row, 1.0, 0.0).astype(BF)
    beta = exact(thirds(strength_ref[...]), pick)
    decay = thirds(decay_ref[...])
    at = iota((tokens, steps), 0)
    lane_half = iota((tokens, steps), 1) // tokens
    middle = lane_half * half + half // 2
    opening = (at >= lane_half * half) & (at < middle)
    closing = (at >= middle) & (at < (lane_half + 1) * half)
    to_middle = jnp.exp(-exact(decay, jnp.where(opening, 1.0, 0.0).astype(BF)))
    to_end = jnp.exp(-exact(decay, jnp.where(closing, 1.0, 0.0).astype(BF)))
    open_lane_ref[...] = open_row
    whole_row = jnp.where(lane < tokens, whole[0], whole[1])
    for which, table in enumerate(
        (
            beta,
            beta * to_end * same_row[0:1],
            to_middle,
            to_middle * to_end * whole_row[0:1],
        )
    ):
        for h in range(2):
            place = (2 * which + h) * heads
            rows_ref[place : place + heads, :] = table[:, h * tokens : (h + 1) * tokens]
    middle_col = (token_col // half) * half + half // 2
    past_col = jnp.where(iota(square, 1) <= token_col, 1.0, 0.0) - jnp.where(
        iota(square, 1) < middle_col, 1.0, 0.0
    )
    past_col = past_col.astype(BF)
    from_middle_col = sum(
        lax.dot_general(past_col, piece, NT, preferred_element_type=F32)
        for piece in decay
    )
    run_cols_ref[0] = jnp.exp(-from_middle_col)
    run_cols_ref[1] = jnp.exp(from_middle_col)

    lane_head = iota((tokens, heads), 1)
    eye = jnp.where(iota((width, width), 0) == iota((width, width), 1), 1.0, 0.0)
    unit_eye = eye.astype(BF)
    both = range(GROUP)

    def convolved(u, head, lane, kernel_ref, column, h):
        taps = [kernel_ref[head, lag : lag + 1, column : column + width] for lag in range(4)]
        pieces = []
        loaded = [
            ext_ref[u, lane, pl.ds(16 + h * half + k, ROWS, stride=half // ROWS), :]
            for k in range(-3, half // ROWS)
        ]
        for i in range(half // ROWS):
            rows = slice(h * half + i * ROWS, h * half + (i + 1) * ROWS)
            summed = taps[0] * loaded[i + 3]
            for lag in range(1, 4):
                summed = summed + usable_ref[lag - 1, rows, :] * (taps[lag] * loaded[i + 3 - lag])
            pieces.append(summed)
        summed = jnp.concatenate(pieces, axis=0)
        return summed / (1.0 + jnp.exp(-summed))

    def unit(rows):
        scale = lax.rsqrt(jnp.sum(rows * rows, axis=1, keepdims=True) + 1e-6)
        return (rows * scale).astype(BF)

    def column(which, head, h):
        rows = slice(h * half, (h + 1) * half)
        return jnp.sum(
            jnp.where(lane_head[:half] == head, run_cols_ref[which, rows, :], 0.0),
            axis=1,
            keepdims=True,
        )

    def split(a):
        high = a.astype(BF)
        return high, (a - high.astype(F32)).astype(BF)

    def stage(part):
        for u in both:
            head = part * GROUP + u
            for j in range(2):
                lanes = slice(j * width, (j + 1) * width)
                ext_ref[head, 1 + j, 16 : 16 + tokens] = k_ref[head, :, lanes].astype(F32)
                ext_ref[head, 3 + j, 16 : 16 + tokens] = v_ref[head, :, lanes].astype(F32)

    def edges(part):
        for u in both:
            for place in range(1, 5):
                place_edge(part * GROUP + u, u, part * (GROUP // 4) + u // 4, place)

    def prepare(part, h):
        ids = [part * GROUP + u for u in both]

        def row(which, u):
            return rows_ref[pl.ds((2 * which + h) * heads + ids[u], 1), :]

        keys = [
            jnp.concatenate(
                [
                    unit(convolved(head, head, 1 + j, ck_ref, j * width, h))
                    for j in range(2)
                ],
                axis=0,
            )
            for head in ids
        ]
        products = [
            lax.dot_general(
                jnp.concatenate([key, unit_eye], axis=0), key, NT, preferred_element_type=F32
            )
            for key in keys
        ]
        for u in both:
            place = 2 * ids[u] + h
            keys_ref[ids[u], h] = keys[u]
            weighted_ref[place] = (products[u][tokens:] * row(1, u)).astype(BF)
            block = (products[u][:tokens] * ordered_ref[h]) * row(0, u)
            inverse_ref[place] = jnp.where(level_ref[...] == 0.0, block + eye, 0.0).astype(BF)
            system_ref[place] = block.astype(BF)
        for head in ids:
            scale = column(1, head, h)
            for j in range(2):
                rows = convolved(head, head, 3 + j, cv_ref, j * width, h).astype(BF).astype(F32)
                values_ref[head, h, j * half : (j + 1) * half] = (rows * scale).astype(BF)

    def invert(part):
        base = part * 2 * GROUP
        depth = level_ref[...]
        count = range(2 * GROUP)
        for low in range(1, int(half).bit_length(), 2):
            fresh = depth >= low * 1.0
            near = (depth == low * 1.0) | (depth == low + 1.0)
            far = depth == low + 1.0
            ahead = [
                mm(
                    inverse_ref[base + i],
                    jnp.where(fresh, system_ref[base + i].astype(F32), 0.0),
                ).astype(BF)
                for i in count
            ]
            wide = [
                mm(ahead[i], jnp.concatenate([ahead[i], inverse_ref[base + i]], axis=1))
                for i in count
            ]
            for i in count:
                once = jnp.where(near, wide[i][:, tokens:], inverse_ref[base + i].astype(F32))
                twice = mm(wide[i][:, :tokens], once)
                inverse_ref[base + i] = jnp.where(far, once + twice, once).astype(BF)

    def solve(part):
        ids = [part * PART + u for u in range(PART)]
        base = 2 * part * PART
        sides = [(u, h) for u in range(PART) for h in range(2)]

        def row(which, u, h):
            return rows_ref[pl.ds((2 * which + h) * heads + ids[u], 1), :]

        scaled = [mm(inverse_ref[base + i], values_ref[ids[u], h]) for i, (u, h) in enumerate(sides)]
        opens = [
            open_lane_ref[0:1, h * tokens : (h + 1) * tokens].astype(BF) for h in range(2)
        ]
        carried = [mm(inverse_ref[base + i] * opens[h], keys_ref[ids[u], h]) for i, (u, h) in enumerate(sides)]
        start = [row(2, u, 0) for u in range(PART)]
        first = [
            split(jnp.concatenate([scaled[2 * u], carried[2 * u] * start[u]], axis=1))
            for u in range(PART)
        ]
        moved = [mm(weighted_ref[base + 2 * u], first[u][0]) for u in range(PART)]
        through = [[row(3, u, h) for h in range(2)] for u in range(PART)]
        terms = [moved[u][:, :width] for u in range(PART)]
        transit = [through[u][0] * eye - moved[u][:, width:] for u in range(PART)]
        later = [row(2, u, 1) for u in range(PART)]
        between = [
            jnp.concatenate(
                [(later[u] * terms[u]).astype(BF), (later[u] * transit[u]).astype(BF)], axis=1
            )
            for u in range(PART)
        ]
        brought = [mm(carried[2 * u + 1], between[u]) for u in range(PART)]
        second = [
            split(
                jnp.concatenate(
                    [scaled[2 * u + 1] - brought[u][:, :width], brought[u][:, width:]], axis=1
                )
            )
            for u in range(PART)
        ]
        moved = [mm(weighted_ref[base + 2 * u + 1], second[u][0]) for u in range(PART)]
        for u in range(PART):
            term = through[u][1] * terms[u] + moved[u][:, :width]
            on = (through[u][1] * transit[u] - moved[u][:, width:]).astype(BF)
            maps_ref[ids[u], side] = jnp.concatenate([term.astype(BF), on], axis=1)
            middle_ref[ids[u]] = between[u]
            for h, solved in enumerate((first[u], second[u])):
                solved_ref[ids[u], h] = solved[0]
                rest_ref[ids[u], h] = solved[1]

    def read_local(part):
        some = range(PART)
        ids = [part * PART + u for u in some]
        for u in some:
            place_edge(ids[u], u, part, 0)
            ext_ref[ids[u], 0, 16 : 16 + tokens] = q_ref[ids[u]].astype(F32)
        query = [
            jnp.concatenate(
                [unit(convolved(head, head, 0, cq_ref, 0, h)) for h in range(2)], axis=0
            )
            for head in ids
        ]
        sides = [(u, h) for u in some for h in range(2)]

        def here(rows, h):
            return rows[h * half : (h + 1) * half]

        def row(which, u, h):
            return rows_ref[pl.ds((2 * which + h) * heads + ids[u], 1), :]

        scores = [
            lax.dot_general(
                here(query[u], h), keys_ref[ids[u], h], NT, preferred_element_type=F32
            )
            for u, h in sides
        ]
        mixing = [
            split((scores[i] * reads_ref[h]) * row(0, u, h))
            for i, (u, h) in enumerate(sides)
        ]
        gathered = [
            mm(jnp.concatenate(mixing[i], axis=0), solved_ref[ids[u], h])
            for i, (u, h) in enumerate(sides)
        ]
        gathered = [
            gathered[i][:half] + (gathered[i][half:] + mm(mixing[i][0], rest_ref[ids[u], h]))
            for i, (u, h) in enumerate(sides)
        ]
        opened = [query[u].astype(F32) * open_ref[...] for u in some]
        brought = [mm(here(opened[u], 1), middle_ref[ids[u]]) for u in some]
        for u in some:
            start = row(2, u, 0)
            early, late = gathered[2 * u], gathered[2 * u + 1]
            local_ref[ids[u]] = jnp.concatenate(
                [early[:, :width], brought[u][:, :width] + late[:, :width]], axis=0
            )
            correction_ref[ids[u]] = jnp.concatenate(
                [
                    (start * here(opened[u], 0) - early[:, width:]).astype(BF),
                    (brought[u][:, width:] - late[:, width:]).astype(BF),
                ],
                axis=0,
            )

    def finish_rows(u, head, state):
        rows = local_ref[head] + mm(correction_ref[head], state)
        rows = rows * jnp.concatenate([column(0, head, h) for h in range(2)], axis=0)
        for h in range(2):
            for i in range(half // ROWS):
                spread_ref[u, pl.ds(h * half + i, ROWS, stride=half // ROWS), :] = rows[
                    h * half + i * ROWS : h * half + (i + 1) * ROWS
                ]
        out_ref[head] = spread_ref[u].astype(BF)

    some = range(PART)
    pieces = heads // PART
    owned = PART // 2
    items = heads // 2 // TOGETHER

    def mine(index):
        return (index // owned) * PART + side * owned + index % owned

    def theirs(index):
        return (index // owned) * PART + (1 - side) * owned + index % owned

    def send_maps(part):
        for u in range(owned):
            pair_copy(theirs(part * owned + u)).start()

    def compose(part):
        ids = [mine(part * owned + u) for u in range(owned)]
        for head in ids:
            pair_arrival(head).wait_recv()
        composed = [mm(maps_ref[head, 1, :, width:], maps_ref[head, 0]) for head in ids]
        for head, both_maps in zip(ids, composed):
            terms_ref[head] = maps_ref[head, 1, :, :width].astype(F32) + both_maps[:, :width]
            transit_ref[head] = both_maps[:, width:].astype(BF)

    def chain(item):
        ids = [mine(item * TOGETHER + u) for u in range(TOGETHER)]

        @pl.when(chip > 0)
        def _():
            for head in ids:
                state_copy(head).wait_recv()

        steps_on = [
            mm(
                jnp.concatenate([transit_ref[head], maps_ref[head, 0, :, width:]], axis=0),
                states_ref[head, 0],
            )
            for head in ids
        ]
        for head, both_ends in zip(ids, steps_on):
            leaving_ref[head] = (terms_ref[head] + both_ends[:width]).astype(BF)
            inner = maps_ref[head, 0, :, :width].astype(F32) + both_ends[width:]
            states_ref[head, 1] = inner.astype(BF)

        @pl.when(forwards)
        def _():
            for head in ids:
                state_copy(head).start()

        for head in ids:
            back_copy(head).start()

    def read(part):
        ids = [part * PART + u for u in some]

        for u in range(owned):
            back_arrival(theirs(part * owned + u)).wait_recv()

        for u in some:
            finish_rows(u, ids[u], states_ref[ids[u], side])

    early = items // parts
    each = GROUP // PART

    def chain_range(first, last):
        lax.fori_loop(first, last, lambda item, none: (chain(item), none)[1], 0)

    def later_half(step, carry):
        for part in range(parts):

            @pl.when(step == part)
            def _():
                for copy in wide_loads[part]:
                    copy.wait()

        stage(step)
        prepare(step, 1)
        return carry

    lax.fori_loop(0, parts, later_half, 0)

    @pl.when(has_left)
    def _():
        border_copy.wait_recv()

    def first_phase(step, carry):
        edges(step)
        prepare(step, 0)

        @pl.when(step == 1)
        def _():
            for sub in range(each):
                compose(sub)

            @pl.when(chip == 0)
            def _():
                chain_range(0, early)

        invert(step)

        def finish_solve(sub, none):
            solve(step * each + sub)
            send_maps(step * each + sub)
            return none

        lax.fori_loop(0, each, finish_solve, 0)
        return carry

    lax.fori_loop(0, parts, first_phase, 0)

    @pl.when(chip == 1)
    def _():
        chain_range(0, early)

    middle = early // 2
    compose(each)

    @pl.when(chip == 0)
    def _():
        chain_range(early, early + middle)


    def second_phase(slot, carry):
        @pl.when(slot < pieces)
        def _():
            read_local(slot)

        @pl.when(slot == 0)
        def _():
            for sub in range(1, each):
                compose(each + sub)

        @pl.when(slot == pieces)
        def _():
            def sent(index, none):
                pair_copy(theirs(index)).wait_send()
                return none

            lax.fori_loop(0, heads // 2, sent, 0)

        def pick(places):
            first, last = 0, 0
            for at, start, end in places:
                first = jnp.where(slot == at, start, first)
                last = jnp.where(slot == at, end, last)
            return first, last

        late = early + middle
        plans = [
            pick([(0, late, items)]),
            pick([(2, early, late), (3, late, items)]),
            pick([(2, 0, middle), (3, middle, early), (4, early, items)]),
            pick([(4, 0, late), (6, late, items)]),
        ]
        first, last = plans[3]
        for which in range(3):
            first = jnp.where(chip == which, plans[which][0], first)
            last = jnp.where(chip == which, plans[which][1], last)
        chain_range(first, last)

        @pl.when(slot > pieces)
        def _():
            read(slot - pieces - 1)

        return carry

    lax.fori_loop(0, 2 * pieces + 1, second_phase, 0)

    @pl.when(has_right)
    def _():
        border_copy.wait_send()

    def finish(index, carry):
        back_copy(mine(index)).wait_send()

        @pl.when(forwards)
        def _():
            state_copy(mine(index)).wait_send()

        return carry

    lax.fori_loop(0, heads // 2, finish, 0)


def body(
    queries,
    key_pairs,
    value_pairs,
    strengths,
    decays,
    conv_query,
    conv_key,
    conv_value,
    doc_lengths,
):
    heads, tokens, width = queries.shape
    n_seq = lax.axis_size("seq")
    steps = 2 * tokens
    vmem = pl.BlockSpec(memory_space=pltpu.VMEM)
    return pl.pallas_call(
        functools.partial(kernel, n_seq),
        out_shape=pltpu.VMEM((heads, tokens, width), BF),
        in_specs=[pl.BlockSpec(memory_space=pltpu.HBM)] * 9,
        out_specs=vmem,
        scratch_shapes=[
            pltpu.SMEM(doc_lengths.shape, jnp.int32),
            pltpu.VMEM(queries.shape, BF),
            pltpu.VMEM(key_pairs.shape, BF),
            pltpu.VMEM(value_pairs.shape, BF),
            pltpu.VMEM(strengths.shape, F32),
            pltpu.VMEM(decays.shape, F32),
            pltpu.VMEM(conv_query.shape, F32),
            pltpu.VMEM(conv_key.shape, F32),
            pltpu.VMEM(conv_value.shape, F32),
            pltpu.VMEM((heads, 16, width), BF),
            pltpu.VMEM((heads, 16, 2 * width), BF),
            pltpu.VMEM((heads, 16, 2 * width), BF),
            pltpu.VMEM((4 * heads, 5 * width), BF),
            pltpu.VMEM((4 * heads, 5 * width), BF),
            pltpu.VMEM((heads, 5, 16 + tokens, width), F32),
            pltpu.VMEM((3, tokens, tokens), F32),
            pltpu.VMEM((2, tokens, tokens), F32),
            pltpu.VMEM((2, tokens // 2, tokens), F32),
            pltpu.VMEM((tokens, tokens), F32),
            pltpu.VMEM((tokens, tokens), F32),
            pltpu.VMEM((8 * heads, tokens), F32),
            pltpu.VMEM((8, steps), F32),
            pltpu.VMEM((2, tokens, heads), F32),
            pltpu.VMEM((2 * heads, tokens, tokens), BF),
            pltpu.VMEM((2 * heads, tokens, tokens), BF),
            pltpu.VMEM((2 * heads, tokens, tokens), BF),
            pltpu.VMEM((heads, 2, tokens, width), BF),
            pltpu.VMEM((heads, 2, tokens, width), BF),
            pltpu.VMEM((heads, 2, tokens, 2 * width), BF),
            pltpu.VMEM((heads, 2, tokens, 2 * width), BF),
            pltpu.VMEM((heads, width, 2 * width), BF),
            pltpu.VMEM((PART, tokens, width), F32),
            pltpu.VMEM((heads, width, width), F32),
            pltpu.VMEM((heads, width, width), BF),
            pltpu.VMEM((heads, tokens, width), F32),
            pltpu.VMEM((heads, tokens, width), BF),
            pltpu.VMEM((heads, width, width), BF),
            pltpu.VMEM((heads, 2, width, 2 * width), BF),
            pltpu.VMEM((heads, 2, width, width), BF),
            pltpu.SemaphoreType.DMA((9 + 3 * (heads // GROUP),)),
            pltpu.SemaphoreType.DMA,
            pltpu.SemaphoreType.DMA,
            pltpu.SemaphoreType.DMA((heads,)),
            pltpu.SemaphoreType.DMA((heads,)),
            pltpu.SemaphoreType.DMA((heads,)),
            pltpu.SemaphoreType.DMA((heads,)),
            pltpu.SemaphoreType.DMA((heads,)),
            pltpu.SemaphoreType.DMA((heads,)),
        ],
        compiler_params=pltpu.CompilerParams(
            collective_id=0, has_side_effects=True, vmem_limit_bytes=60 << 20
        ),
        name="delta_product",
    )(
        doc_lengths,
        queries,
        key_pairs,
        value_pairs,
        strengths,
        decays,
        conv_query,
        conv_key,
        conv_value,
    )


def solution(mesh):
    in_specs = (
        P(None, ("dp", "seq"), None),
        P(None, ("dp", "seq"), None),
        P(None, ("dp", "seq"), None),
        P(None, ("dp", "seq")),
        P(None, ("dp", "seq")),
        P(),
        P(),
        P(),
        P("dp"),
    )
    out_specs = P(None, ("dp", "seq"), None)
    return jax.shard_map(body, mesh=mesh, in_specs=in_specs, out_specs=out_specs, check_vma=False)
```

```python
import functools

import jax
import jax.numpy as jnp
from jax import lax
from jax.experimental import pallas as pl
from jax.experimental.pallas import tpu as pltpu
from jax.sharding import PartitionSpec as P

MESH = pl.DeviceIdType.MESH
BF = jnp.bfloat16
F32 = jnp.float32
GROUP = 8
PART = 4
TOGETHER = 1
ROWS = 8
NT = (((1,), (1,)), ((), ()))
NN = (((1,), (0,)), ((), ()))


def mm(a, b):
    return jnp.dot(a.astype(BF), b.astype(BF), preferred_element_type=F32)


def thirds(a):
    high = a.astype(BF)
    rest = a - high.astype(F32)
    middle = rest.astype(BF)
    return high, middle, (rest - middle.astype(F32)).astype(BF)


def iota(shape, axis):
    return lax.broadcasted_iota(jnp.int32, shape, axis)


def token_in_half(index):
    return index // ROWS + ROWS * (index % ROWS)


def kernel(
    n_seq,
    docs_hbm,
    q_hbm,
    k_hbm,
    v_hbm,
    strength_hbm,
    decay_hbm,
    cq_hbm,
    ck_hbm,
    cv_hbm,
    out_ref,
    docs_ref,
    q_ref,
    k_ref,
    v_ref,
    strength_ref,
    decay_ref,
    cq_ref,
    ck_ref,
    cv_ref,
    bq_ref,
    bk_ref,
    bv_ref,
    edge_out_ref,
    edge_in_ref,
    ext_ref,
    usable_ref,
    ordered_ref,
    reads_ref,
    open_ref,
    level_ref,
    rows_ref,
    open_lane_ref,
    run_cols_ref,
    weighted_ref,
    inverse_ref,
    system_ref,
    values_ref,
    keys_ref,
    solved_ref,
    rest_ref,
    middle_ref,
    spread_ref,
    terms_ref,
    transit_ref,
    local_ref,
    correction_ref,
    leaving_ref,
    maps_ref,
    states_ref,
    load_sem,
    border_send,
    border_recv,
    pair_send,
    pair_recv,
    state_send,
    state_recv,
    back_send,
    back_recv,
):
    heads, tokens, width = q_ref.shape
    half = tokens // 2
    steps = 2 * tokens
    parts = heads // GROUP
    me = lax.axis_index("seq")
    chip = me // 2
    chips = n_seq // 2
    upper = me % 2 == 1
    lower = me % 2 == 0
    offset = me * tokens
    has_left = me > 0
    has_right = me < n_seq - 1
    barrier = pltpu.get_barrier_semaphore()

    side = me % 2
    partner = me + 1 - 2 * side
    forwards = chip < chips - 1
    pl.semaphore_signal(barrier, inc=1, device_id={"seq": partner}, device_id_type=MESH)

    @pl.when(lower & has_left)
    def _():
        pl.semaphore_signal(barrier, inc=1, device_id={"seq": me - 1}, device_id_type=MESH)

    @pl.when(chip > 0)
    def _():
        pl.semaphore_signal(barrier, inc=1, device_id={"seq": me - 2}, device_id_type=MESH)

    spans = [pl.ds(part * GROUP, GROUP) for part in range(parts)]
    wide = [(q_hbm, q_ref), (k_hbm, k_ref), (v_hbm, v_ref)]
    small = [
        (docs_hbm, docs_ref),
        (decay_hbm, decay_ref),
        (strength_hbm, strength_ref),
        (cq_hbm, cq_ref),
        (ck_hbm, ck_ref),
        (cv_hbm, cv_ref),
    ]
    small_loads = [
        pltpu.make_async_copy(source, target, load_sem.at[i])
        for i, (source, target) in enumerate(small)
    ]
    wide_loads = [
        [
            pltpu.make_async_copy(
                source.at[span], target.at[span], load_sem.at[len(small) + 3 * part + i]
            )
            for i, (source, target) in enumerate(wide)
        ]
        for part, span in enumerate(spans)
    ]
    tails = [
        pltpu.make_async_copy(
            source.at[:, pl.ds(tokens - 16, 16), :], target, load_sem.at[len(small) + 3 * parts + i]
        )
        for i, (source, target) in enumerate([(q_hbm, bq_ref), (k_hbm, bk_ref), (v_hbm, bv_ref)])
    ]
    for copy in tails + small_loads + sum(wide_loads, []):
        copy.start()

    border_copy = pltpu.make_async_remote_copy(
        src_ref=edge_out_ref,
        dst_ref=edge_in_ref,
        send_sem=border_send,
        recv_sem=border_recv,
        device_id={"seq": me + 1},
        device_id_type=MESH,
    )
    columns = [(bq_ref, 0), (bk_ref, 0), (bk_ref, width), (bv_ref, 0), (bv_ref, width)]

    def pack_edges():
        low = iota((ROWS, width), 0) < 4
        for place, (tail_ref, lane) in enumerate(columns):
            for quad in range(heads // 4):
                rows = [
                    tail_ref[4 * quad + i, :, lane : lane + width].astype(F32)[8:16]
                    for i in range(4)
                ]
                tiles = [
                    jnp.where(low, pltpu.roll(rows[2 * i], 4, 0), rows[2 * i + 1])
                    for i in range(2)
                ]
                edge_out_ref[16 * quad : 16 * quad + 16, place * width : (place + 1) * width] = (
                    jnp.concatenate(tiles, axis=0).astype(BF)
                )

    def place_edge(slot, u, quad, place):
        rows = edge_in_ref[
            pl.ds(pl.multiple_of(16 * quad, 16), 16), place * width : (place + 1) * width
        ].astype(F32)
        tile = rows[8 * (u % 4 // 2) : 8 * (u % 4 // 2) + 8]
        ext_ref[slot, place, 8:16] = pltpu.roll(tile, 4, 0) if u % 2 == 0 else tile

    def exchange(source, target, head, sends, receives, device):
        return pltpu.make_async_remote_copy(
            src_ref=source,
            dst_ref=target,
            send_sem=sends.at[head],
            recv_sem=receives.at[head],
            device_id={"seq": device},
            device_id_type=MESH,
        )

    def pair_copy(head):
        place = maps_ref.at[head, side]
        return exchange(place, place, head, pair_send, pair_recv, partner)

    def pair_arrival(head):
        place = maps_ref.at[head, 1 - side]
        return exchange(place, place, head, pair_send, pair_recv, partner)

    def state_copy(head):
        return exchange(
            leaving_ref.at[head], states_ref.at[head, 0], head, state_send, state_recv, me + 2
        )

    def back_copy(head):
        place = states_ref.at[head, 1 - side]
        return exchange(place, place, head, back_send, back_recv, partner)

    def back_arrival(head):
        place = states_ref.at[head, side]
        return exchange(place, place, head, back_send, back_recv, partner)

    for copy in tails:
        copy.wait()
    pack_edges()

    @pl.when(forwards)
    def _():
        pl.semaphore_wait(barrier, 2 + side)

    @pl.when(jnp.logical_not(forwards))
    def _():
        pl.semaphore_wait(barrier, 1)

    @pl.when(has_right)
    def _():
        border_copy.start()

    @pl.when(me == 0)
    def _():
        edge_in_ref[...] = jnp.zeros_like(edge_in_ref)

    @pl.when(chip == 0)
    def _():
        states_ref[...] = jnp.zeros_like(states_ref)

    for copy in small_loads:
        copy.wait()

    starts = []
    total = jnp.int32(0)
    for m in range(docs_ref.shape[0]):
        starts.append(total)
        total = total + docs_ref[m]

    def latest_of(position):
        latest = jnp.zeros_like(position)
        for start in starts:
            latest = jnp.where(start <= position, start, latest)
        return latest

    def token_of(row):
        return (row // half) * half + token_in_half(row % half)

    def lane_token(lane):
        return (lane // tokens) * half + token_in_half(lane % half)

    square = (tokens, tokens)
    token_col = token_of(iota(square, 0))
    latest_col = latest_of(offset + token_col)
    since = offset + token_col - latest_col
    for lag in range(1, 4):
        usable_ref[lag - 1] = jnp.where(since >= lag, 1.0, 0.0)
    lane = iota((8, steps), 1)
    token_row = lane_token(lane)
    latest_row = latest_of(offset + token_row)
    half_start = offset + (lane // tokens) * half
    open_row = jnp.where(latest_row < half_start, 1.0, 0.0)
    final = [
        jnp.max(latest_row[:, h * tokens : (h + 1) * tokens], axis=1, keepdims=True)
        for h in range(2)
    ]
    same_row = jnp.where(
        latest_row == jnp.where(lane < tokens, final[0], final[1]), 1.0, 0.0
    )
    whole = [jnp.where(final[h] < offset + h * half, 1.0, 0.0) for h in range(2)]
    for h in range(2):
        here = slice(h * half, (h + 1) * half)
        lanes = slice(h * tokens, (h + 1) * tokens)
        sub_row = 2 * token_row[0:1, lanes] + (iota((1, tokens), 1) // half)
        token_here = jnp.concatenate([token_col[here], token_col[here]], axis=0)
        latest_here = jnp.concatenate([latest_col[here], latest_col[here]], axis=0)
        sub_col = 2 * token_here + iota(square, 0) // half
        linked = (latest_here == latest_row[0:1, lanes]) & (sub_col > sub_row)
        ordered_ref[h] = jnp.where(linked, -1.0, 0.0)
        reads = (latest_col[here] == latest_row[0:1, lanes]) & (
            token_col[here] >= token_row[0:1, lanes]
        )
        reads_ref[h] = jnp.where(reads, 1.0, 0.0)
    open_col = latest_col < offset + (iota(square, 0) // half) * half
    open_ref[...] = jnp.where(open_col, 1.0, 0.0)
    apart = token_in_half(iota(square, 0) % half) ^ token_in_half(iota(square, 1) % half)
    depth = jnp.zeros(square, F32)
    level = 1
    while level < half:
        depth = depth + jnp.where(apart >= level, 1.0, 0.0)
        level *= 2
    level_ref[...] = depth

    def exact(pieces, chosen, dims=NN):
        return sum(
            lax.dot_general(piece, chosen, dims, preferred_element_type=F32)
            for piece in pieces
        )

    sub_row = 2 * token_row[0:1] + (iota((1, steps), 1) % tokens) // half
    pick = jnp.where(iota((steps, steps), 0) == sub_row, 1.0, 0.0).astype(BF)
    beta = exact(thirds(strength_ref[...]), pick)
    decay = thirds(decay_ref[...])
    at = iota((tokens, steps), 0)
    lane_half = iota((tokens, steps), 1) // tokens
    middle = lane_half * half + half // 2
    opening = (at >= lane_half * half) & (at < middle)
    closing = (at >= middle) & (at < (lane_half + 1) * half)
    to_middle = jnp.exp(-exact(decay, jnp.where(opening, 1.0, 0.0).astype(BF)))
    to_end = jnp.exp(-exact(decay, jnp.where(closing, 1.0, 0.0).astype(BF)))
    open_lane_ref[...] = open_row
    whole_row = jnp.where(lane < tokens, whole[0], whole[1])
    for which, table in enumerate(
        (
            beta,
            beta * to_end * same_row[0:1],
            to_middle,
            to_middle * to_end * whole_row[0:1],
        )
    ):
        for h in range(2):
            place = (2 * which + h) * heads
            rows_ref[place : place + heads, :] = table[:, h * tokens : (h + 1) * tokens]
    middle_col = (token_col // half) * half + half // 2
    past_col = jnp.where(iota(square, 1) <= token_col, 1.0, 0.0) - jnp.where(
        iota(square, 1) < middle_col, 1.0, 0.0
    )
    past_col = past_col.astype(BF)
    from_middle_col = sum(
        lax.dot_general(past_col, piece, NT, preferred_element_type=F32)
        for piece in decay
    )
    run_cols_ref[0] = jnp.exp(-from_middle_col)
    run_cols_ref[1] = jnp.exp(from_middle_col)

    lane_head = iota((tokens, heads), 1)
    eye = jnp.where(iota((width, width), 0) == iota((width, width), 1), 1.0, 0.0)
    unit_eye = eye.astype(BF)
    both = range(GROUP)

    def convolved(u, head, lane, kernel_ref, column, h):
        taps = [kernel_ref[head, lag : lag + 1, column : column + width] for lag in range(4)]
        pieces = []
        loaded = [
            ext_ref[u, lane, pl.ds(16 + h * half + k, ROWS, stride=half // ROWS), :]
            for k in range(-3, half // ROWS)
        ]
        for i in range(half // ROWS):
            rows = slice(h * half + i * ROWS, h * half + (i + 1) * ROWS)
            summed = taps[0] * loaded[i + 3]
            for lag in range(1, 4):
                summed = summed + usable_ref[lag - 1, rows, :] * (taps[lag] * loaded[i + 3 - lag])
            pieces.append(summed)
        summed = jnp.concatenate(pieces, axis=0)
        return summed / (1.0 + jnp.exp(-summed))

    def unit(rows):
        scale = lax.rsqrt(jnp.sum(rows * rows, axis=1, keepdims=True) + 1e-6)
        return (rows * scale).astype(BF)

    def column(which, head, h):
        rows = slice(h * half, (h + 1) * half)
        return jnp.sum(
            jnp.where(lane_head[:half] == head, run_cols_ref[which, rows, :], 0.0),
            axis=1,
            keepdims=True,
        )

    def split(a):
        high = a.astype(BF)
        return high, (a - high.astype(F32)).astype(BF)

    def stage(part):
        for u in both:
            head = part * GROUP + u
            for j in range(2):
                lanes = slice(j * width, (j + 1) * width)
                ext_ref[head, 1 + j, 16 : 16 + tokens] = k_ref[head, :, lanes].astype(F32)
                ext_ref[head, 3 + j, 16 : 16 + tokens] = v_ref[head, :, lanes].astype(F32)

    def edges(part):
        for u in both:
            for place in range(1, 5):
                place_edge(part * GROUP + u, u, part * (GROUP // 4) + u // 4, place)

    def prepare(part, h):
        ids = [part * GROUP + u for u in both]

        def row(which, u):
            return rows_ref[pl.ds((2 * which + h) * heads + ids[u], 1), :]

        keys = [
            jnp.concatenate(
                [
                    unit(convolved(head, head, 1 + j, ck_ref, j * width, h))
                    for j in range(2)
                ],
                axis=0,
            )
            for head in ids
        ]
        products = [
            lax.dot_general(
                jnp.concatenate([key, unit_eye], axis=0), key, NT, preferred_element_type=F32
            )
            for key in keys
        ]
        for u in both:
            place = 2 * ids[u] + h
            keys_ref[ids[u], h] = keys[u]
            weighted_ref[place] = (products[u][tokens:] * row(1, u)).astype(BF)
            block = (products[u][:tokens] * ordered_ref[h]) * row(0, u)
            inverse_ref[place] = jnp.where(level_ref[...] == 0.0, block + eye, 0.0).astype(BF)
            system_ref[place] = block.astype(BF)
        for head in ids:
            scale = column(1, head, h)
            for j in range(2):
                rows = convolved(head, head, 3 + j, cv_ref, j * width, h).astype(BF).astype(F32)
                values_ref[head, h, j * half : (j + 1) * half] = (rows * scale).astype(BF)

    def invert(part):
        base = part * 2 * GROUP
        depth = level_ref[...]
        count = range(2 * GROUP)
        for low in range(1, int(half).bit_length(), 2):
            fresh = depth >= low * 1.0
            near = (depth == low * 1.0) | (depth == low + 1.0)
            far = depth == low + 1.0
            ahead = [
                mm(
                    inverse_ref[base + i],
                    jnp.where(fresh, system_ref[base + i].astype(F32), 0.0),
                ).astype(BF)
                for i in count
            ]
            wide = [
                mm(ahead[i], jnp.concatenate([ahead[i], inverse_ref[base + i]], axis=1))
                for i in count
            ]
            for i in count:
                once = jnp.where(near, wide[i][:, tokens:], inverse_ref[base + i].astype(F32))
                twice = mm(wide[i][:, :tokens], once)
                inverse_ref[base + i] = jnp.where(far, once + twice, once).astype(BF)

    def solve(part):
        ids = [part * PART + u for u in range(PART)]
        base = 2 * part * PART
        sides = [(u, h) for u in range(PART) for h in range(2)]

        def row(which, u, h):
            return rows_ref[pl.ds((2 * which + h) * heads + ids[u], 1), :]

        scaled = [mm(inverse_ref[base + i], values_ref[ids[u], h]) for i, (u, h) in enumerate(sides)]
        opens = [
            open_lane_ref[0:1, h * tokens : (h + 1) * tokens].astype(BF) for h in range(2)
        ]
        carried = [mm(inverse_ref[base + i] * opens[h], keys_ref[ids[u], h]) for i, (u, h) in enumerate(sides)]
        start = [row(2, u, 0) for u in range(PART)]
        first = [
            split(jnp.concatenate([scaled[2 * u], carried[2 * u] * start[u]], axis=1))
            for u in range(PART)
        ]
        moved = [mm(weighted_ref[base + 2 * u], first[u][0]) for u in range(PART)]
        through = [[row(3, u, h) for h in range(2)] for u in range(PART)]
        terms = [moved[u][:, :width] for u in range(PART)]
        transit = [through[u][0] * eye - moved[u][:, width:] for u in range(PART)]
        later = [row(2, u, 1) for u in range(PART)]
        between = [
            jnp.concatenate(
                [(later[u] * terms[u]).astype(BF), (later[u] * transit[u]).astype(BF)], axis=1
            )
            for u in range(PART)
        ]
        brought = [mm(carried[2 * u + 1], between[u]) for u in range(PART)]
        second = [
            split(
                jnp.concatenate(
                    [scaled[2 * u + 1] - brought[u][:, :width], brought[u][:, width:]], axis=1
                )
            )
            for u in range(PART)
        ]
        moved = [mm(weighted_ref[base + 2 * u + 1], second[u][0]) for u in range(PART)]
        for u in range(PART):
            term = through[u][1] * terms[u] + moved[u][:, :width]
            on = (through[u][1] * transit[u] - moved[u][:, width:]).astype(BF)
            maps_ref[ids[u], side] = jnp.concatenate([term.astype(BF), on], axis=1)
            middle_ref[ids[u]] = between[u]
            for h, solved in enumerate((first[u], second[u])):
                solved_ref[ids[u], h] = solved[0]
                rest_ref[ids[u], h] = solved[1]

    def read_local(part):
        some = range(PART)
        ids = [part * PART + u for u in some]
        for u in some:
            place_edge(ids[u], u, part, 0)
            ext_ref[ids[u], 0, 16 : 16 + tokens] = q_ref[ids[u]].astype(F32)
        query = [
            jnp.concatenate(
                [unit(convolved(head, head, 0, cq_ref, 0, h)) for h in range(2)], axis=0
            )
            for head in ids
        ]
        sides = [(u, h) for u in some for h in range(2)]

        def here(rows, h):
            return rows[h * half : (h + 1) * half]

        def row(which, u, h):
            return rows_ref[pl.ds((2 * which + h) * heads + ids[u], 1), :]

        scores = [
            lax.dot_general(
                here(query[u], h), keys_ref[ids[u], h], NT, preferred_element_type=F32
            )
            for u, h in sides
        ]
        mixing = [
            split((scores[i] * reads_ref[h]) * row(0, u, h))
            for i, (u, h) in enumerate(sides)
        ]
        gathered = [
            mm(jnp.concatenate(mixing[i], axis=0), solved_ref[ids[u], h])
            for i, (u, h) in enumerate(sides)
        ]
        gathered = [
            gathered[i][:half] + (gathered[i][half:] + mm(mixing[i][0], rest_ref[ids[u], h]))
            for i, (u, h) in enumerate(sides)
        ]
        opened = [query[u].astype(F32) * open_ref[...] for u in some]
        brought = [mm(here(opened[u], 1), middle_ref[ids[u]]) for u in some]
        for u in some:
            start = row(2, u, 0)
            early, late = gathered[2 * u], gathered[2 * u + 1]
            local_ref[ids[u]] = jnp.concatenate(
                [early[:, :width], brought[u][:, :width] + late[:, :width]], axis=0
            )
            correction_ref[ids[u]] = jnp.concatenate(
                [
                    (start * here(opened[u], 0) - early[:, width:]).astype(BF),
                    (brought[u][:, width:] - late[:, width:]).astype(BF),
                ],
                axis=0,
            )

    def finish_rows(u, head, state):
        rows = local_ref[head] + mm(correction_ref[head], state)
        rows = rows * jnp.concatenate([column(0, head, h) for h in range(2)], axis=0)
        for h in range(2):
            for i in range(half // ROWS):
                spread_ref[u, pl.ds(h * half + i, ROWS, stride=half // ROWS), :] = rows[
                    h * half + i * ROWS : h * half + (i + 1) * ROWS
                ]
        out_ref[head] = spread_ref[u].astype(BF)

    some = range(PART)
    pieces = heads // PART
    owned = PART // 2
    items = heads // 2 // TOGETHER

    def mine(index):
        return (index // owned) * PART + side * owned + index % owned

    def theirs(index):
        return (index // owned) * PART + (1 - side) * owned + index % owned

    def send_maps(part):
        for u in range(owned):
            pair_copy(theirs(part * owned + u)).start()

    def compose(part):
        ids = [mine(part * owned + u) for u in range(owned)]
        for head in ids:
            pair_arrival(head).wait_recv()
        composed = [mm(maps_ref[head, 1, :, width:], maps_ref[head, 0]) for head in ids]
        for head, both_maps in zip(ids, composed):
            terms_ref[head] = maps_ref[head, 1, :, :width].astype(F32) + both_maps[:, :width]
            transit_ref[head] = both_maps[:, width:].astype(BF)

    def chain(item):
        ids = [mine(item * TOGETHER + u) for u in range(TOGETHER)]

        @pl.when(chip > 0)
        def _():
            for head in ids:
                state_copy(head).wait_recv()

        steps_on = [
            mm(
                jnp.concatenate([transit_ref[head], maps_ref[head, 0, :, width:]], axis=0),
                states_ref[head, 0],
            )
            for head in ids
        ]
        for head, both_ends in zip(ids, steps_on):
            leaving_ref[head] = (terms_ref[head] + both_ends[:width]).astype(BF)
            inner = maps_ref[head, 0, :, :width].astype(F32) + both_ends[width:]
            states_ref[head, 1] = inner.astype(BF)

        @pl.when(forwards)
        def _():
            for head in ids:
                state_copy(head).start()

        for head in ids:
            back_copy(head).start()

    def read(part):
        ids = [part * PART + u for u in some]

        for u in range(owned):
            back_arrival(theirs(part * owned + u)).wait_recv()

        for u in some:
            finish_rows(u, ids[u], states_ref[ids[u], side])

    early = items // parts
    each = GROUP // PART

    def chain_range(first, last):
        lax.fori_loop(first, last, lambda item, none: (chain(item), none)[1], 0)

    def later_half(part):
        for copy in wide_loads[part]:
            copy.wait()

        stage(part)
        prepare(part, 1)

    later_half(0)

    @pl.when(has_left)
    def _():
        border_copy.wait_recv()

    middle = early // 2

    def first_phase(step, carry):
        again = step == 1

        @pl.when(again)
        def _():
            later_half(1)
            for sub in range(each):
                compose(sub)

        @pl.when(again & (chip == 0))
        def _():
            chain_range(0, early)

        edges(step)
        prepare(step, 0)
        invert(step)

        def finish_solve(sub, none):
            solve(step * each + sub)
            send_maps(step * each + sub)

            @pl.when(again & (chip == 1))
            def _():
                chain_range(sub * middle, (sub + 1) * middle)

            return none

        lax.fori_loop(0, each, finish_solve, 0)
        return carry

    lax.fori_loop(0, parts, first_phase, 0)

    compose(each)

    @pl.when(chip == 0)
    def _():
        chain_range(early, early + middle)


    def second_phase(slot, carry):
        @pl.when(slot < pieces)
        def _():
            read_local(slot)

        @pl.when(slot == 0)
        def _():
            for sub in range(1, each):
                compose(each + sub)

        @pl.when(slot == pieces)
        def _():
            def sent(index, none):
                pair_copy(theirs(index)).wait_send()
                return none

            lax.fori_loop(0, heads // 2, sent, 0)

        def pick(places):
            first, last = 0, 0
            for at, start, end in places:
                first = jnp.where(slot == at, start, first)
                last = jnp.where(slot == at, end, last)
            return first, last

        late = early + middle
        plans = [
            pick([(0, late, items)]),
            pick([(2, early, late), (3, late, items)]),
            pick([(1, 0, middle), (2, middle, early), (3, early, late), (4, late, items)]),
            pick([(4, 0, late), (6, late, items)]),
        ]
        first, last = plans[3]
        for which in range(3):
            first = jnp.where(chip == which, plans[which][0], first)
            last = jnp.where(chip == which, plans[which][1], last)
        chain_range(first, last)

        @pl.when(slot > pieces)
        def _():
            read(slot - pieces - 1)

        return carry

    lax.fori_loop(0, 2 * pieces + 1, second_phase, 0)

    @pl.when(has_right)
    def _():
        border_copy.wait_send()

    def finish(index, carry):
        back_copy(mine(index)).wait_send()

        @pl.when(forwards)
        def _():
            state_copy(mine(index)).wait_send()

        return carry

    lax.fori_loop(0, heads // 2, finish, 0)


def body(
    queries,
    key_pairs,
    value_pairs,
    strengths,
    decays,
    conv_query,
    conv_key,
    conv_value,
    doc_lengths,
):
    heads, tokens, width = queries.shape
    n_seq = lax.axis_size("seq")
    steps = 2 * tokens
    vmem = pl.BlockSpec(memory_space=pltpu.VMEM)
    return pl.pallas_call(
        functools.partial(kernel, n_seq),
        out_shape=pltpu.VMEM((heads, tokens, width), BF),
        in_specs=[pl.BlockSpec(memory_space=pltpu.HBM)] * 9,
        out_specs=vmem,
        scratch_shapes=[
            pltpu.SMEM(doc_lengths.shape, jnp.int32),
            pltpu.VMEM(queries.shape, BF),
            pltpu.VMEM(key_pairs.shape, BF),
            pltpu.VMEM(value_pairs.shape, BF),
            pltpu.VMEM(strengths.shape, F32),
            pltpu.VMEM(decays.shape, F32),
            pltpu.VMEM(conv_query.shape, F32),
            pltpu.VMEM(conv_key.shape, F32),
            pltpu.VMEM(conv_value.shape, F32),
            pltpu.VMEM((heads, 16, width), BF),
            pltpu.VMEM((heads, 16, 2 * width), BF),
            pltpu.VMEM((heads, 16, 2 * width), BF),
            pltpu.VMEM((4 * heads, 5 * width), BF),
            pltpu.VMEM((4 * heads, 5 * width), BF),
            pltpu.VMEM((heads, 5, 16 + tokens, width), F32),
            pltpu.VMEM((3, tokens, tokens), F32),
            pltpu.VMEM((2, tokens, tokens), F32),
            pltpu.VMEM((2, tokens // 2, tokens), F32),
            pltpu.VMEM((tokens, tokens), F32),
            pltpu.VMEM((tokens, tokens), F32),
            pltpu.VMEM((8 * heads, tokens), F32),
            pltpu.VMEM((8, steps), F32),
            pltpu.VMEM((2, tokens, heads), F32),
            pltpu.VMEM((2 * heads, tokens, tokens), BF),
            pltpu.VMEM((2 * heads, tokens, tokens), BF),
            pltpu.VMEM((2 * heads, tokens, tokens), BF),
            pltpu.VMEM((heads, 2, tokens, width), BF),
            pltpu.VMEM((heads, 2, tokens, width), BF),
            pltpu.VMEM((heads, 2, tokens, 2 * width), BF),
            pltpu.VMEM((heads, 2, tokens, 2 * width), BF),
            pltpu.VMEM((heads, width, 2 * width), BF),
            pltpu.VMEM((PART, tokens, width), F32),
            pltpu.VMEM((heads, width, width), F32),
            pltpu.VMEM((heads, width, width), BF),
            pltpu.VMEM((heads, tokens, width), F32),
            pltpu.VMEM((heads, tokens, width), BF),
            pltpu.VMEM((heads, width, width), BF),
            pltpu.VMEM((heads, 2, width, 2 * width), BF),
            pltpu.VMEM((heads, 2, width, width), BF),
            pltpu.SemaphoreType.DMA((9 + 3 * (heads // GROUP),)),
            pltpu.SemaphoreType.DMA,
            pltpu.SemaphoreType.DMA,
            pltpu.SemaphoreType.DMA((heads,)),
            pltpu.SemaphoreType.DMA((heads,)),
            pltpu.SemaphoreType.DMA((heads,)),
            pltpu.SemaphoreType.DMA((heads,)),
            pltpu.SemaphoreType.DMA((heads,)),
            pltpu.SemaphoreType.DMA((heads,)),
        ],
        compiler_params=pltpu.CompilerParams(
            collective_id=0, has_side_effects=True, vmem_limit_bytes=60 << 20
        ),
        name="delta_product",
    )(
        doc_lengths,
        queries,
        key_pairs,
        value_pairs,
        strengths,
        decays,
        conv_query,
        conv_key,
        conv_value,
    )


def solution(mesh):
    in_specs = (
        P(None, ("dp", "seq"), None),
        P(None, ("dp", "seq"), None),
        P(None, ("dp", "seq"), None),
        P(None, ("dp", "seq")),
        P(None, ("dp", "seq")),
        P(),
        P(),
        P(),
        P("dp"),
    )
    out_specs = P(None, ("dp", "seq"), None)
    return jax.shard_map(body, mesh=mesh, in_specs=in_specs, out_specs=out_specs, check_vma=False)
```

```python
import functools

import jax
import jax.numpy as jnp
from jax import lax
from jax.experimental import pallas as pl
from jax.experimental.pallas import tpu as pltpu
from jax.sharding import PartitionSpec as P

MESH = pl.DeviceIdType.MESH
BF = jnp.bfloat16
F32 = jnp.float32
GROUP = 8
PART = 4
TOGETHER = 1
ROWS = 8
NT = (((1,), (1,)), ((), ()))
NN = (((1,), (0,)), ((), ()))


def mm(a, b):
    return jnp.dot(a.astype(BF), b.astype(BF), preferred_element_type=F32)


def thirds(a):
    high = a.astype(BF)
    rest = a - high.astype(F32)
    middle = rest.astype(BF)
    return high, middle, (rest - middle.astype(F32)).astype(BF)


def iota(shape, axis):
    return lax.broadcasted_iota(jnp.int32, shape, axis)


def token_in_half(index):
    return index // ROWS + ROWS * (index % ROWS)


def kernel(
    n_seq,
    docs_hbm,
    q_hbm,
    k_hbm,
    v_hbm,
    strength_hbm,
    decay_hbm,
    cq_hbm,
    ck_hbm,
    cv_hbm,
    out_ref,
    docs_ref,
    q_ref,
    k_ref,
    v_ref,
    strength_ref,
    decay_ref,
    cq_ref,
    ck_ref,
    cv_ref,
    bq_ref,
    bk_ref,
    bv_ref,
    edge_out_ref,
    edge_in_ref,
    ext_ref,
    usable_ref,
    ordered_ref,
    reads_ref,
    open_ref,
    level_ref,
    twin_ref,
    rows_ref,
    open_lane_ref,
    run_cols_ref,
    weighted_ref,
    inverse_ref,
    system_ref,
    values_ref,
    keys_ref,
    solved_ref,
    rest_ref,
    middle_ref,
    spread_ref,
    terms_ref,
    transit_ref,
    local_ref,
    correction_ref,
    leaving_ref,
    maps_ref,
    states_ref,
    load_sem,
    border_send,
    border_recv,
    pair_send,
    pair_recv,
    state_send,
    state_recv,
    back_send,
    back_recv,
):
    heads, tokens, width = q_ref.shape
    half = tokens // 2
    steps = 2 * tokens
    parts = heads // GROUP
    me = lax.axis_index("seq")
    chip = me // 2
    chips = n_seq // 2
    upper = me % 2 == 1
    lower = me % 2 == 0
    offset = me * tokens
    has_left = me > 0
    has_right = me < n_seq - 1
    barrier = pltpu.get_barrier_semaphore()

    side = me % 2
    partner = me + 1 - 2 * side
    forwards = chip < chips - 1
    pl.semaphore_signal(barrier, inc=1, device_id={"seq": partner}, device_id_type=MESH)

    @pl.when(lower & has_left)
    def _():
        pl.semaphore_signal(barrier, inc=1, device_id={"seq": me - 1}, device_id_type=MESH)

    @pl.when(chip > 0)
    def _():
        pl.semaphore_signal(barrier, inc=1, device_id={"seq": me - 2}, device_id_type=MESH)

    spans = [pl.ds(part * GROUP, GROUP) for part in range(parts)]
    wide = [(q_hbm, q_ref), (k_hbm, k_ref), (v_hbm, v_ref)]
    small = [
        (docs_hbm, docs_ref),
        (decay_hbm, decay_ref),
        (strength_hbm, strength_ref),
        (cq_hbm, cq_ref),
        (ck_hbm, ck_ref),
        (cv_hbm, cv_ref),
    ]
    small_loads = [
        pltpu.make_async_copy(source, target, load_sem.at[i])
        for i, (source, target) in enumerate(small)
    ]
    wide_loads = [
        [
            pltpu.make_async_copy(
                source.at[span], target.at[span], load_sem.at[len(small) + 3 * part + i]
            )
            for i, (source, target) in enumerate(wide)
        ]
        for part, span in enumerate(spans)
    ]
    tails = [
        pltpu.make_async_copy(
            source.at[:, pl.ds(tokens - 16, 16), :], target, load_sem.at[len(small) + 3 * parts + i]
        )
        for i, (source, target) in enumerate([(q_hbm, bq_ref), (k_hbm, bk_ref), (v_hbm, bv_ref)])
    ]
    for copy in tails + small_loads + sum(wide_loads, []):
        copy.start()

    border_copy = pltpu.make_async_remote_copy(
        src_ref=edge_out_ref,
        dst_ref=edge_in_ref,
        send_sem=border_send,
        recv_sem=border_recv,
        device_id={"seq": me + 1},
        device_id_type=MESH,
    )
    columns = [(bq_ref, 0), (bk_ref, 0), (bk_ref, width), (bv_ref, 0), (bv_ref, width)]

    def pack_edges():
        low = iota((ROWS, width), 0) < 4
        for place, (tail_ref, lane) in enumerate(columns):
            for quad in range(heads // 4):
                rows = [
                    tail_ref[4 * quad + i, :, lane : lane + width].astype(F32)[8:16]
                    for i in range(4)
                ]
                tiles = [
                    jnp.where(low, pltpu.roll(rows[2 * i], 4, 0), rows[2 * i + 1])
                    for i in range(2)
                ]
                edge_out_ref[16 * quad : 16 * quad + 16, place * width : (place + 1) * width] = (
                    jnp.concatenate(tiles, axis=0).astype(BF)
                )

    def place_edge(slot, u, quad, place):
        rows = edge_in_ref[
            pl.ds(pl.multiple_of(16 * quad, 16), 16), place * width : (place + 1) * width
        ].astype(F32)
        tile = rows[8 * (u % 4 // 2) : 8 * (u % 4 // 2) + 8]
        ext_ref[slot, place, 8:16] = pltpu.roll(tile, 4, 0) if u % 2 == 0 else tile

    def exchange(source, target, head, sends, receives, device):
        return pltpu.make_async_remote_copy(
            src_ref=source,
            dst_ref=target,
            send_sem=sends.at[head],
            recv_sem=receives.at[head],
            device_id={"seq": device},
            device_id_type=MESH,
        )

    def pair_copy(head):
        place = maps_ref.at[head, side]
        return exchange(place, place, head, pair_send, pair_recv, partner)

    def pair_arrival(head):
        place = maps_ref.at[head, 1 - side]
        return exchange(place, place, head, pair_send, pair_recv, partner)

    def state_copy(head):
        return exchange(
            leaving_ref.at[head], states_ref.at[head, 0], head, state_send, state_recv, me + 2
        )

    def back_copy(head):
        place = states_ref.at[head, 1 - side]
        return exchange(place, place, head, back_send, back_recv, partner)

    def back_arrival(head):
        place = states_ref.at[head, side]
        return exchange(place, place, head, back_send, back_recv, partner)

    for copy in tails:
        copy.wait()
    pack_edges()

    @pl.when(forwards)
    def _():
        pl.semaphore_wait(barrier, 2 + side)

    @pl.when(jnp.logical_not(forwards))
    def _():
        pl.semaphore_wait(barrier, 1)

    @pl.when(has_right)
    def _():
        border_copy.start()

    @pl.when(me == 0)
    def _():
        edge_in_ref[...] = jnp.zeros_like(edge_in_ref)

    @pl.when(chip == 0)
    def _():
        states_ref[...] = jnp.zeros_like(states_ref)

    for copy in small_loads:
        copy.wait()

    starts = []
    total = jnp.int32(0)
    for m in range(docs_ref.shape[0]):
        starts.append(total)
        total = total + docs_ref[m]

    def latest_of(position):
        latest = jnp.zeros_like(position)
        for start in starts:
            latest = jnp.where(start <= position, start, latest)
        return latest

    def token_of(row):
        return (row // half) * half + token_in_half(row % half)

    def lane_token(lane):
        return (lane // tokens) * half + token_in_half(lane % half)

    square = (tokens, tokens)
    token_col = token_of(iota(square, 0))
    latest_col = latest_of(offset + token_col)
    since = offset + token_col - latest_col
    for lag in range(1, 4):
        usable_ref[lag - 1] = jnp.where(since >= lag, 1.0, 0.0)
    lane = iota((8, steps), 1)
    token_row = lane_token(lane)
    latest_row = latest_of(offset + token_row)
    half_start = offset + (lane // tokens) * half
    open_row = jnp.where(latest_row < half_start, 1.0, 0.0)
    final = [
        jnp.max(latest_row[:, h * tokens : (h + 1) * tokens], axis=1, keepdims=True)
        for h in range(2)
    ]
    same_row = jnp.where(
        latest_row == jnp.where(lane < tokens, final[0], final[1]), 1.0, 0.0
    )
    whole = [jnp.where(final[h] < offset + h * half, 1.0, 0.0) for h in range(2)]
    for h in range(2):
        here = slice(h * half, (h + 1) * half)
        lanes = slice(h * tokens, (h + 1) * tokens)
        sub_row = 2 * token_row[0:1, lanes] + (iota((1, tokens), 1) // half)
        token_here = jnp.concatenate([token_col[here], token_col[here]], axis=0)
        latest_here = jnp.concatenate([latest_col[here], latest_col[here]], axis=0)
        sub_col = 2 * token_here + iota(square, 0) // half
        linked = (latest_here == latest_row[0:1, lanes]) & (sub_col > sub_row)
        ordered_ref[h] = jnp.where(linked, -1.0, 0.0)
        reads = (latest_col[here] == latest_row[0:1, lanes]) & (
            token_col[here] >= token_row[0:1, lanes]
        )
        reads_ref[h] = jnp.where(reads, 1.0, 0.0)
    open_col = latest_col < offset + (iota(square, 0) // half) * half
    open_ref[...] = jnp.where(open_col, 1.0, 0.0)
    apart = token_in_half(iota(square, 0) % half) ^ token_in_half(iota(square, 1) % half)
    depth = jnp.zeros(square, F32)
    level = 1
    while level < half:
        depth = depth + jnp.where(apart >= level, 1.0, 0.0)
        level *= 2
    level_ref[...] = depth
    twin_ref[...] = jnp.where(apart == 0, 1.0, 0.0)

    def exact(pieces, chosen, dims=NN):
        return sum(
            lax.dot_general(piece, chosen, dims, preferred_element_type=F32)
            for piece in pieces
        )

    sub_row = 2 * token_row[0:1] + (iota((1, steps), 1) % tokens) // half
    pick = jnp.where(iota((steps, steps), 0) == sub_row, 1.0, 0.0).astype(BF)
    beta = exact(thirds(strength_ref[...]), pick)
    decay = thirds(decay_ref[...])
    at = iota((tokens, steps), 0)
    lane_half = iota((tokens, steps), 1) // tokens
    middle = lane_half * half + half // 2
    opening = (at >= lane_half * half) & (at < middle)
    closing = (at >= middle) & (at < (lane_half + 1) * half)
    to_middle = jnp.exp(-exact(decay, jnp.where(opening, 1.0, 0.0).astype(BF)))
    to_end = jnp.exp(-exact(decay, jnp.where(closing, 1.0, 0.0).astype(BF)))
    open_lane_ref[...] = open_row
    whole_row = jnp.where(lane < tokens, whole[0], whole[1])
    for which, table in enumerate(
        (
            beta,
            beta * to_end * same_row[0:1],
            to_middle,
            to_middle * to_end * whole_row[0:1],
        )
    ):
        for h in range(2):
            place = (2 * which + h) * heads
            rows_ref[place : place + heads, :] = table[:, h * tokens : (h + 1) * tokens]
    middle_col = (token_col // half) * half + half // 2
    past_col = jnp.where(iota(square, 1) <= token_col, 1.0, 0.0) - jnp.where(
        iota(square, 1) < middle_col, 1.0, 0.0
    )
    past_col = past_col.astype(BF)
    from_middle_col = sum(
        lax.dot_general(past_col, piece, NT, preferred_element_type=F32)
        for piece in decay
    )
    run_cols_ref[0] = jnp.exp(-from_middle_col)
    run_cols_ref[1] = jnp.exp(from_middle_col)

    lane_head = iota((tokens, heads), 1)
    eye = jnp.where(iota((width, width), 0) == iota((width, width), 1), 1.0, 0.0)
    unit_eye = eye.astype(BF)
    both = range(GROUP)

    def convolved(u, head, lane, kernel_ref, column, h):
        taps = [kernel_ref[head, lag : lag + 1, column : column + width] for lag in range(4)]
        pieces = []
        loaded = [
            ext_ref[u, lane, pl.ds(16 + h * half + k, ROWS, stride=half // ROWS), :]
            for k in range(-3, half // ROWS)
        ]
        for i in range(half // ROWS):
            rows = slice(h * half + i * ROWS, h * half + (i + 1) * ROWS)
            summed = taps[0] * loaded[i + 3]
            for lag in range(1, 4):
                summed = summed + usable_ref[lag - 1, rows, :] * (taps[lag] * loaded[i + 3 - lag])
            pieces.append(summed)
        summed = jnp.concatenate(pieces, axis=0)
        return summed / (1.0 + jnp.exp(-summed))

    def unit(rows):
        scale = lax.rsqrt(jnp.sum(rows * rows, axis=1, keepdims=True) + 1e-6)
        return (rows * scale).astype(BF)

    def column(which, head, h):
        rows = slice(h * half, (h + 1) * half)
        return jnp.sum(
            jnp.where(lane_head[:half] == head, run_cols_ref[which, rows, :], 0.0),
            axis=1,
            keepdims=True,
        )

    def split(a):
        high = a.astype(BF)
        return high, (a - high.astype(F32)).astype(BF)

    def stage(part):
        for u in both:
            head = part * GROUP + u
            for j in range(2):
                lanes = slice(j * width, (j + 1) * width)
                ext_ref[head, 1 + j, 16 : 16 + tokens] = k_ref[head, :, lanes].astype(F32)
                ext_ref[head, 3 + j, 16 : 16 + tokens] = v_ref[head, :, lanes].astype(F32)

    def edges(part):
        for u in both:
            for place in range(1, 5):
                place_edge(part * GROUP + u, u, part * (GROUP // 4) + u // 4, place)

    def prepare(part, h):
        ids = [part * GROUP + u for u in both]

        def row(which, u):
            return rows_ref[pl.ds((2 * which + h) * heads + ids[u], 1), :]

        keys = [
            jnp.concatenate(
                [
                    unit(convolved(head, head, 1 + j, ck_ref, j * width, h))
                    for j in range(2)
                ],
                axis=0,
            )
            for head in ids
        ]
        products = [
            lax.dot_general(
                jnp.concatenate([key, unit_eye], axis=0), key, NT, preferred_element_type=F32
            )
            for key in keys
        ]
        for u in both:
            place = 2 * ids[u] + h
            keys_ref[ids[u], h] = keys[u]
            weighted_ref[place] = (products[u][tokens:] * row(1, u)).astype(BF)
            block = (products[u][:tokens] * ordered_ref[h]) * row(0, u)
            inverse_ref[place] = (block * twin_ref[...] + eye).astype(BF)
            system_ref[place] = block.astype(BF)
        for head in ids:
            scale = column(1, head, h)
            for j in range(2):
                rows = convolved(head, head, 3 + j, cv_ref, j * width, h).astype(BF).astype(F32)
                values_ref[head, h, j * half : (j + 1) * half] = (rows * scale).astype(BF)

    def invert(part):
        base = part * 2 * GROUP
        depth = level_ref[...]
        count = range(2 * GROUP)
        for low in range(1, int(half).bit_length(), 2):
            fresh = depth >= low * 1.0
            near = (depth == low * 1.0) | (depth == low + 1.0)
            far = depth == low + 1.0
            ahead = [
                mm(
                    inverse_ref[base + i],
                    jnp.where(fresh, system_ref[base + i].astype(F32), 0.0),
                ).astype(BF)
                for i in count
            ]
            wide = [
                mm(ahead[i], jnp.concatenate([ahead[i], inverse_ref[base + i]], axis=1))
                for i in count
            ]
            for i in count:
                once = jnp.where(near, wide[i][:, tokens:], inverse_ref[base + i].astype(F32))
                twice = mm(wide[i][:, :tokens], once)
                inverse_ref[base + i] = jnp.where(far, once + twice, once).astype(BF)

    def solve(part):
        ids = [part * PART + u for u in range(PART)]
        base = 2 * part * PART
        sides = [(u, h) for u in range(PART) for h in range(2)]

        def row(which, u, h):
            return rows_ref[pl.ds((2 * which + h) * heads + ids[u], 1), :]

        scaled = [mm(inverse_ref[base + i], values_ref[ids[u], h]) for i, (u, h) in enumerate(sides)]
        opens = [
            open_lane_ref[0:1, h * tokens : (h + 1) * tokens].astype(BF) for h in range(2)
        ]
        carried = [mm(inverse_ref[base + i] * opens[h], keys_ref[ids[u], h]) for i, (u, h) in enumerate(sides)]
        start = [row(2, u, 0) for u in range(PART)]
        first = [
            split(jnp.concatenate([scaled[2 * u], carried[2 * u] * start[u]], axis=1))
            for u in range(PART)
        ]
        moved = [mm(weighted_ref[base + 2 * u], first[u][0]) for u in range(PART)]
        through = [[row(3, u, h) for h in range(2)] for u in range(PART)]
        terms = [moved[u][:, :width] for u in range(PART)]
        transit = [through[u][0] * eye - moved[u][:, width:] for u in range(PART)]
        later = [row(2, u, 1) for u in range(PART)]
        between = [
            jnp.concatenate(
                [(later[u] * terms[u]).astype(BF), (later[u] * transit[u]).astype(BF)], axis=1
            )
            for u in range(PART)
        ]
        brought = [mm(carried[2 * u + 1], between[u]) for u in range(PART)]
        second = [
            split(
                jnp.concatenate(
                    [scaled[2 * u + 1] - brought[u][:, :width], brought[u][:, width:]], axis=1
                )
            )
            for u in range(PART)
        ]
        moved = [mm(weighted_ref[base + 2 * u + 1], second[u][0]) for u in range(PART)]
        for u in range(PART):
            term = through[u][1] * terms[u] + moved[u][:, :width]
            on = (through[u][1] * transit[u] - moved[u][:, width:]).astype(BF)
            maps_ref[ids[u], side] = jnp.concatenate([term.astype(BF), on], axis=1)
            middle_ref[ids[u]] = between[u]
            for h, solved in enumerate((first[u], second[u])):
                solved_ref[ids[u], h] = solved[0]
                rest_ref[ids[u], h] = solved[1]

    def read_local(part):
        some = range(PART)
        ids = [part * PART + u for u in some]
        for u in some:
            place_edge(ids[u], u, part, 0)
            ext_ref[ids[u], 0, 16 : 16 + tokens] = q_ref[ids[u]].astype(F32)
        query = [
            jnp.concatenate(
                [unit(convolved(head, head, 0, cq_ref, 0, h)) for h in range(2)], axis=0
            )
            for head in ids
        ]
        sides = [(u, h) for u in some for h in range(2)]

        def here(rows, h):
            return rows[h * half : (h + 1) * half]

        def row(which, u, h):
            return rows_ref[pl.ds((2 * which + h) * heads + ids[u], 1), :]

        scores = [
            lax.dot_general(
                here(query[u], h), keys_ref[ids[u], h], NT, preferred_element_type=F32
            )
            for u, h in sides
        ]
        mixing = [
            split((scores[i] * reads_ref[h]) * row(0, u, h))
            for i, (u, h) in enumerate(sides)
        ]
        gathered = [
            mm(jnp.concatenate(mixing[i], axis=0), solved_ref[ids[u], h])
            for i, (u, h) in enumerate(sides)
        ]
        gathered = [
            gathered[i][:half] + (gathered[i][half:] + mm(mixing[i][0], rest_ref[ids[u], h]))
            for i, (u, h) in enumerate(sides)
        ]
        opened = [query[u].astype(F32) * open_ref[...] for u in some]
        brought = [mm(here(opened[u], 1), middle_ref[ids[u]]) for u in some]
        for u in some:
            start = row(2, u, 0)
            early, late = gathered[2 * u], gathered[2 * u + 1]
            local_ref[ids[u]] = jnp.concatenate(
                [early[:, :width], brought[u][:, :width] + late[:, :width]], axis=0
            )
            correction_ref[ids[u]] = jnp.concatenate(
                [
                    (start * here(opened[u], 0) - early[:, width:]).astype(BF),
                    (brought[u][:, width:] - late[:, width:]).astype(BF),
                ],
                axis=0,
            )

    def finish_rows(u, head, state):
        rows = local_ref[head] + mm(correction_ref[head], state)
        rows = rows * jnp.concatenate([column(0, head, h) for h in range(2)], axis=0)
        for h in range(2):
            for i in range(half // ROWS):
                spread_ref[u, pl.ds(h * half + i, ROWS, stride=half // ROWS), :] = rows[
                    h * half + i * ROWS : h * half + (i + 1) * ROWS
                ]
        out_ref[head] = spread_ref[u].astype(BF)

    some = range(PART)
    pieces = heads // PART
    owned = PART // 2
    items = heads // 2 // TOGETHER

    def mine(index):
        return (index // owned) * PART + side * owned + index % owned

    def theirs(index):
        return (index // owned) * PART + (1 - side) * owned + index % owned

    def send_maps(part):
        for u in range(owned):
            pair_copy(theirs(part * owned + u)).start()

    def compose(part):
        ids = [mine(part * owned + u) for u in range(owned)]
        for head in ids:
            pair_arrival(head).wait_recv()
        composed = [mm(maps_ref[head, 1, :, width:], maps_ref[head, 0]) for head in ids]
        for head, both_maps in zip(ids, composed):
            terms_ref[head] = maps_ref[head, 1, :, :width].astype(F32) + both_maps[:, :width]
            transit_ref[head] = both_maps[:, width:].astype(BF)

    def chain(item):
        ids = [mine(item * TOGETHER + u) for u in range(TOGETHER)]

        @pl.when(chip > 0)
        def _():
            for head in ids:
                state_copy(head).wait_recv()

        steps_on = [
            mm(
                jnp.concatenate([transit_ref[head], maps_ref[head, 0, :, width:]], axis=0),
                states_ref[head, 0],
            )
            for head in ids
        ]
        for head, both_ends in zip(ids, steps_on):
            leaving_ref[head] = (terms_ref[head] + both_ends[:width]).astype(BF)
            inner = maps_ref[head, 0, :, :width].astype(F32) + both_ends[width:]
            states_ref[head, 1] = inner.astype(BF)

        @pl.when(forwards)
        def _():
            for head in ids:
                state_copy(head).start()

        for head in ids:
            back_copy(head).start()

    def read(part):
        ids = [part * PART + u for u in some]

        for u in range(owned):
            back_arrival(theirs(part * owned + u)).wait_recv()

        for u in some:
            finish_rows(u, ids[u], states_ref[ids[u], side])

    early = items // parts
    each = GROUP // PART

    def chain_range(first, last):
        lax.fori_loop(first, last, lambda item, none: (chain(item), none)[1], 0)

    def later_half(part):
        for copy in wide_loads[part]:
            copy.wait()

        stage(part)
        prepare(part, 1)

    later_half(0)

    @pl.when(has_left)
    def _():
        border_copy.wait_recv()

    middle = early // 2

    def first_phase(step, carry):
        again = step == 1

        @pl.when(again)
        def _():
            later_half(1)
            for sub in range(each):
                compose(sub)

                @pl.when(chip == 0)
                def _():
                    chain_range(sub * middle, (sub + 1) * middle)

        edges(step)
        prepare(step, 0)
        invert(step)

        def finish_solve(sub, none):
            solve(step * each + sub)
            send_maps(step * each + sub)

            @pl.when(again & (chip == 1))
            def _():
                chain_range(sub * middle, (sub + 1) * middle)

            return none

        lax.fori_loop(0, each, finish_solve, 0)
        return carry

    lax.fori_loop(0, parts, first_phase, 0)

    compose(each)

    @pl.when(chip == 0)
    def _():
        chain_range(early, early + middle)


    def second_phase(slot, carry):
        @pl.when(slot < pieces)
        def _():
            read_local(slot)

        @pl.when(slot == 0)
        def _():
            for sub in range(1, each):
                compose(each + sub)

        @pl.when(slot == pieces)
        def _():
            def sent(index, none):
                pair_copy(theirs(index)).wait_send()
                return none

            lax.fori_loop(0, heads // 2, sent, 0)

        def pick(places):
            first, last = 0, 0
            for at, start, end in places:
                first = jnp.where(slot == at, start, first)
                last = jnp.where(slot == at, end, last)
            return first, last

        late = early + middle
        plans = [
            pick([(0, late, items)]),
            pick([(2, early, late), (3, late, items)]),
            pick([(1, 0, middle), (2, middle, early), (3, early, late), (4, late, items)]),
            pick([(4, 0, late), (6, late, items)]),
        ]
        first, last = plans[3]
        for which in range(3):
            first = jnp.where(chip == which, plans[which][0], first)
            last = jnp.where(chip == which, plans[which][1], last)
        chain_range(first, last)

        @pl.when(slot > pieces)
        def _():
            read(slot - pieces - 1)

        return carry

    lax.fori_loop(0, 2 * pieces + 1, second_phase, 0)

    @pl.when(has_right)
    def _():
        border_copy.wait_send()

    def finish(index, carry):
        back_copy(mine(index)).wait_send()

        @pl.when(forwards)
        def _():
            state_copy(mine(index)).wait_send()

        return carry

    lax.fori_loop(0, heads // 2, finish, 0)


def body(
    queries,
    key_pairs,
    value_pairs,
    strengths,
    decays,
    conv_query,
    conv_key,
    conv_value,
    doc_lengths,
):
    heads, tokens, width = queries.shape
    n_seq = lax.axis_size("seq")
    steps = 2 * tokens
    vmem = pl.BlockSpec(memory_space=pltpu.VMEM)
    return pl.pallas_call(
        functools.partial(kernel, n_seq),
        out_shape=pltpu.VMEM((heads, tokens, width), BF),
        in_specs=[pl.BlockSpec(memory_space=pltpu.HBM)] * 9,
        out_specs=vmem,
        scratch_shapes=[
            pltpu.SMEM(doc_lengths.shape, jnp.int32),
            pltpu.VMEM(queries.shape, BF),
            pltpu.VMEM(key_pairs.shape, BF),
            pltpu.VMEM(value_pairs.shape, BF),
            pltpu.VMEM(strengths.shape, F32),
            pltpu.VMEM(decays.shape, F32),
            pltpu.VMEM(conv_query.shape, F32),
            pltpu.VMEM(conv_key.shape, F32),
            pltpu.VMEM(conv_value.shape, F32),
            pltpu.VMEM((heads, 16, width), BF),
            pltpu.VMEM((heads, 16, 2 * width), BF),
            pltpu.VMEM((heads, 16, 2 * width), BF),
            pltpu.VMEM((4 * heads, 5 * width), BF),
            pltpu.VMEM((4 * heads, 5 * width), BF),
            pltpu.VMEM((heads, 5, 16 + tokens, width), F32),
            pltpu.VMEM((3, tokens, tokens), F32),
            pltpu.VMEM((2, tokens, tokens), F32),
            pltpu.VMEM((2, tokens // 2, tokens), F32),
            pltpu.VMEM((tokens, tokens), F32),
            pltpu.VMEM((tokens, tokens), F32),
            pltpu.VMEM((tokens, tokens), F32),
            pltpu.VMEM((8 * heads, tokens), F32),
            pltpu.VMEM((8, steps), F32),
            pltpu.VMEM((2, tokens, heads), F32),
            pltpu.VMEM((2 * heads, tokens, tokens), BF),
            pltpu.VMEM((2 * heads, tokens, tokens), BF),
            pltpu.VMEM((2 * heads, tokens, tokens), BF),
            pltpu.VMEM((heads, 2, tokens, width), BF),
            pltpu.VMEM((heads, 2, tokens, width), BF),
            pltpu.VMEM((heads, 2, tokens, 2 * width), BF),
            pltpu.VMEM((heads, 2, tokens, 2 * width), BF),
            pltpu.VMEM((heads, width, 2 * width), BF),
            pltpu.VMEM((PART, tokens, width), F32),
            pltpu.VMEM((heads, width, width), F32),
            pltpu.VMEM((heads, width, width), BF),
            pltpu.VMEM((heads, tokens, width), F32),
            pltpu.VMEM((heads, tokens, width), BF),
            pltpu.VMEM((heads, width, width), BF),
            pltpu.VMEM((heads, 2, width, 2 * width), BF),
            pltpu.VMEM((heads, 2, width, width), BF),
            pltpu.SemaphoreType.DMA((9 + 3 * (heads // GROUP),)),
            pltpu.SemaphoreType.DMA,
            pltpu.SemaphoreType.DMA,
            pltpu.SemaphoreType.DMA((heads,)),
            pltpu.SemaphoreType.DMA((heads,)),
            pltpu.SemaphoreType.DMA((heads,)),
            pltpu.SemaphoreType.DMA((heads,)),
            pltpu.SemaphoreType.DMA((heads,)),
            pltpu.SemaphoreType.DMA((heads,)),
        ],
        compiler_params=pltpu.CompilerParams(
            collective_id=0, has_side_effects=True, vmem_limit_bytes=60 << 20
        ),
        name="delta_product",
    )(
        doc_lengths,
        queries,
        key_pairs,
        value_pairs,
        strengths,
        decays,
        conv_query,
        conv_key,
        conv_value,
    )


def solution(mesh):
    in_specs = (
        P(None, ("dp", "seq"), None),
        P(None, ("dp", "seq"), None),
        P(None, ("dp", "seq"), None),
        P(None, ("dp", "seq")),
        P(None, ("dp", "seq")),
        P(),
        P(),
        P(),
        P("dp"),
    )
    out_specs = P(None, ("dp", "seq"), None)
    return jax.shard_map(body, mesh=mesh, in_specs=in_specs, out_specs=out_specs, check_vma=False)
```

```python
import functools

import jax
import jax.numpy as jnp
from jax import lax
from jax.experimental import pallas as pl
from jax.experimental.pallas import tpu as pltpu
from jax.sharding import PartitionSpec as P

MESH = pl.DeviceIdType.MESH
BF = jnp.bfloat16
F32 = jnp.float32
GROUP = 8
PART = 4
TOGETHER = 1
ROWS = 8
NT = (((1,), (1,)), ((), ()))
NN = (((1,), (0,)), ((), ()))


def mm(a, b):
    return jnp.dot(a.astype(BF), b.astype(BF), preferred_element_type=F32)


def thirds(a):
    high = a.astype(BF)
    rest = a - high.astype(F32)
    middle = rest.astype(BF)
    return high, middle, (rest - middle.astype(F32)).astype(BF)


def iota(shape, axis):
    return lax.broadcasted_iota(jnp.int32, shape, axis)


def token_in_half(index):
    return index // ROWS + ROWS * (index % ROWS)


def kernel(
    n_seq,
    docs_hbm,
    q_hbm,
    k_hbm,
    v_hbm,
    strength_hbm,
    decay_hbm,
    cq_hbm,
    ck_hbm,
    cv_hbm,
    out_ref,
    docs_ref,
    q_ref,
    k_ref,
    v_ref,
    strength_ref,
    decay_ref,
    cq_ref,
    ck_ref,
    cv_ref,
    bq_ref,
    bk_ref,
    bv_ref,
    edge_out_ref,
    edge_in_ref,
    ext_ref,
    usable_ref,
    ordered_ref,
    reads_ref,
    open_ref,
    level_ref,
    twin_ref,
    rows_ref,
    open_lane_ref,
    run_cols_ref,
    weighted_ref,
    inverse_ref,
    system_ref,
    values_ref,
    keys_ref,
    solved_ref,
    rest_ref,
    middle_ref,
    spread_ref,
    terms_ref,
    transit_ref,
    local_ref,
    correction_ref,
    leaving_ref,
    maps_ref,
    states_ref,
    load_sem,
    border_send,
    border_recv,
    pair_send,
    pair_recv,
    state_send,
    state_recv,
    back_send,
    back_recv,
):
    heads, tokens, width = q_ref.shape
    half = tokens // 2
    steps = 2 * tokens
    parts = heads // GROUP
    me = lax.axis_index("seq")
    chip = me // 2
    chips = n_seq // 2
    upper = me % 2 == 1
    lower = me % 2 == 0
    offset = me * tokens
    has_left = me > 0
    has_right = me < n_seq - 1
    barrier = pltpu.get_barrier_semaphore()

    side = me % 2
    partner = me + 1 - 2 * side
    forwards = chip < chips - 1
    pl.semaphore_signal(barrier, inc=1, device_id={"seq": partner}, device_id_type=MESH)

    @pl.when(lower & has_left)
    def _():
        pl.semaphore_signal(barrier, inc=1, device_id={"seq": me - 1}, device_id_type=MESH)

    @pl.when(chip > 0)
    def _():
        pl.semaphore_signal(barrier, inc=1, device_id={"seq": me - 2}, device_id_type=MESH)

    spans = [pl.ds(part * GROUP, GROUP) for part in range(parts)]
    wide = [(q_hbm, q_ref), (k_hbm, k_ref), (v_hbm, v_ref)]
    small = [
        (docs_hbm, docs_ref),
        (decay_hbm, decay_ref),
        (strength_hbm, strength_ref),
        (cq_hbm, cq_ref),
        (ck_hbm, ck_ref),
        (cv_hbm, cv_ref),
    ]
    small_loads = [
        pltpu.make_async_copy(source, target, load_sem.at[i])
        for i, (source, target) in enumerate(small)
    ]
    wide_loads = [
        [
            pltpu.make_async_copy(
                source.at[span], target.at[span], load_sem.at[len(small) + 3 * part + i]
            )
            for i, (source, target) in enumerate(wide)
        ]
        for part, span in enumerate(spans)
    ]
    tails = [
        pltpu.make_async_copy(
            source.at[:, pl.ds(tokens - 16, 16), :], target, load_sem.at[len(small) + 3 * parts + i]
        )
        for i, (source, target) in enumerate([(q_hbm, bq_ref), (k_hbm, bk_ref), (v_hbm, bv_ref)])
    ]
    for copy in tails + small_loads + sum(wide_loads, []):
        copy.start()

    border_copy = pltpu.make_async_remote_copy(
        src_ref=edge_out_ref,
        dst_ref=edge_in_ref,
        send_sem=border_send,
        recv_sem=border_recv,
        device_id={"seq": me + 1},
        device_id_type=MESH,
    )
    columns = [(bq_ref, 0), (bk_ref, 0), (bk_ref, width), (bv_ref, 0), (bv_ref, width)]

    def pack_edges():
        low = iota((ROWS, width), 0) < 4
        for place, (tail_ref, lane) in enumerate(columns):
            for quad in range(heads // 4):
                rows = [
                    tail_ref[4 * quad + i, :, lane : lane + width].astype(F32)[8:16]
                    for i in range(4)
                ]
                tiles = [
                    jnp.where(low, pltpu.roll(rows[2 * i], 4, 0), rows[2 * i + 1])
                    for i in range(2)
                ]
                edge_out_ref[16 * quad : 16 * quad + 16, place * width : (place + 1) * width] = (
                    jnp.concatenate(tiles, axis=0).astype(BF)
                )

    def place_edge(slot, u, quad, place):
        rows = edge_in_ref[
            pl.ds(pl.multiple_of(16 * quad, 16), 16), place * width : (place + 1) * width
        ].astype(F32)
        tile = rows[8 * (u % 4 // 2) : 8 * (u % 4 // 2) + 8]
        ext_ref[slot, place, 8:16] = pltpu.roll(tile, 4, 0) if u % 2 == 0 else tile

    def exchange(source, target, head, sends, receives, device):
        return pltpu.make_async_remote_copy(
            src_ref=source,
            dst_ref=target,
            send_sem=sends.at[head],
            recv_sem=receives.at[head],
            device_id={"seq": device},
            device_id_type=MESH,
        )

    def pair_copy(head):
        place = maps_ref.at[head, side]
        return exchange(place, place, head, pair_send, pair_recv, partner)

    def pair_arrival(head):
        place = maps_ref.at[head, 1 - side]
        return exchange(place, place, head, pair_send, pair_recv, partner)

    def state_copy(head):
        return exchange(
            leaving_ref.at[head], states_ref.at[head, 0], head, state_send, state_recv, me + 2
        )

    def back_copy(head):
        place = states_ref.at[head, 1 - side]
        return exchange(place, place, head, back_send, back_recv, partner)

    def back_arrival(head):
        place = states_ref.at[head, side]
        return exchange(place, place, head, back_send, back_recv, partner)

    for copy in tails:
        copy.wait()
    pack_edges()

    @pl.when(forwards)
    def _():
        pl.semaphore_wait(barrier, 2 + side)

    @pl.when(jnp.logical_not(forwards))
    def _():
        pl.semaphore_wait(barrier, 1)

    @pl.when(has_right)
    def _():
        border_copy.start()

    @pl.when(me == 0)
    def _():
        edge_in_ref[...] = jnp.zeros_like(edge_in_ref)

    @pl.when(chip == 0)
    def _():
        states_ref[...] = jnp.zeros_like(states_ref)

    for copy in small_loads:
        copy.wait()

    starts = []
    total = jnp.int32(0)
    for m in range(docs_ref.shape[0]):
        starts.append(total)
        total = total + docs_ref[m]

    def latest_of(position):
        latest = jnp.zeros_like(position)
        for start in starts:
            latest = jnp.where(start <= position, start, latest)
        return latest

    def token_of(row):
        return (row // half) * half + token_in_half(row % half)

    def lane_token(lane):
        return (lane // tokens) * half + token_in_half(lane % half)

    square = (tokens, tokens)
    token_col = token_of(iota(square, 0))
    latest_col = latest_of(offset + token_col)
    since = offset + token_col - latest_col
    for lag in range(1, 4):
        usable_ref[lag - 1] = jnp.where(since >= lag, 1.0, 0.0)
    lane = iota((8, steps), 1)
    token_row = lane_token(lane)
    latest_row = latest_of(offset + token_row)
    half_start = offset + (lane // tokens) * half
    open_row = jnp.where(latest_row < half_start, 1.0, 0.0)
    final = [
        jnp.max(latest_row[:, h * tokens : (h + 1) * tokens], axis=1, keepdims=True)
        for h in range(2)
    ]
    same_row = jnp.where(
        latest_row == jnp.where(lane < tokens, final[0], final[1]), 1.0, 0.0
    )
    whole = [jnp.where(final[h] < offset + h * half, 1.0, 0.0) for h in range(2)]
    for h in range(2):
        here = slice(h * half, (h + 1) * half)
        lanes = slice(h * tokens, (h + 1) * tokens)
        sub_row = 2 * token_row[0:1, lanes] + (iota((1, tokens), 1) // half)
        token_here = jnp.concatenate([token_col[here], token_col[here]], axis=0)
        latest_here = jnp.concatenate([latest_col[here], latest_col[here]], axis=0)
        sub_col = 2 * token_here + iota(square, 0) // half
        linked = (latest_here == latest_row[0:1, lanes]) & (sub_col > sub_row)
        ordered_ref[h] = jnp.where(linked, -1.0, 0.0)
        reads = (latest_col[here] == latest_row[0:1, lanes]) & (
            token_col[here] >= token_row[0:1, lanes]
        )
        reads_ref[h] = jnp.where(reads, 1.0, 0.0)
    open_col = latest_col < offset + (iota(square, 0) // half) * half
    open_ref[...] = jnp.where(open_col, 1.0, 0.0)
    apart = token_in_half(iota(square, 0) % half) ^ token_in_half(iota(square, 1) % half)
    depth = jnp.zeros(square, F32)
    level = 1
    while level < half:
        depth = depth + jnp.where(apart >= level, 1.0, 0.0)
        level *= 2
    level_ref[...] = depth
    twin_ref[...] = jnp.where(apart == 0, 1.0, 0.0)

    def exact(pieces, chosen, dims=NN):
        return sum(
            lax.dot_general(piece, chosen, dims, preferred_element_type=F32)
            for piece in pieces
        )

    sub_row = 2 * token_row[0:1] + (iota((1, steps), 1) % tokens) // half
    pick = jnp.where(iota((steps, steps), 0) == sub_row, 1.0, 0.0).astype(BF)
    beta = exact(thirds(strength_ref[...]), pick)
    decay = thirds(decay_ref[...])
    at = iota((tokens, steps), 0)
    lane_half = iota((tokens, steps), 1) // tokens
    middle = lane_half * half + half // 2
    opening = (at >= lane_half * half) & (at < middle)
    closing = (at >= middle) & (at < (lane_half + 1) * half)
    to_middle = jnp.exp(-exact(decay, jnp.where(opening, 1.0, 0.0).astype(BF)))
    to_end = jnp.exp(-exact(decay, jnp.where(closing, 1.0, 0.0).astype(BF)))
    open_lane_ref[...] = open_row
    whole_row = jnp.where(lane < tokens, whole[0], whole[1])
    for which, table in enumerate(
        (
            beta,
            beta * to_end * same_row[0:1],
            to_middle,
            to_middle * to_end * whole_row[0:1],
        )
    ):
        for h in range(2):
            place = (2 * which + h) * heads
            rows_ref[place : place + heads, :] = table[:, h * tokens : (h + 1) * tokens]
    middle_col = (token_col // half) * half + half // 2
    past_col = jnp.where(iota(square, 1) <= token_col, 1.0, 0.0) - jnp.where(
        iota(square, 1) < middle_col, 1.0, 0.0
    )
    past_col = past_col.astype(BF)
    from_middle_col = sum(
        lax.dot_general(past_col, piece, NT, preferred_element_type=F32)
        for piece in decay
    )
    run_cols_ref[0] = jnp.exp(-from_middle_col)
    run_cols_ref[1] = jnp.exp(from_middle_col)

    lane_head = iota((tokens, heads), 1)
    eye = jnp.where(iota((width, width), 0) == iota((width, width), 1), 1.0, 0.0)
    unit_eye = eye.astype(BF)
    both = range(GROUP)

    def convolved(u, head, lane, kernel_ref, column, h):
        taps = [kernel_ref[head, lag : lag + 1, column : column + width] for lag in range(4)]
        pieces = []
        loaded = [
            ext_ref[u, lane, pl.ds(16 + h * half + k, ROWS, stride=half // ROWS), :]
            for k in range(-3, half // ROWS)
        ]
        for i in range(half // ROWS):
            rows = slice(h * half + i * ROWS, h * half + (i + 1) * ROWS)
            summed = taps[0] * loaded[i + 3]
            for lag in range(1, 4):
                summed = summed + usable_ref[lag - 1, rows, :] * (taps[lag] * loaded[i + 3 - lag])
            pieces.append(summed)
        summed = jnp.concatenate(pieces, axis=0)
        return summed / (1.0 + jnp.exp(-summed))

    def unit(rows):
        scale = lax.rsqrt(jnp.sum(rows * rows, axis=1, keepdims=True) + 1e-6)
        return (rows * scale).astype(BF)

    def column(which, head, h):
        rows = slice(h * half, (h + 1) * half)
        return jnp.sum(
            jnp.where(lane_head[:half] == head, run_cols_ref[which, rows, :], 0.0),
            axis=1,
            keepdims=True,
        )

    def split(a):
        high = a.astype(BF)
        return high, (a - high.astype(F32)).astype(BF)

    def stage(part):
        for u in both:
            head = part * GROUP + u
            for j in range(2):
                lanes = slice(j * width, (j + 1) * width)
                ext_ref[head, 1 + j, 16 : 16 + tokens] = k_ref[head, :, lanes].astype(F32)
                ext_ref[head, 3 + j, 16 : 16 + tokens] = v_ref[head, :, lanes].astype(F32)

    def edges(part):
        for u in both:
            for place in range(1, 5):
                place_edge(part * GROUP + u, u, part * (GROUP // 4) + u // 4, place)

    def prepare(part, h):
        ids = [part * GROUP + u for u in both]

        def row(which, u):
            return rows_ref[pl.ds((2 * which + h) * heads + ids[u], 1), :]

        keys = [
            jnp.concatenate(
                [
                    unit(convolved(head, head, 1 + j, ck_ref, j * width, h))
                    for j in range(2)
                ],
                axis=0,
            )
            for head in ids
        ]
        products = [
            lax.dot_general(
                jnp.concatenate([key, unit_eye], axis=0), key, NT, preferred_element_type=F32
            )
            for key in keys
        ]
        for u in both:
            place = 2 * ids[u] + h
            keys_ref[ids[u], h] = keys[u]
            weighted_ref[place] = (products[u][tokens:] * row(1, u)).astype(BF)
            block = (products[u][:tokens] * ordered_ref[h]) * row(0, u)
            inverse_ref[place] = (block * twin_ref[...] + eye).astype(BF)
            system_ref[place] = block.astype(BF)
        for head in ids:
            scale = column(1, head, h)
            for j in range(2):
                rows = convolved(head, head, 3 + j, cv_ref, j * width, h).astype(BF).astype(F32)
                values_ref[head, h, j * half : (j + 1) * half] = (rows * scale).astype(BF)

    def invert(part):
        base = part * 2 * GROUP
        depth = level_ref[...]
        count = range(2 * GROUP)
        for low in range(1, int(half).bit_length(), 2):
            fresh = depth >= low * 1.0
            near = (depth == low * 1.0) | (depth == low + 1.0)
            far = depth == low + 1.0
            ahead = [
                mm(
                    inverse_ref[base + i],
                    jnp.where(fresh, system_ref[base + i].astype(F32), 0.0),
                ).astype(BF)
                for i in count
            ]
            wide = [
                mm(ahead[i], jnp.concatenate([ahead[i], inverse_ref[base + i]], axis=1))
                for i in count
            ]
            for i in count:
                once = jnp.where(near, wide[i][:, tokens:], inverse_ref[base + i].astype(F32))
                twice = mm(wide[i][:, :tokens], once)
                inverse_ref[base + i] = jnp.where(far, once + twice, once).astype(BF)

    def solve(part):
        ids = [part * PART + u for u in range(PART)]
        base = 2 * part * PART
        sides = [(u, h) for u in range(PART) for h in range(2)]

        def row(which, u, h):
            return rows_ref[pl.ds((2 * which + h) * heads + ids[u], 1), :]

        scaled = [mm(inverse_ref[base + i], values_ref[ids[u], h]) for i, (u, h) in enumerate(sides)]
        opens = [
            open_lane_ref[0:1, h * tokens : (h + 1) * tokens].astype(BF) for h in range(2)
        ]
        carried = [mm(inverse_ref[base + i] * opens[h], keys_ref[ids[u], h]) for i, (u, h) in enumerate(sides)]
        start = [row(2, u, 0) for u in range(PART)]
        first = [
            split(jnp.concatenate([scaled[2 * u], carried[2 * u] * start[u]], axis=1))
            for u in range(PART)
        ]
        moved = [mm(weighted_ref[base + 2 * u], first[u][0]) for u in range(PART)]
        through = [[row(3, u, h) for h in range(2)] for u in range(PART)]
        terms = [moved[u][:, :width] for u in range(PART)]
        transit = [through[u][0] * eye - moved[u][:, width:] for u in range(PART)]
        later = [row(2, u, 1) for u in range(PART)]
        between = [
            jnp.concatenate(
                [(later[u] * terms[u]).astype(BF), (later[u] * transit[u]).astype(BF)], axis=1
            )
            for u in range(PART)
        ]
        brought = [mm(carried[2 * u + 1], between[u]) for u in range(PART)]
        second = [
            split(
                jnp.concatenate(
                    [scaled[2 * u + 1] - brought[u][:, :width], brought[u][:, width:]], axis=1
                )
            )
            for u in range(PART)
        ]
        moved = [mm(weighted_ref[base + 2 * u + 1], second[u][0]) for u in range(PART)]
        for u in range(PART):
            term = through[u][1] * terms[u] + moved[u][:, :width]
            on = (through[u][1] * transit[u] - moved[u][:, width:]).astype(BF)
            maps_ref[ids[u], side] = jnp.concatenate([term.astype(BF), on], axis=1)
            middle_ref[ids[u]] = between[u]
            for h, solved in enumerate((first[u], second[u])):
                solved_ref[ids[u], h] = solved[0]
                rest_ref[ids[u], h] = solved[1]

    def read_local(part):
        some = range(PART)
        ids = [part * PART + u for u in some]
        for u in some:
            place_edge(ids[u], u, part, 0)
            ext_ref[ids[u], 0, 16 : 16 + tokens] = q_ref[ids[u]].astype(F32)
        query = [
            jnp.concatenate(
                [unit(convolved(head, head, 0, cq_ref, 0, h)) for h in range(2)], axis=0
            )
            for head in ids
        ]
        sides = [(u, h) for u in some for h in range(2)]

        def here(rows, h):
            return rows[h * half : (h + 1) * half]

        def row(which, u, h):
            return rows_ref[pl.ds((2 * which + h) * heads + ids[u], 1), :]

        scores = [
            lax.dot_general(
                here(query[u], h), keys_ref[ids[u], h], NT, preferred_element_type=F32
            )
            for u, h in sides
        ]
        mixing = [
            split((scores[i] * reads_ref[h]) * row(0, u, h))
            for i, (u, h) in enumerate(sides)
        ]
        gathered = [
            mm(jnp.concatenate(mixing[i], axis=0), solved_ref[ids[u], h])
            for i, (u, h) in enumerate(sides)
        ]
        gathered = [
            gathered[i][:half] + (gathered[i][half:] + mm(mixing[i][0], rest_ref[ids[u], h]))
            for i, (u, h) in enumerate(sides)
        ]
        opened = [query[u].astype(F32) * open_ref[...] for u in some]
        brought = [mm(here(opened[u], 1), middle_ref[ids[u]]) for u in some]
        for u in some:
            start = row(2, u, 0)
            early, late = gathered[2 * u], gathered[2 * u + 1]
            local_ref[ids[u]] = jnp.concatenate(
                [early[:, :width], brought[u][:, :width] + late[:, :width]], axis=0
            )
            correction_ref[ids[u]] = jnp.concatenate(
                [
                    (start * here(opened[u], 0) - early[:, width:]).astype(BF),
                    (brought[u][:, width:] - late[:, width:]).astype(BF),
                ],
                axis=0,
            )

    def finish_rows(u, head, state):
        rows = local_ref[head] + mm(correction_ref[head], state)
        rows = rows * jnp.concatenate([column(0, head, h) for h in range(2)], axis=0)
        for h in range(2):
            for i in range(half // ROWS):
                spread_ref[u, pl.ds(h * half + i, ROWS, stride=half // ROWS), :] = rows[
                    h * half + i * ROWS : h * half + (i + 1) * ROWS
                ]
        out_ref[head] = spread_ref[u].astype(BF)

    some = range(PART)
    pieces = heads // PART
    owned = PART // 2
    items = heads // 2 // TOGETHER

    def mine(index):
        return (index // owned) * PART + side * owned + index % owned

    def theirs(index):
        return (index // owned) * PART + (1 - side) * owned + index % owned

    def send_maps(part):
        for u in range(owned):
            pair_copy(theirs(part * owned + u)).start()

    def compose(part):
        ids = [mine(part * owned + u) for u in range(owned)]
        for head in ids:
            pair_arrival(head).wait_recv()
        composed = [mm(maps_ref[head, 1, :, width:], maps_ref[head, 0]) for head in ids]
        for head, both_maps in zip(ids, composed):
            terms_ref[head] = maps_ref[head, 1, :, :width].astype(F32) + both_maps[:, :width]
            transit_ref[head] = both_maps[:, width:].astype(BF)

    def chain(item):
        ids = [mine(item * TOGETHER + u) for u in range(TOGETHER)]

        @pl.when(chip > 0)
        def _():
            for head in ids:
                state_copy(head).wait_recv()

        steps_on = [
            mm(
                jnp.concatenate([transit_ref[head], maps_ref[head, 0, :, width:]], axis=0),
                states_ref[head, 0],
            )
            for head in ids
        ]
        for head, both_ends in zip(ids, steps_on):
            leaving_ref[head] = (terms_ref[head] + both_ends[:width]).astype(BF)
            inner = maps_ref[head, 0, :, :width].astype(F32) + both_ends[width:]
            states_ref[head, 1] = inner.astype(BF)

        @pl.when(forwards)
        def _():
            for head in ids:
                state_copy(head).start()

        for head in ids:
            back_copy(head).start()

    def read(part):
        ids = [part * PART + u for u in some]

        for u in range(owned):
            back_arrival(theirs(part * owned + u)).wait_recv()

        for u in some:
            finish_rows(u, ids[u], states_ref[ids[u], side])

    early = items // parts
    each = GROUP // PART

    def chain_range(first, last):
        lax.fori_loop(first, last, lambda item, none: (chain(item), none)[1], 0)

    def later_half(part):
        for copy in wide_loads[part]:
            copy.wait()

        stage(part)
        prepare(part, 1)

    later_half(0)

    @pl.when(has_left)
    def _():
        border_copy.wait_recv()

    middle = early // 2

    def first_phase(step, carry):
        again = step == 1

        @pl.when(again)
        def _():
            later_half(1)
            for sub in range(each):
                compose(sub)

                @pl.when(chip == 0)
                def _():
                    chain_range(sub * middle, (sub + 1) * middle)

        edges(step)
        prepare(step, 0)
        invert(step)

        def finish_solve(sub, none):
            solve(step * each + sub)
            send_maps(step * each + sub)

            @pl.when(again & (chip == 1))
            def _():
                chain_range(sub * middle, (sub + 1) * middle)

            return none

        lax.fori_loop(0, each, finish_solve, 0)
        return carry

    lax.fori_loop(0, parts, first_phase, 0)


    @pl.when(chip == 0)
    def _():
        compose(each)
        chain_range(early, early + middle)


    def second_phase(slot, carry):
        @pl.when(slot < pieces)
        def _():
            read_local(slot)

        @pl.when(slot == 0)
        def _():
            @pl.when(chip > 0)
            def _():
                compose(each)

            for sub in range(1, each):
                compose(each + sub)

        @pl.when(slot == pieces)
        def _():
            def sent(index, none):
                pair_copy(theirs(index)).wait_send()
                return none

            lax.fori_loop(0, heads // 2, sent, 0)

        @pl.when(slot == 2 * pieces - 1)
        def _():
            def returned(index, none):
                back_copy(mine(index)).wait_send()
                return none

            lax.fori_loop(0, early, returned, 0)

        def pick(places):
            first, last = 0, 0
            for at, start, end in places:
                first = jnp.where(slot == at, start, first)
                last = jnp.where(slot == at, end, last)
            return first, last

        late = early + middle
        plans = [
            pick([(0, late, items)]),
            pick([(2, early, late), (3, late, items)]),
            pick([(1, 0, middle), (2, middle, early), (3, early, late), (4, late, items)]),
            pick([(4, 0, late), (6, late, items)]),
        ]
        first, last = plans[3]
        for which in range(3):
            first = jnp.where(chip == which, plans[which][0], first)
            last = jnp.where(chip == which, plans[which][1], last)
        chain_range(first, last)

        @pl.when(slot > pieces)
        def _():
            read(slot - pieces - 1)

        return carry

    lax.fori_loop(0, 2 * pieces + 1, second_phase, 0)

    @pl.when(has_right)
    def _():
        border_copy.wait_send()

    def finish(index, carry):
        @pl.when(index >= early)
        def _():
            back_copy(mine(index)).wait_send()

        @pl.when(forwards)
        def _():
            state_copy(mine(index)).wait_send()

        return carry

    lax.fori_loop(0, heads // 2, finish, 0)


def body(
    queries,
    key_pairs,
    value_pairs,
    strengths,
    decays,
    conv_query,
    conv_key,
    conv_value,
    doc_lengths,
):
    heads, tokens, width = queries.shape
    n_seq = lax.axis_size("seq")
    steps = 2 * tokens
    vmem = pl.BlockSpec(memory_space=pltpu.VMEM)
    return pl.pallas_call(
        functools.partial(kernel, n_seq),
        out_shape=pltpu.VMEM((heads, tokens, width), BF),
        in_specs=[pl.BlockSpec(memory_space=pltpu.HBM)] * 9,
        out_specs=vmem,
        scratch_shapes=[
            pltpu.SMEM(doc_lengths.shape, jnp.int32),
            pltpu.VMEM(queries.shape, BF),
            pltpu.VMEM(key_pairs.shape, BF),
            pltpu.VMEM(value_pairs.shape, BF),
            pltpu.VMEM(strengths.shape, F32),
            pltpu.VMEM(decays.shape, F32),
            pltpu.VMEM(conv_query.shape, F32),
            pltpu.VMEM(conv_key.shape, F32),
            pltpu.VMEM(conv_value.shape, F32),
            pltpu.VMEM((heads, 16, width), BF),
            pltpu.VMEM((heads, 16, 2 * width), BF),
            pltpu.VMEM((heads, 16, 2 * width), BF),
            pltpu.VMEM((4 * heads, 5 * width), BF),
            pltpu.VMEM((4 * heads, 5 * width), BF),
            pltpu.VMEM((heads, 5, 16 + tokens, width), F32),
            pltpu.VMEM((3, tokens, tokens), F32),
            pltpu.VMEM((2, tokens, tokens), F32),
            pltpu.VMEM((2, tokens // 2, tokens), F32),
            pltpu.VMEM((tokens, tokens), F32),
            pltpu.VMEM((tokens, tokens), F32),
            pltpu.VMEM((tokens, tokens), F32),
            pltpu.VMEM((8 * heads, tokens), F32),
            pltpu.VMEM((8, steps), F32),
            pltpu.VMEM((2, tokens, heads), F32),
            pltpu.VMEM((2 * heads, tokens, tokens), BF),
            pltpu.VMEM((2 * heads, tokens, tokens), BF),
            pltpu.VMEM((2 * heads, tokens, tokens), BF),
            pltpu.VMEM((heads, 2, tokens, width), BF),
            pltpu.VMEM((heads, 2, tokens, width), BF),
            pltpu.VMEM((heads, 2, tokens, 2 * width), BF),
            pltpu.VMEM((heads, 2, tokens, 2 * width), BF),
            pltpu.VMEM((heads, width, 2 * width), BF),
            pltpu.VMEM((PART, tokens, width), F32),
            pltpu.VMEM((heads, width, width), F32),
            pltpu.VMEM((heads, width, width), BF),
            pltpu.VMEM((heads, tokens, width), F32),
            pltpu.VMEM((heads, tokens, width), BF),
            pltpu.VMEM((heads, width, width), BF),
            pltpu.VMEM((heads, 2, width, 2 * width), BF),
            pltpu.VMEM((heads, 2, width, width), BF),
            pltpu.SemaphoreType.DMA((9 + 3 * (heads // GROUP),)),
            pltpu.SemaphoreType.DMA,
            pltpu.SemaphoreType.DMA,
            pltpu.SemaphoreType.DMA((heads,)),
            pltpu.SemaphoreType.DMA((heads,)),
            pltpu.SemaphoreType.DMA((heads,)),
            pltpu.SemaphoreType.DMA((heads,)),
            pltpu.SemaphoreType.DMA((heads,)),
            pltpu.SemaphoreType.DMA((heads,)),
        ],
        compiler_params=pltpu.CompilerParams(
            collective_id=0, has_side_effects=True, vmem_limit_bytes=60 << 20
        ),
        name="delta_product",
    )(
        doc_lengths,
        queries,
        key_pairs,
        value_pairs,
        strengths,
        decays,
        conv_query,
        conv_key,
        conv_value,
    )


def solution(mesh):
    in_specs = (
        P(None, ("dp", "seq"), None),
        P(None, ("dp", "seq"), None),
        P(None, ("dp", "seq"), None),
        P(None, ("dp", "seq")),
        P(None, ("dp", "seq")),
        P(),
        P(),
        P(),
        P("dp"),
    )
    out_specs = P(None, ("dp", "seq"), None)
    return jax.shard_map(body, mesh=mesh, in_specs=in_specs, out_specs=out_specs, check_vma=False)
```
